32 devices in a mesh: dp: 8 (over z, x), tensor: 4 (over y, core).
Axes of the slice: x: 2, y: 2, z: 4, core: 2. Of those that a mesh axis runs over, the one named last changes fastest.
Arguments:
- tokens: bfloat16 [2048, 2048], P('dp'), may hold values from -6 to 6
- cotangent: bfloat16 [2048, 2048], P('dp'), may hold values from -6 to 6
- lengths: int32 [16], P('dp'), may hold values from 32 to 128, as said below
- master: float32 [4, 23389184], P('tensor', 'dp'), may hold values from -8 to 8
- moment_one: float32 [4, 23389184], P('tensor', 'dp'), may hold values from -60 to 60
- moment_two: float32 [4, 23389184], P('tensor', 'dp'), may hold values from 10 to 1000
Outputs:
- output: bfloat16 [2048, 2048], P('dp')
- input_grad: float32 [2048, 2048], P('dp')
- master_new: float32 [4, 23389184], P('tensor', 'dp')
- moment_one_new: float32 [4, 23389184], P('tensor', 'dp')
- moment_two_new: float32 [4, 23389184], P('tensor', 'dp')
- weights_copy: bfloat16 [4, 23389184], P('tensor', 'dp')
- weight_grads: float32 [4, 23389184], P('tensor', 'dp')
- norms: float32 [19, 2], replicated
The draws below stay inside these ranges and needn't reach their ends.
Inputs may be any that keep to these rules, and one draw needn't show every extreme that they name: `lengths`: each slot's valid rows form a prefix of the slot; in every draw some slot is full.
All inputs are finite; a program needn't handle non-finite values.
Results may differ from the reference program's by a relative error of at most 0.038.
Values may be sent and summed in bfloat16 or wider, within the bound.
A program may use at most 576 MiB of HBM per device.

```python
import math
from functools import partial
from functools import reduce
import jax
import jax.numpy as jnp
from jax import lax

D = 2048
INNER = 4096
NSTATE = 16
DTR = 128
HEADS = 32
HEAD_DIM = 64
FF = 4096
CONV = 4
WINDOW = 2048
SLOT = 128
EI = 1024
FI = 1024
HI = 8
DG = 512
PT = 23389184
SLOTS = 16
TOKENS = 2048
N_TENSOR = 4


def layout_drawn(d_model, e_in, f_in, h_width, n_state, conv_len, dt_rank, d_gain):
    entries = [('gain', (4, d_gain)), ('w_in', (d_model, 2 * e_in)), ('conv_w', (conv_len, e_in)), ('conv_b', (e_in,)), ('dt_bias', (e_in,)), ('d_skip', (e_in,)), ('a_log', (n_state, e_in)), ('w_x', (e_in, dt_rank + 2 * n_state)), ('w_dt', (dt_rank, e_in)), ('w_out', (e_in, d_model)), ('w_gu1', (d_model, 2 * f_in)), ('w_down1', (f_in, d_model)), ('w_qkv', (d_model, 3 * h_width)), ('w_o', (h_width, d_model)), ('w_gu2', (d_model, 2 * f_in)), ('w_down2', (f_in, d_model))]
    placed = []
    offset = 0
    for entry_name, entry_shape in entries:
        placed.append((entry_name, entry_shape, offset))
        offset = offset + math.prod(entry_shape)
    return placed


def entry_value(entry_name, normal, unif):
    if entry_name == 'gain':
        return 0.7 + 0.6 * unif
    if entry_name == 'conv_w':
        return normal * 0.5
    if entry_name == 'conv_b':
        return normal * 0.3
    if entry_name == 'dt_bias':
        step_init = jnp.exp(math.log(0.002) + unif * math.log(50.0))
        return jnp.log(jnp.expm1(step_init))
    if entry_name == 'd_skip':
        return 0.5 + unif
    if entry_name == 'a_log':
        return jnp.log(1.0 + 7.0 * unif)
    if entry_name == 'w_x' or entry_name == 'w_out':
        return normal * INNER ** (-0.5) * (2.0 if entry_name == 'w_out' else 1.0)
    if entry_name == 'w_dt':
        return normal * DTR ** (-0.5)
    if entry_name == 'w_down1' or entry_name == 'w_down2':
        return normal * FF ** (-0.5)
    if entry_name == 'w_o':
        return normal * 4.0 * (HEADS * HEAD_DIM) ** (-0.5)
    return normal * D ** (-0.5)


def draw_master(key, part):
    placed = layout_drawn(D, EI, FI, HI * HEAD_DIM, NSTATE, CONV, DTR, DG)
    key_normal, key_unif = jax.random.split(key)
    normal = jnp.clip(jax.random.normal(key_normal, (N_TENSOR, PT), jnp.float32), -6.0, 6.0)
    unif = jax.random.uniform(key_unif, (N_TENSOR, PT), jnp.float32)
    columns = jnp.arange(PT)[None, :]
    result = normal * 0.02
    for entry_name, entry_shape, offset in placed:
        count = math.prod(entry_shape)
        within_bounds = (columns >= offset) & (columns < offset + count)
        result = jnp.where(within_bounds, entry_value(entry_name, normal, unif), result)
    return result


def draw_lengths(key, part):
    key_vals, key_full = jax.random.split(key)
    drawn = jax.random.randint(key_vals, (SLOTS,), SLOT // 4, SLOT + 1)
    full_slot = jax.random.randint(key_full, (), 0, SLOTS)
    return jnp.where(jnp.arange(SLOTS) == full_slot, SLOT, drawn).astype(jnp.int32)


def block_scale(stream_key, dims, shards, low, top_value):
    loudness, own = 1.0, jax.random.fold_in(stream_key, 6)
    for dim, blocks in shards:
        heights = jnp.exp(jax.random.uniform(jax.random.fold_in(own, dim), (blocks,), jnp.float32, low / len(shards), top_value / len(shards)))
        loudness = loudness * jnp.repeat(heights, dims[dim] // blocks).reshape([-1 if axis == dim else 1 for axis in range(len(dims))])
    return loudness


def scatter_about(key, extent, width, limit, cuts=(), kind=jnp.bfloat16):
    values = width * jax.random.normal(key, extent, jnp.float32)
    if cuts:
        values = values * block_scale(key, extent, cuts, -0.22, 0.18)
    return jnp.clip(values, -limit, limit).astype(kind)


def setup_inputs(seed: int = 0) -> dict:
    arg_keys = jax.random.split(jax.random.key(seed), 7)
    return {
        "tokens": scatter_about(arg_keys[0], (TOKENS, D), 1.0, 6.0, ((0, 8),)),
        "cotangent": scatter_about(arg_keys[1], (TOKENS, D), 1.0, 6.0, ((0, 8),)),
        "lengths": draw_lengths(jax.random.fold_in(arg_keys[6], 71), 0),
        "master": draw_master(jax.random.fold_in(arg_keys[6], 71), 0),
        "moment_one": scatter_about(arg_keys[4], (N_TENSOR, PT), 10.0, 60.0, ((0, 4), (1, 8)), jnp.float32),
        "moment_two": jnp.clip(jnp.exp(math.log(1000.0) - 4.6051702 * jax.random.uniform(arg_keys[5], (N_TENSOR, PT), jnp.float32) ** block_scale(arg_keys[5], (N_TENSOR, PT), ((0, 4), (1, 8)), -0.2, 0.2)), 10.0, 1000.0),
    }


EPS_NORM = 1e-05
TRUST_EPSILON = 1e-06
ROPE_BASE = 10000.0
BETA_ONE = 0.5
BETA_TWO = 0.55
ADAM_EPS = 1e-06
DECAY_W = 0.01
LEARN_RATE = 0.2
NEG_FILL = -1e+30
PRECISE = lax.Precision.HIGHEST

@jax.custom_vjp
def low(v):
    return lax.optimization_barrier(v.astype(jnp.bfloat16)).astype(jnp.float32)

@jax.custom_vjp
def low_back(v):
    return v

def low_keep(v):
    return (low(v), None)

def low_pass(kept, grad):
    return (grad,)

def back_keep(v):
    return (v, None)

def back_low(kept, grad):
    return (low(grad),)
low.defvjp(low_keep, low_pass)
low_back.defvjp(back_keep, back_low)

def layout(d_model, e_in, f_in, h_width, n_state, conv_len, dt_rank, d_gain):
    entries = [('gain', (4, d_gain)), ('w_in', (d_model, 2 * e_in)), ('conv_w', (conv_len, e_in)), ('conv_b', (e_in,)), ('dt_bias', (e_in,)), ('d_skip', (e_in,)), ('a_log', (n_state, e_in)), ('w_x', (e_in, dt_rank + 2 * n_state)), ('w_dt', (dt_rank, e_in)), ('w_out', (e_in, d_model)), ('w_gu1', (d_model, 2 * f_in)), ('w_down1', (f_in, d_model)), ('w_qkv', (d_model, 3 * h_width)), ('w_o', (h_width, d_model)), ('w_gu2', (d_model, 2 * f_in)), ('w_down2', (f_in, d_model))]
    placed = []
    offset = 0
    for entry_name, entry_shape in entries:
        placed.append((entry_name, entry_shape, offset))
        offset = offset + math.prod(entry_shape)
    return (placed, offset)

def group_bounds(placed):
    bounds = []
    for entry_name, entry_shape, offset in placed:
        if entry_name == 'gain':
            for row_index in range(entry_shape[0]):
                bounds.append((offset + row_index * entry_shape[1], offset + (row_index + 1) * entry_shape[1]))
        else:
            bounds.append((offset, offset + math.prod(entry_shape)))
    return bounds

def silu(values):
    return values * jax.nn.sigmoid(values)

def softplus(values):
    return jnp.maximum(values, 0.0) + jnp.log1p(jnp.exp(-jnp.abs(values)))

def matmul(left, right):
    return jnp.dot(left, right, precision=PRECISE)

def rope_tables(length, head_dim):
    half_dim = head_dim // 2
    freq_index = jnp.arange(half_dim, dtype=jnp.float32)
    inv_freq = jnp.exp(-math.log(ROPE_BASE) * 2.0 * freq_index / head_dim)
    angles = jnp.arange(length, dtype=jnp.float32)[:, None] * inv_freq[None, :]
    return (jnp.cos(angles)[:, None, :], jnp.sin(angles)[:, None, :])

def rope_apply(values, cosine, sine):
    half_dim = values.shape[-1] // 2
    first_half = values[..., :half_dim]
    second_half = values[..., half_dim:]
    return jnp.concatenate([first_half * cosine - second_half * sine, second_half * cosine + first_half * sine], axis=-1)

def rms_apply(resid, gain_row):
    return resid * lax.rsqrt(lax.optimization_barrier(jnp.mean(resid * resid, axis=-1, keepdims=True)) + EPS_NORM) * gain_row

def conv_act(mix_x, conv_w, conv_b):
    length = mix_x.shape[0]
    tap_count = conv_w.shape[0]
    padded = jnp.pad(mix_x, ((tap_count - 1, 0), (0, 0)))
    summed = conv_b[None, :] + conv_w[0][None, :] * padded[0:length]
    for tap_index in range(1, tap_count):
        summed = summed + conv_w[tap_index][None, :] * padded[tap_index:tap_index + length]
    return silu(summed)

def mixer_scan(gate_z, unit_vals, proj, w_dt, dt_bias, a_log, d_skip):
    dt_rank = w_dt.shape[0]
    n_state = a_log.shape[0]
    step_size = softplus(jnp.dot(proj[:, :dt_rank], w_dt, precision=PRECISE) + dt_bias[None, :])
    b_in = proj[:, dt_rank:dt_rank + n_state]
    c_out = proj[:, dt_rank + n_state:]
    rates = -jnp.exp(a_log)

    def advance(state, inputs):
        step_row, unit_row, b_row, c_row = inputs
        state = jnp.exp(step_row[None, :] * rates) * state + b_row[:, None] * (step_row * unit_row)[None, :]
        return (state, jnp.dot(c_row, state, precision=PRECISE))
    initial = jnp.zeros(rates.shape, jnp.float32)
    final_state, scanned = lax.scan(advance, initial, (step_size, unit_vals, b_in, c_out))
    return (scanned + d_skip[None, :] * unit_vals) * silu(gate_z)

def mamba_branch(hidden, params):
    e_in = params['conv_b'].shape[1]
    parts = []
    kept = []
    for rank_index in range(params['w_in'].shape[0]):
        rank_in = low_back(hidden)
        mixed = low_back(matmul(rank_in, params['w_in'][rank_index]))
        unit_vals = low(conv_act(mixed[:, :e_in], params['conv_w'][rank_index], params['conv_b'][rank_index]))
        parts.append(low(matmul(unit_vals, params['w_x'][rank_index])))
        kept.append((mixed, unit_vals))
    proj = low(low_back(reduce(jnp.add, parts)))
    outs = []
    for rank_index in range(params['w_in'].shape[0]):
        mixed, unit_vals = kept[rank_index]
        gated = mixer_scan(mixed[:, e_in:], unit_vals, low_back(proj), params['w_dt'][rank_index], params['dt_bias'][rank_index], params['a_log'][rank_index], params['d_skip'][rank_index])
        outs.append(low(matmul(low(gated), params['w_out'][rank_index])))
    return low_back(reduce(jnp.add, outs))

def ffn_branch(hidden, w_gu, w_down):
    f_in = w_down.shape[1]
    parts = []
    for rank_index in range(w_gu.shape[0]):
        rank_in = low_back(hidden)
        pre_act = low_back(matmul(rank_in, w_gu[rank_index]))
        activ = low(silu(pre_act[:, :f_in]) * pre_act[:, f_in:])
        parts.append(low(matmul(activ, w_down[rank_index])))
    return low_back(reduce(jnp.add, parts))

def attention_branch(hidden, w_qkv, w_o, cosine, sine):
    length = hidden.shape[0]
    scale = HEAD_DIM ** (-0.5)
    positions = jnp.arange(length)
    distance = positions[:, None] - positions[None, :]
    allowed = (distance >= 0) & (distance < WINDOW)
    parts = []
    for rank_index in range(w_qkv.shape[0]):
        rank_in = low_back(hidden)
        packed = low_back(matmul(rank_in, w_qkv[rank_index])).reshape(length, 3, HI, HEAD_DIM)
        query = low(rope_apply(packed[:, 0], cosine, sine))
        keys = low(rope_apply(packed[:, 1], cosine, sine))
        values = low(packed[:, 2])
        scores = low_back(jnp.einsum('qhd,khd->hqk', query, keys, precision=PRECISE) * scale)
        scores = jnp.where(allowed[None], scores, NEG_FILL)
        expo = jnp.exp(scores - lax.optimization_barrier(jnp.max(scores, axis=-1, keepdims=True)))
        probs = low(expo / lax.optimization_barrier(jnp.sum(expo, axis=-1, keepdims=True)))
        attended = jnp.einsum('hqk,khd->qhd', probs, values, precision=PRECISE)
        attended = low(low_back(attended)).reshape(length, HI * HEAD_DIM)
        parts.append(low(matmul(attended, w_o[rank_index])))
    return low_back(reduce(jnp.add, parts))

def layer_forward(resid, params, cosine, sine):
    gains = jnp.transpose(params['gain'], (1, 0, 2)).reshape(4, -1)
    resid = resid + mamba_branch(low(rms_apply(resid, gains[0])), params)
    resid = resid + ffn_branch(low(rms_apply(resid, gains[1])), params['w_gu1'], params['w_down1'])
    resid = resid + attention_branch(low(rms_apply(resid, gains[2])), params['w_qkv'], params['w_o'], cosine, sine)
    resid = resid + ffn_branch(low(rms_apply(resid, gains[3])), params['w_gu2'], params['w_down2'])
    return resid

def reference(tokens, cotangent, lengths, master, moment_one, moment_two):
    placed, raw_count = layout(D, EI, FI, HI * HEAD_DIM, NSTATE, CONV, DTR, DG)
    rounded = master.astype(jnp.bfloat16).astype(jnp.float32)
    params = {}
    for entry_name, entry_shape, offset in placed:
        count = math.prod(entry_shape)
        params[entry_name] = rounded[:, offset:offset + count].reshape((N_TENSOR,) + entry_shape)
    cosine, sine = rope_tables(SLOT, HEAD_DIM)
    slot_tokens = tokens.astype(jnp.float32).reshape(SLOTS, SLOT, D)
    slot_cots = cotangent.astype(jnp.float32).reshape(SLOTS, SLOT, D)
    positions = jnp.arange(SLOT, dtype=jnp.int32)
    forward_fn = partial(layer_forward, cosine=cosine, sine=sine)

    def per_slot(totals, inputs):
        one_tokens, one_cot, one_length = inputs
        valid = (positions < one_length).astype(jnp.float32)
        outputs, backward = jax.vjp(forward_fn, one_tokens, params)
        grad_in, grad_params = backward(one_cot * valid[:, None])
        return (jax.tree.map(jnp.add, totals, grad_params), (outputs, grad_in))
    zeros_tree = jax.tree.map(jnp.zeros_like, params)
    totals, (outputs, grad_in) = lax.scan(per_slot, zeros_tree, (slot_tokens, slot_cots, lengths))
    pieces = [totals[entry_name].reshape(N_TENSOR, -1) for entry_name, entry_shape, offset in placed]
    pieces.append(jnp.zeros((N_TENSOR, PT - raw_count), jnp.float32))
    grads = jnp.concatenate(pieces, axis=1)
    first = BETA_ONE * moment_one + (1.0 - BETA_ONE) * grads
    second = BETA_TWO * moment_two + (1.0 - BETA_TWO) * grads * grads
    trust_ratio = first / (jnp.sqrt(second) + ADAM_EPS) + DECAY_W * master
    columns = jnp.arange(PT, dtype=jnp.int32)
    column_trust = jnp.zeros((PT,), jnp.float32)
    weight_sq = []
    trust_ratio_squared = []
    for lower_end, upper_end in group_bounds(placed):
        within_bounds = (columns >= lower_end) & (columns < upper_end)
        weight_norm_squared = jnp.sum(jnp.where(within_bounds[None, :], master * master, 0.0))
        update_norm_squared = jnp.sum(jnp.where(within_bounds[None, :], trust_ratio * trust_ratio, 0.0))
        weight_sq.append(weight_norm_squared)
        trust_ratio_squared.append(update_norm_squared)
        trust_factor = jnp.sqrt(weight_norm_squared + TRUST_EPSILON) * lax.rsqrt(update_norm_squared + TRUST_EPSILON)
        column_trust = jnp.where(within_bounds, trust_factor, column_trust)
    master_new = master - LEARN_RATE * column_trust[None, :] * trust_ratio
    norms = jnp.sqrt(jnp.stack([jnp.stack(weight_sq), jnp.stack(trust_ratio_squared)], axis=1))
    return (outputs.reshape(TOKENS, D).astype(jnp.bfloat16), grad_in.reshape(TOKENS, D), master_new, first, second, master_new.astype(jnp.bfloat16), grads, norms)
```

```python
import functools
import math

import jax
import jax.numpy as jnp
from jax import lax
from jax.experimental import pallas as pl
from jax.experimental.pallas import tpu as pltpu
from jax.sharding import PartitionSpec as P

D = 2048
INNER = 4096
NSTATE = 16
DTR = 128
HEADS = 32
HEAD_DIM = 64
FF = 4096
CONV = 4
WINDOW = 2048
SLOT = 128
LANES = 128

EPS_NORM = 1e-05
TRUST_EPSILON = 1e-06
ROPE_BASE = 10000.0
BETA_ONE = 0.5
BETA_TWO = 0.55
ADAM_EPS = 1e-06
DECAY_W = 0.01
LEARN_RATE = 0.2
NEG_FILL = -1e30
LOG2E = 1.4426950408889634
MESH = pl.DeviceIdType.MESH
BF = jnp.bfloat16
F32 = jnp.float32

EI = INNER // 4
FI = FF // 4
HW = HEADS * HEAD_DIM // 4
DG = D // 4

SMALL = [
    ("conv_w", (CONV, EI)),
    ("conv_b", (EI,)),
    ("dt_bias", (EI,)),
    ("d_skip", (EI,)),
    ("a_log", (NSTATE, EI)),
    ("w_x", (EI, DTR + 2 * NSTATE)),
    ("w_dt", (DTR, EI)),
]
SMALL_ROWS = sum(math.prod(s) for _, s in SMALL) // LANES
GAIN_ROWS = 4 * DG // LANES
BIG = [
    ("w_in", D),
    ("w_out", EI),
    ("w_gu1", D),
    ("w_down1", FI),
    ("w_qkv", D * 3 * HW // D),
    ("w_o", HW),
    ("w_gu2", D),
    ("w_down2", FI),
]
BIG_OFF = {}
_at = 0
for _name, _rows in BIG:
    BIG_OFF[_name] = _at
    _at += _rows
BIG_ROWS = _at
LINES = D // LANES
FIRST = BIG_OFF["w_out"] * LINES
LEAD = GAIN_ROWS


def group_bounds():
    bounds = []
    for k in range(4):
        bounds.append((k * DG, (k + 1) * DG))
    at = 4 * DG
    entries = [("w_in", D * 2 * EI)]
    entries += [(name, math.prod(shape)) for name, shape in SMALL]
    entries += [
        ("w_out", EI * D),
        ("w_gu1", D * 2 * FI),
        ("w_down1", FI * D),
        ("w_qkv", D * 3 * HW),
        ("w_o", HW * D),
        ("w_gu2", D * 2 * FI),
        ("w_down2", FI * D),
    ]
    for _, count in entries:
        bounds.append((at, at + count))
        at += count
    return bounds


def silu(v):
    return v * jax.nn.sigmoid(v)


def softplus(v):
    return jnp.maximum(v, 0.0) + jnp.log1p(jnp.exp(-jnp.abs(v)))


def mat_nn(a, b):
    return jnp.dot(a, b, preferred_element_type=F32)


def mat_tn(a, b):
    return lax.dot_general(a, b, (((0,), (0,)), ((), ())), preferred_element_type=F32)


def mat_nt(a, b):
    return lax.dot_general(a, b, (((1,), (1,)), ((), ())), preferred_element_type=F32)


def ring_pos(d, n):
    return jnp.where(lax.rem(d, 2) == 0, lax.div(d, 2), n - 1 - lax.div(d, 2))


def ring_dev(p, n):
    return jnp.where(p < n // 2, 2 * p, 2 * (n - 1 - p) + 1)


def ring_neighbours(n):
    d = lax.axis_index("dp")
    p = ring_pos(d, n)
    right = ring_dev(lax.rem(p + 1, n), n)
    left = ring_dev(lax.rem(p + n - 1, n), n)
    return d, p, right, left


def ring_barrier(left, right, t):
    barrier = pltpu.get_barrier_semaphore()
    for nb in (left, right):
        pl.semaphore_signal(barrier, inc=1, device_id=(nb, t), device_id_type=MESH)
    pl.semaphore_wait(barrier, 2)


def gather_kernel(n, subs, own_ref, out_ref, hold, local_sem, ssem, rsem):
    t = lax.axis_index("tensor")
    d, p, right, left = ring_neighbours(n)
    rows = own_ref.shape[0]
    half = rows // 2
    sub = half // subs
    fetch = pltpu.make_async_copy(own_ref, hold, local_sem.at[0])
    fetch.start()
    ring_barrier(left, right, t)

    def copy(way, step, c, from_own):
        target = right if way == 0 else left
        owner = ring_dev(lax.rem(p + (n - step if way == 0 else step), n), n)
        at = pl.multiple_of(owner * rows + way * half + c * sub, 8)
        src = own_ref.at[pl.ds(way * half + c * sub, sub)] if from_own else out_ref.at[pl.ds(at, sub)]
        return pltpu.make_async_remote_copy(
            src_ref=src,
            dst_ref=out_ref.at[pl.ds(at, sub)],
            send_sem=ssem.at[way, step, c],
            recv_sem=rsem.at[way, step, c],
            device_id=(target, t),
            device_id_type=MESH,
        )

    for c in range(subs):
        for way in (0, 1):
            copy(way, 0, c, True).start()
    fetch.wait()
    store = pltpu.make_async_copy(
        hold, out_ref.at[pl.ds(pl.multiple_of(d * rows, 8), rows)], local_sem.at[1]
    )
    store.start()
    for step in range(1, n - 1):
        for c in range(subs):
            for way in (0, 1):
                copy(way, step - 1, c, step == 1).wait_recv()
                copy(way, step, c, False).start()
    for c in range(subs):
        for way in (0, 1):
            copy(way, n - 2, c, n == 2).wait_recv()
    store.wait()
    for step in range(n - 1):
        for c in range(subs):
            for way in (0, 1):
                copy(way, step, c, step == 0).wait_send()


def ring_gather(own, n):
    rows, cols = own.shape
    subs = 2
    return pl.pallas_call(
        functools.partial(gather_kernel, n, subs),
        out_shape=jax.ShapeDtypeStruct((n * rows, cols), own.dtype),
        in_specs=[pl.BlockSpec(memory_space=pl.ANY)],
        out_specs=pl.BlockSpec(memory_space=pl.ANY),
        scratch_shapes=[
            pltpu.VMEM((rows, cols), own.dtype),
            pltpu.SemaphoreType.DMA((2,)),
            pltpu.SemaphoreType.DMA((2, n - 1, subs)),
            pltpu.SemaphoreType.DMA((2, n - 1, subs)),
        ],
        compiler_params=pltpu.CompilerParams(
            collective_id=0, has_side_effects=True, vmem_limit_bytes=32 << 20
        ),
        name="ring_gather",
    )(own)


def piece_of(half):
    for size in (64, 32, 16):
        if half % size == 0:
            return size


def reduce_kernel(n, left_ref, right_refs, qkv_ref, out_ref, slots, ssem, rsem, out_sem):
    t = lax.axis_index("tensor")
    d, p, right, left = ring_neighbours(n)
    rows = out_ref.shape[0]
    half = rows // 2
    SUB = piece_of(half)
    subs = half // SUB
    ring_barrier(left, right, t)
    qkv_at = BIG_OFF["w_qkv"]
    qkv_rows = dict(BIG)["w_qkv"]

    def own_into(at, put):
        in_qkv = jnp.logical_and(at >= qkv_at, at < qkv_at + qkv_rows)
        which = jnp.int32(0)
        for name, _ in BIG[1:]:
            if name != "w_qkv":
                which = which + jnp.where(at >= BIG_OFF[name], 1, 0)

        @pl.when(in_qkv)
        def _():
            put(qkv_ref[pl.ds(pl.multiple_of(at - qkv_at, SUB), SUB), :].astype(F32))

        @pl.when(jnp.logical_not(in_qkv))
        def _():
            row = jnp.where(at >= qkv_at + qkv_rows, at - qkv_rows, at)
            lt = left_ref[pl.ds(pl.multiple_of(row, SUB), SUB), :]
            put(jnp.dot(lt, right_refs[which], preferred_element_type=F32))

    def owner_of(way, step):
        return ring_dev(lax.rem(p + (n - 1 - step if way == 0 else 1 + step), n), n)

    def copy(way, step, c):
        target = right if way == 0 else left
        return pltpu.make_async_remote_copy(
            src_ref=slots.at[way, step, pl.ds(pl.multiple_of(c * SUB, SUB), SUB)],
            dst_ref=slots.at[way, step + 1, pl.ds(pl.multiple_of(c * SUB, SUB), SUB)],
            send_sem=ssem.at[way, step, c],
            recv_sem=rsem.at[way, step, c],
            device_id=(target, t),
            device_id_type=MESH,
        )

    def run(step):
        @pl.loop(0, subs)
        def _(c):
            here = pl.ds(pl.multiple_of(c * SUB, SUB), SUB)
            for way in (0, 1):
                at = owner_of(way, step) * rows + way * half + c * SUB
                if step > 0:
                    copy(way, step - 1, c).wait_recv()

                def put(value):
                    if step > 0:
                        value = value + slots[way, step, here, :].astype(F32)
                    slots[way, step, here, :] = value.astype(BF)

                own_into(at, put)
                if step < n - 1:
                    copy(way, step, c).start()
                else:
                    pltpu.make_async_copy(
                        slots.at[way, step, here],
                        out_ref.at[pl.ds(pl.multiple_of(way * half + c * SUB, SUB), SUB)],
                        out_sem.at[way, c],
                    ).start()

    for step in range(n):
        run(step)

    @pl.loop(0, subs)
    def _(c):
        here = pl.ds(pl.multiple_of(c * SUB, SUB), SUB)
        for way in (0, 1):
            for step in range(n - 1):
                copy(way, step, c).wait_send()
            pltpu.make_async_copy(
                slots.at[way, n - 1, here],
                out_ref.at[pl.ds(pl.multiple_of(way * half + c * SUB, SUB), SUB)],
                out_sem.at[way, c],
            ).wait()


def ring_reduce(left_t, rights, qkv_grad, n):
    rows = BIG_ROWS // n
    subs = rows // 2 // piece_of(rows // 2)
    vm = pl.BlockSpec(memory_space=pltpu.VMEM)
    return pl.pallas_call(
        functools.partial(reduce_kernel, n),
        out_shape=jax.ShapeDtypeStruct((rows, D), BF),
        in_specs=[vm, vm, vm],
        out_specs=pl.BlockSpec(memory_space=pl.ANY),
        scratch_shapes=[
            pltpu.VMEM((2, n, rows // 2, D), BF),
            pltpu.SemaphoreType.DMA((2, n - 1, subs)),
            pltpu.SemaphoreType.DMA((2, n - 1, subs)),
            pltpu.SemaphoreType.DMA((2, subs)),
        ],
        compiler_params=pltpu.CompilerParams(
            collective_id=1, has_side_effects=True, vmem_limit_bytes=67043328
        ),
        name="ring_reduce",
    )(left_t, rights, qkv_grad)


def spread(ref, value):
    rows = value.shape[0]
    for j in range(EI // LANES):
        ref[pl.ds(j, rows, stride=EI // LANES), :] = value[:, j * LANES : (j + 1) * LANES]


def collect(ref, rows):
    return jnp.concatenate(
        [ref[pl.ds(j, rows, stride=EI // LANES), :] for j in range(EI // LANES)], axis=1
    )


SUBL = EI // LANES


def scan_kernel(slots, proj_ref, bc_ref, unit_ref, gate_ref, w_dt_ref, bias_ref, skip_ref, alog_ref,
                gated_ref, step_s, su_s, y_s, rate_s):
    pre = jnp.dot(proj_ref[:, :DTR], w_dt_ref[...], preferred_element_type=F32) + bias_ref[...]
    step = softplus(pre)
    unit = unit_ref[...].astype(F32)
    spread(step_s, step)
    spread(su_s, step * unit)
    rate_s[...] = -jnp.exp(alog_ref[...]) * LOG2E

    def body(t, states):
        new = []
        for m in range(slots):
            r = m * SLOT + t
            row = pl.ds(pl.multiple_of(r * SUBL, SUBL), SUBL)
            st = step_s[row, :]
            su = su_s[row, :]
            y = jnp.zeros((SUBL, LANES), F32)
            for k in range(NSTATE):
                dec = jnp.exp2(rate_s[k * SUBL : (k + 1) * SUBL, :] * st)
                s = dec * states[m * NSTATE + k] + bc_ref[r, k] * su
                y = y + bc_ref[r, NSTATE + k] * s
                new.append(s)
            y_s[row, :] = y
        return tuple(new)

    init = tuple(jnp.zeros((SUBL, LANES), F32) for _ in range(slots * NSTATE))
    lax.fori_loop(0, SLOT, body, init)
    y = collect(y_s, slots * SLOT) + skip_ref[...] * unit
    z = gate_ref[...]
    gated_ref[...] = (y * silu(z)).astype(BF)


def scan_forward(proj, bc, unit, gate, w_dt, dt_bias, d_skip, a_log):
    rows = unit.shape[0]
    vm = pl.BlockSpec(memory_space=pltpu.VMEM)
    sm = pl.BlockSpec(memory_space=pltpu.SMEM)
    return pl.pallas_call(
        functools.partial(scan_kernel, rows // SLOT),
        out_shape=jax.ShapeDtypeStruct((rows, EI), BF),
        in_specs=[vm, sm, vm, vm, vm, vm, vm, vm],
        out_specs=vm,
        scratch_shapes=[
            pltpu.VMEM((rows * SUBL, LANES), F32),
            pltpu.VMEM((rows * SUBL, LANES), F32),
            pltpu.VMEM((rows * SUBL, LANES), F32),
            pltpu.VMEM((NSTATE * SUBL, LANES), F32),
        ],
        compiler_params=pltpu.CompilerParams(vmem_limit_bytes=60 << 20),
        name="scan_forward",
    )(proj, bc, unit, gate, w_dt, dt_bias, d_skip, a_log)


def adjoint_kernel(slots, proj_ref, bc_ref, unit_ref, gate_ref, w_dt_ref, bias_ref, skip_ref, alog_ref,
                   grad_ref, gz_ref, gunit_ref, gproj_ref, gdt_ref, gbias_ref, gskip_ref, galog_ref,
                   step_s, su_s, unit_s, y_s, gy_s, gs_s, lb_s, rate_s, hist, lams):
    rows = slots * SLOT
    pre = jnp.dot(proj_ref[:, :DTR], w_dt_ref[...], preferred_element_type=F32) + bias_ref[...]
    step = softplus(pre)
    unit = unit_ref[...].astype(F32)
    spread(step_s, step)
    spread(unit_s, unit)
    spread(su_s, step * unit)
    z = gate_ref[...]
    sig = jax.nn.sigmoid(z)
    gg = grad_ref[...]
    gy = gg * z * sig
    spread(gy_s, gy)
    rate_s[...] = -jnp.exp(alog_ref[...])
    galog_ref[...] = jnp.zeros_like(galog_ref)
    zero = jnp.zeros((SUBL, LANES), F32)
    span = SLOT + 1

    def hist_at(k, t):
        return pl.ds(pl.multiple_of((k * span + t) * SUBL, SUBL), SUBL)

    def lam_at(k, t):
        return pl.ds(pl.multiple_of((k * SLOT + t) * SUBL, SUBL), SUBL)

    for m in range(slots):
        for k in range(NSTATE):
            hist[hist_at(k, 0), :] = zero

        def forward(t, states):
            r = m * SLOT + t
            row = pl.ds(pl.multiple_of(r * SUBL, SUBL), SUBL)
            st = step_s[row, :] * LOG2E
            su = su_s[row, :]
            y = zero
            new = []
            for k in range(NSTATE):
                dec = jnp.exp2(rate_s[k * SUBL : (k + 1) * SUBL, :] * st)
                s = dec * states[k] + bc_ref[r, k] * su
                y = y + bc_ref[r, NSTATE + k] * s
                hist[hist_at(k, t + 1), :] = s
                new.append(s)
            y_s[row, :] = y
            return tuple(new)

        lax.fori_loop(0, SLOT, forward, tuple(zero for _ in range(NSTATE)))

        def backward(i, carry):
            t = SLOT - 1 - i
            r = m * SLOT + t
            row = pl.ds(pl.multiple_of(r * SUBL, SUBL), SUBL)
            st = step_s[row, :]
            st2 = st * LOG2E
            gyt = gy_s[row, :]
            lb = zero
            gs = zero
            new = []
            for k in range(NSTATE):
                rate = rate_s[k * SUBL : (k + 1) * SUBL, :]
                dec = jnp.exp2(rate * st2)
                lam = bc_ref[r, NSTATE + k] * gyt + carry[k]
                ld = dec * lam
                new.append(ld)
                lams[lam_at(k, t), :] = lam
                lb = lb + bc_ref[r, k] * lam
                x = ld * hist[hist_at(k, t), :]
                gs = gs + rate * x
                at = slice(k * SUBL, (k + 1) * SUBL)
                galog_ref[at, :] = galog_ref[at, :] + st * x
            lb_s[row, :] = lb
            gs_s[row, :] = gs + unit_s[row, :] * lb
            return tuple(new)

        lax.fori_loop(0, SLOT, backward, tuple(zero for _ in range(NSTATE)))
        out = slice(m * SLOT, (m + 1) * SLOT)
        base = m * SLOT * SUBL

        lane = lax.broadcasted_iota(jnp.int32, (SLOT, LANES), 1)

        def reduce_state(k, acc):
            ab = jnp.zeros((SLOT, LANES), F32)
            ac = jnp.zeros((SLOT, LANES), F32)
            for j in range(SUBL):
                cols = slice(j * LANES, (j + 1) * LANES)
                lam = lams[pl.ds(k * SLOT * SUBL + j, SLOT, stride=SUBL), :]
                h = hist[pl.ds((k * span + 1) * SUBL + j, SLOT, stride=SUBL), :]
                sj = su_s[pl.ds(base + j, SLOT, stride=SUBL), :]
                gj = gy_s[pl.ds(base + j, SLOT, stride=SUBL), :]
                ab = ab + lam * sj
                ac = ac + h * gj
            sb = jnp.sum(ab, axis=1, keepdims=True)
            sc = jnp.sum(ac, axis=1, keepdims=True)
            return acc + jnp.where(lane == k, sb, 0.0) + jnp.where(lane == NSTATE + k, sc, 0.0)

        sums = lax.fori_loop(0, NSTATE, reduce_state, jnp.zeros((SLOT, LANES), F32))
        gproj_ref[out, DTR : DTR + LANES] = sums.astype(BF)
    galog_ref[...] = galog_ref[...] * rate_s[...]
    y = collect(y_s, rows) + skip_ref[...] * unit
    gz_ref[...] = (gg * y * sig * (1.0 + z * (1.0 - sig))).astype(BF)
    gunit_ref[...] = gy * skip_ref[...] + step * collect(lb_s, rows)
    gskip_ref[...] = jnp.sum(gy * unit, axis=0, keepdims=True)
    q = collect(gs_s, rows) * jax.nn.sigmoid(pre)
    gbias_ref[...] = jnp.sum(q, axis=0, keepdims=True)
    ql = q.astype(BF)
    gdt_ref[...] = mat_tn(proj_ref[:, :DTR], ql)
    gproj_ref[:, :DTR] = mat_nt(ql, w_dt_ref[...]).astype(BF)


def scan_backward(proj, bc, unit, gate, w_dt, dt_bias, d_skip, a_log, grad):
    rows = unit.shape[0]
    vm = pl.BlockSpec(memory_space=pltpu.VMEM)
    sm = pl.BlockSpec(memory_space=pltpu.SMEM)
    sds = jax.ShapeDtypeStruct
    flat = pltpu.VMEM((rows * SUBL, LANES), F32)
    return pl.pallas_call(
        functools.partial(adjoint_kernel, rows // SLOT),
        out_shape=(
            sds((rows, EI), BF),
            sds((rows, EI), F32),
            sds((rows, DTR + LANES), BF),
            sds((DTR, EI), F32),
            sds((1, EI), F32),
            sds((1, EI), F32),
            sds((NSTATE * SUBL, LANES), F32),
        ),
        in_specs=[vm, sm, vm, vm, vm, vm, vm, vm, vm],
        out_specs=(vm,) * 7,
        scratch_shapes=[flat] * 7
        + [
            pltpu.VMEM((NSTATE * SUBL, LANES), F32),
            pltpu.VMEM((NSTATE * (SLOT + 1) * SUBL, LANES), F32),
            pltpu.VMEM((NSTATE * SLOT * SUBL, LANES), F32),
        ],
        compiler_params=pltpu.CompilerParams(vmem_limit_bytes=60 << 20),
        name="scan_backward",
    )(proj, bc, unit, gate, w_dt, dt_bias, d_skip, a_log, grad)


def rope_tables(length, head_dim):
    half_dim = head_dim // 2
    freq_index = jnp.arange(half_dim, dtype=F32)
    inv_freq = jnp.exp(-math.log(ROPE_BASE) * 2.0 * freq_index / head_dim)
    angles = jnp.arange(length, dtype=F32)[:, None] * inv_freq[None, :]
    return (jnp.cos(angles)[None, :, None, :], jnp.sin(angles)[None, :, None, :])


def rope_apply(values, cosine, sine):
    half_dim = values.shape[-1] // 2
    a = values[..., :half_dim]
    b = values[..., half_dim:]
    return jnp.concatenate([a * cosine - b * sine, b * cosine + a * sine], axis=-1)


def rms_parts(v, g):
    s = lax.rsqrt(jnp.mean(v * v, axis=-1, keepdims=True) + EPS_NORM)
    return s, v * s


def rms_back(v, g, gh):
    s, nrm = rms_parts(v, g)
    gg = jnp.sum(gh * nrm, axis=0)
    gv = s * (gh * g - nrm * jnp.mean(gh * g * nrm, axis=-1, keepdims=True))
    return gv, gg


def total(partial_out):
    return lax.psum(partial_out.astype(BF), "tensor").astype(F32)


def shift_down(v, by):
    if by == 0:
        return v
    return jnp.pad(v, ((0, 0), (by, 0), (0, 0)))[:, : v.shape[1]]


def shift_up(v, by):
    if by == 0:
        return v
    return jnp.pad(v, ((0, 0), (0, by), (0, 0)))[:, by:]


def attend(query, keys, values):
    scale = HEAD_DIM ** (-0.5)
    distance = jnp.arange(SLOT)[:, None] - jnp.arange(SLOT)[None, :]
    allowed = (distance >= 0) & (distance < WINDOW)
    scores = jnp.einsum("mqhd,mkhd->mhqk", query, keys, preferred_element_type=F32) * scale
    scores = jnp.where(allowed, scores, NEG_FILL)
    expo = jnp.exp(scores - jnp.max(scores, axis=-1, keepdims=True))
    return expo / jnp.sum(expo, axis=-1, keepdims=True)


def ffn_forward(h, w_gu, w_down):
    pre = mat_nn(h, w_gu)
    act = (silu(pre[:, :FI]) * pre[:, FI:]).astype(BF)
    return total(mat_nn(act, w_down)), pre, act


def ffn_backward(pre, w_gu, w_down, grad_low):
    gate = pre[:, :FI]
    up = pre[:, FI:]
    ga = mat_nt(grad_low, w_down)
    sig = jax.nn.sigmoid(gate)
    grad_gate = ga * up * sig * (1.0 + gate * (1.0 - sig))
    grad_up = ga * gate * sig
    gp = jnp.concatenate([grad_gate, grad_up], axis=1).astype(BF)
    return total(mat_nt(gp, w_gu)), gp


def layer(x, grad_out, w, small, gains, n):
    rows = x.shape[0]
    m = rows // SLOT
    hr = HW // HEAD_DIM
    cosine, sine = rope_tables(SLOT, HEAD_DIM)
    s1, n1 = rms_parts(x, gains[0])
    h1 = (n1 * gains[0]).astype(BF)
    mixed = mat_nn(h1, w["w_in"])
    mix_x = mixed[:, :EI].reshape(m, SLOT, EI)
    gate_z = mixed[:, EI:]
    conv_w = small["conv_w"].astype(F32)
    pre_conv = small["conv_b"].astype(F32)[None, None, :]
    for j in range(CONV):
        pre_conv = pre_conv + conv_w[j] * shift_down(mix_x, CONV - 1 - j)
    unit = silu(pre_conv).astype(BF).reshape(rows, EI)
    proj = lax.psum(mat_nn(unit, small["w_x"]).astype(BF), "tensor")
    bc = proj[:, DTR:].astype(F32)
    scan_args = (
        proj[:, :DTR],
        bc,
        unit,
        gate_z,
        small["w_dt"],
        small["dt_bias"].astype(F32)[None],
        small["d_skip"].astype(F32)[None],
        small["a_log"].astype(F32).reshape(NSTATE * SUBL, LANES),
    )
    gated = scan_forward(*scan_args)
    x1 = x + total(mat_nn(gated, w["w_out"]))
    h2 = (rms_parts(x1, 0)[1] * gains[1]).astype(BF)
    branch, pre1, act1 = ffn_forward(h2, w["w_gu1"], w["w_down1"])
    x2 = x1 + branch
    h3 = (rms_parts(x2, 0)[1] * gains[2]).astype(BF)
    packed = mat_nn(h3, w["w_qkv"]).reshape(m, SLOT, 3, hr, HEAD_DIM)
    query = rope_apply(packed[:, :, 0], cosine, sine).astype(BF)
    keys = rope_apply(packed[:, :, 1], cosine, sine).astype(BF)
    values = packed[:, :, 2].astype(BF)
    probs = attend(query, keys, values)
    probs_low = probs.astype(BF)
    attended = jnp.einsum("mhqk,mkhd->mqhd", probs_low, values, preferred_element_type=F32)
    attended = attended.reshape(rows, HW).astype(BF)
    x3 = x2 + total(mat_nn(attended, w["w_o"]))
    h4 = (rms_parts(x3, 0)[1] * gains[3]).astype(BF)
    branch, pre2, act2 = ffn_forward(h4, w["w_gu2"], w["w_down2"])
    x4 = x3 + branch

    gb4 = grad_out.astype(BF)
    gh, gp2 = ffn_backward(pre2, w["w_gu2"], w["w_down2"], gb4)
    gv, gg4 = rms_back(x3, gains[3], gh)
    g3 = grad_out + gv
    gb3 = g3.astype(BF)
    gatt = mat_nt(gb3, w["w_o"]).astype(BF).reshape(m, SLOT, hr, HEAD_DIM)
    grad_p = jnp.einsum("mqhd,mkhd->mhqk", gatt, values, preferred_element_type=F32)
    inner = jnp.sum(probs * grad_p, axis=-1, keepdims=True)
    gs = (probs * (grad_p - inner)).astype(BF)
    scale = HEAD_DIM ** (-0.5)
    gq = jnp.einsum("mhqk,mkhd->mqhd", gs, keys, preferred_element_type=F32) * scale
    gk = jnp.einsum("mhqk,mqhd->mkhd", gs, query, preferred_element_type=F32) * scale
    gvv = jnp.einsum("mhqk,mqhd->mkhd", probs_low, gatt, preferred_element_type=F32)
    gpk = (
        jnp.stack([rope_apply(gq, cosine, -sine), rope_apply(gk, cosine, -sine), gvv], axis=2)
        .reshape(rows, 3 * HW)
        .astype(BF)
    )
    gv, gg3 = rms_back(x2, gains[2], total(mat_nt(gpk, w["w_qkv"])))
    g2 = g3 + gv
    gb2 = g2.astype(BF)
    gh, gp1 = ffn_backward(pre1, w["w_gu1"], w["w_down1"], gb2)
    gv, gg2 = rms_back(x1, gains[1], gh)
    g1 = g2 + gv
    gb1 = g1.astype(BF)
    ggated = mat_nt(gb1, w["w_out"])
    gz, gunit, gproj, g_dt, g_bias, g_skip, g_alog = scan_backward(*scan_args, ggated)
    gproj = lax.psum(gproj[:, : DTR + 2 * NSTATE], "tensor")
    g_wx = mat_tn(unit, gproj)
    gu = gunit + mat_nt(gproj, small["w_x"])
    sig = jax.nn.sigmoid(pre_conv)
    gpre = gu.reshape(m, SLOT, EI) * sig * (1.0 + pre_conv * (1.0 - sig))
    g_conv_b = jnp.sum(gpre, axis=(0, 1))
    g_conv_w = jnp.stack(
        [jnp.sum(gpre * shift_down(mix_x, CONV - 1 - j), axis=(0, 1)) for j in range(CONV)]
    )
    gmx = sum(conv_w[j] * shift_up(gpre, CONV - 1 - j) for j in range(CONV))
    gmixed = jnp.concatenate([gmx.reshape(rows, EI).astype(BF), gz], axis=1)
    gv, gg1 = rms_back(x, gains[0], total(mat_nt(gmixed, w["w_in"])))
    g0 = g1 + gv

    left_t = jnp.concatenate([h1, gated, h2, act1, attended, h4, act2], axis=1).T
    rights = jnp.stack([gmixed, gb1, gp1, gb2, gb3, gp2, gb4])
    g_qkv = mat_tn(h3, gpk).astype(BF).reshape(-1, D)
    slab = ring_reduce(left_t, rights, g_qkv, n)
    start = lax.axis_index("tensor") * DG
    g_gain = lax.dynamic_slice_in_dim(jnp.stack([gg1, gg2, gg3, gg4]), start, DG, 1)
    pieces = [g_gain, g_conv_w, g_conv_b, g_bias, g_skip, g_alog, g_wx, g_dt]
    small_grads = jnp.concatenate([p.reshape(-1) for p in pieces])
    return x4.astype(BF), g0, slab, small_grads


def extents(n, shard_rows):
    slab = BIG_ROWS * LINES // n
    before = 0
    after = 0
    back_before = 0
    back_after = 0
    for d in range(n):
        lo, hi = slab * d, slab * (d + 1) - 1
        qs = [p + LEAD + (SMALL_ROWS if p >= FIRST else 0) - shard_rows * d for p in (lo, hi)]
        before = max(before, -qs[0])
        after = max(after, qs[1] + 1 - shard_rows)
    return before, after


def shift_perm(n, by):
    return [(i, i + by) for i in range(n) if 0 <= i + by < n]


def stack_own(flat, n):
    lines = flat.shape[0] // LANES
    before, after = extents(n, lines)
    d = lax.axis_index("dp")
    slab = BIG_ROWS * LINES // n
    nxt = lax.ppermute(flat[: after * LANES], "dp", shift_perm(n, -1))
    prv = lax.ppermute(flat[-before * LANES :], "dp", shift_perm(n, 1))
    ext = jnp.concatenate([prv, flat, nxt])
    at = before + slab * d + LEAD - lines * d
    limit = before + lines + after - slab

    def take(a):
        return lax.dynamic_slice_in_dim(ext, jnp.clip(a, 0, limit) * LANES, slab * LANES, 0).reshape(-1, D)

    one = take(at)
    two = take(at + SMALL_ROWS)
    row = lax.broadcasted_iota(jnp.int32, (BIG_ROWS // n, 1), 0) + d * (BIG_ROWS // n)
    return jnp.where(row < FIRST // LINES, one, two)


def window(values, shift, size):
    length = values.shape[0]
    if length >= size:
        s = jnp.clip(shift, 0, length - size)
        got = lax.dynamic_slice_in_dim(values, s, size, 0)
        room = jnp.zeros((3 * size,), values.dtype)
        room = lax.dynamic_update_slice_in_dim(room, got, size + jnp.clip(s - shift, -size, size), 0)
        return room[size : 2 * size]
    padded = jnp.concatenate([jnp.zeros((size,), values.dtype), values, jnp.zeros((size,), values.dtype)])
    return lax.dynamic_slice_in_dim(padded, jnp.clip(shift + size, 0, length + size), size, 0)


def per_device(n, tokens, cotangent, lengths, master, moment_one, moment_two):
    d = lax.axis_index("dp")
    shard = master.shape[1]
    lines = shard // LANES
    own = master[0].astype(BF)
    base = d * shard
    small_own = jnp.concatenate(
        [
            window(own, -base, GAIN_ROWS * LANES),
            window(own, (LEAD + FIRST) * LANES - base, SMALL_ROWS * LANES),
        ]
    )
    small_flat = lax.psum(small_own, "dp")
    gains = lax.all_gather(small_flat[: GAIN_ROWS * LANES].reshape(4, DG), "tensor", axis=1, tiled=True)
    gains = gains.astype(F32)
    small = {}
    at = GAIN_ROWS * LANES
    for name, shape in SMALL:
        count = math.prod(shape)
        small[name] = small_flat[at : at + count].reshape(shape)
        at += count
    weights = ring_gather(stack_own(own, n), n)
    w = {}
    for name, rows in BIG:
        w[name] = weights[BIG_OFF[name] : BIG_OFF[name] + rows]
    w["w_qkv"] = w["w_qkv"].reshape(D, 3 * HW)
    x = tokens.astype(F32)
    pos = lax.broadcasted_iota(jnp.int32, (tokens.shape[0] // SLOT, SLOT), 1)
    valid = (pos < lengths[:, None]).astype(F32).reshape(-1, 1)
    grad = cotangent.astype(F32) * valid
    out, grad_in, slab, small_grads = layer(x, grad, w, small, gains, n)

    small_sum = lax.psum(small_grads.astype(BF), "dp").astype(F32)
    slab_lines = BIG_ROWS * LINES // n
    before, after = extents(n, lines)
    flat = slab.astype(F32).reshape(-1)
    tail = lax.ppermute(slab.reshape(-1)[-after * LANES :], "dp", shift_perm(n, 1)).astype(F32)
    head = lax.ppermute(slab.reshape(-1)[: before * LANES], "dp", shift_perm(n, -1)).astype(F32)
    pad = jnp.zeros((2 * SMALL_ROWS * LANES,), F32)
    ext = jnp.concatenate([pad, tail, flat, head, pad])
    first_at = (2 * SMALL_ROWS + after) * LANES + base - LEAD * LANES - d * slab_lines * LANES
    limit = ext.shape[0] - shard
    one = lax.dynamic_slice_in_dim(ext, jnp.clip(first_at, 0, limit), shard, 0)
    two = lax.dynamic_slice_in_dim(ext, jnp.clip(first_at - SMALL_ROWS * LANES, 0, limit), shard, 0)
    index = base + jnp.arange(shard, dtype=jnp.int32)
    mid = (LEAD + FIRST) * LANES
    end = mid + SMALL_ROWS * LANES
    grad_shard = jnp.where(index < mid, one, two)
    grad_shard = jnp.where(
        index < LEAD * LANES,
        window(small_sum[: LEAD * LANES], base, shard),
        jnp.where((index >= mid) & (index < end), window(small_sum[LEAD * LANES :], base - mid, shard), grad_shard),
    )
    used = end + (BIG_ROWS * LINES - FIRST) * LANES
    grad_shard = jnp.where(index < used, grad_shard, 0.0)

    weights_old = master[0]
    first = BETA_ONE * moment_one[0] + (1.0 - BETA_ONE) * grad_shard
    second = BETA_TWO * moment_two[0] + (1.0 - BETA_TWO) * grad_shard * grad_shard
    trust_ratio = first / (jnp.sqrt(second) + ADAM_EPS) + DECAY_W * weights_old
    bounds = group_bounds()
    pieces = []
    for lower_end, upper_end in bounds:
        within = (index >= lower_end) & (index < upper_end)
        pieces.append(
            jnp.stack(
                [
                    jnp.sum(jnp.where(within, weights_old * weights_old, 0.0)),
                    jnp.sum(jnp.where(within, trust_ratio * trust_ratio, 0.0)),
                ]
            )
        )
    squares = lax.psum(jnp.stack(pieces), ("dp", "tensor"))
    trust_factor = jnp.sqrt(squares[:, 0] + TRUST_EPSILON) * lax.rsqrt(squares[:, 1] + TRUST_EPSILON)
    column_trust = jnp.zeros((shard,), F32)
    for g, (lower_end, upper_end) in enumerate(bounds):
        within = (index >= lower_end) & (index < upper_end)
        column_trust = jnp.where(within, trust_factor[g], column_trust)
    master_new = weights_old - LEARN_RATE * column_trust * trust_ratio
    return (
        out,
        grad_in,
        master_new[None, :],
        first[None, :],
        second[None, :],
        master_new.astype(BF)[None, :],
        grad_shard[None, :],
        jnp.sqrt(squares),
    )


def solution(mesh):
    row = P("dp", None)
    flat = P("tensor", "dp")
    return jax.shard_map(
        functools.partial(per_device, mesh.shape["dp"]),
        mesh=mesh,
        in_specs=(row, row, P("dp"), flat, flat, flat),
        out_specs=(row, row, flat, flat, flat, flat, flat, P()),
        check_vma=False,
    )
```

```python
import functools
import math

import jax
import jax.numpy as jnp
from jax import lax
from jax.experimental import pallas as pl
from jax.experimental.pallas import tpu as pltpu
from jax.sharding import PartitionSpec as P

D = 2048
INNER = 4096
NSTATE = 16
DTR = 128
HEADS = 32
HEAD_DIM = 64
FF = 4096
CONV = 4
WINDOW = 2048
SLOT = 128
LANES = 128

EPS_NORM = 1e-05
TRUST_EPSILON = 1e-06
ROPE_BASE = 10000.0
BETA_ONE = 0.5
BETA_TWO = 0.55
ADAM_EPS = 1e-06
DECAY_W = 0.01
LEARN_RATE = 0.2
NEG_FILL = -1e30
LOG2E = 1.4426950408889634
MESH = pl.DeviceIdType.MESH
BF = jnp.bfloat16
F32 = jnp.float32

EI = INNER // 4
FI = FF // 4
HW = HEADS * HEAD_DIM // 4
DG = D // 4

SMALL = [
    ("conv_w", (CONV, EI)),
    ("conv_b", (EI,)),
    ("dt_bias", (EI,)),
    ("d_skip", (EI,)),
    ("a_log", (NSTATE, EI)),
    ("w_x", (EI, DTR + 2 * NSTATE)),
    ("w_dt", (DTR, EI)),
]
SMALL_ROWS = sum(math.prod(s) for _, s in SMALL) // LANES
GAIN_ROWS = 4 * DG // LANES
BIG = [
    ("w_in", D),
    ("w_out", EI),
    ("w_gu1", D),
    ("w_down1", FI),
    ("w_qkv", D * 3 * HW // D),
    ("w_o", HW),
    ("w_gu2", D),
    ("w_down2", FI),
]
BIG_OFF = {}
_at = 0
for _name, _rows in BIG:
    BIG_OFF[_name] = _at
    _at += _rows
BIG_ROWS = _at
LINES = D // LANES
FIRST = BIG_OFF["w_out"] * LINES
LEAD = GAIN_ROWS
CHUNK = 1024
SLACK = -(-(SMALL_ROWS + GAIN_ROWS) // CHUNK) * CHUNK


def group_bounds():
    bounds = []
    for k in range(4):
        bounds.append((k * DG, (k + 1) * DG))
    at = 4 * DG
    entries = [("w_in", D * 2 * EI)]
    entries += [(name, math.prod(shape)) for name, shape in SMALL]
    entries += [
        ("w_out", EI * D),
        ("w_gu1", D * 2 * FI),
        ("w_down1", FI * D),
        ("w_qkv", D * 3 * HW),
        ("w_o", HW * D),
        ("w_gu2", D * 2 * FI),
        ("w_down2", FI * D),
    ]
    for _, count in entries:
        bounds.append((at, at + count))
        at += count
    return bounds


def silu(v):
    return v * jax.nn.sigmoid(v)


def softplus(v):
    return jnp.maximum(v, 0.0) + jnp.log1p(jnp.exp(-jnp.abs(v)))


def mat_nn(a, b):
    return jnp.dot(a, b, preferred_element_type=F32)


def mat_tn(a, b):
    return lax.dot_general(a, b, (((0,), (0,)), ((), ())), preferred_element_type=F32)


def mat_nt(a, b):
    return lax.dot_general(a, b, (((1,), (1,)), ((), ())), preferred_element_type=F32)


def ring_pos(d, n):
    return jnp.where(lax.rem(d, 2) == 0, lax.div(d, 2), n - 1 - lax.div(d, 2))


def ring_dev(p, n):
    return jnp.where(p < n // 2, 2 * p, 2 * (n - 1 - p) + 1)


def ring_neighbours(n):
    d = lax.axis_index("dp")
    p = ring_pos(d, n)
    right = ring_dev(lax.rem(p + 1, n), n)
    left = ring_dev(lax.rem(p + n - 1, n), n)
    return d, p, right, left


def ring_barrier(left, right, t):
    barrier = pltpu.get_barrier_semaphore()
    for nb in (left, right):
        pl.semaphore_signal(barrier, inc=1, device_id=(nb, t), device_id_type=MESH)
    pl.semaphore_wait(barrier, 2)


def gather_kernel(n, subs, own_ref, out_ref, hold, local_sem, ssem, rsem):
    t = lax.axis_index("tensor")
    d, p, right, left = ring_neighbours(n)
    rows = own_ref.shape[0]
    half = rows // 2
    sub = half // subs
    fetch = pltpu.make_async_copy(own_ref, hold, local_sem.at[0])
    fetch.start()
    ring_barrier(left, right, t)

    def copy(way, step, c, from_own):
        target = right if way == 0 else left
        owner = ring_dev(lax.rem(p + (n - step if way == 0 else step), n), n)
        at = pl.multiple_of(owner * rows + way * half + c * sub, 8)
        src = own_ref.at[pl.ds(way * half + c * sub, sub)] if from_own else out_ref.at[pl.ds(at, sub)]
        return pltpu.make_async_remote_copy(
            src_ref=src,
            dst_ref=out_ref.at[pl.ds(at, sub)],
            send_sem=ssem.at[way, step, c],
            recv_sem=rsem.at[way, step, c],
            device_id=(target, t),
            device_id_type=MESH,
        )

    for c in range(subs):
        for way in (0, 1):
            copy(way, 0, c, True).start()
    fetch.wait()
    store = pltpu.make_async_copy(
        hold, out_ref.at[pl.ds(pl.multiple_of(d * rows, 8), rows)], local_sem.at[1]
    )
    store.start()
    for step in range(1, n - 1):
        for c in range(subs):
            for way in (0, 1):
                copy(way, step - 1, c, step == 1).wait_recv()
                copy(way, step, c, False).start()
    for c in range(subs):
        for way in (0, 1):
            copy(way, n - 2, c, n == 2).wait_recv()
    store.wait()
    for step in range(n - 1):
        for c in range(subs):
            for way in (0, 1):
                copy(way, step, c, step == 0).wait_send()


def ring_gather(own, n):
    rows, cols = own.shape
    subs = 2
    return pl.pallas_call(
        functools.partial(gather_kernel, n, subs),
        out_shape=jax.ShapeDtypeStruct((n * rows, cols), own.dtype),
        in_specs=[pl.BlockSpec(memory_space=pl.ANY)],
        out_specs=pl.BlockSpec(memory_space=pl.ANY),
        scratch_shapes=[
            pltpu.VMEM((rows, cols), own.dtype),
            pltpu.SemaphoreType.DMA((2,)),
            pltpu.SemaphoreType.DMA((2, n - 1, subs)),
            pltpu.SemaphoreType.DMA((2, n - 1, subs)),
        ],
        cost_estimate=pl.CostEstimate(flops=10**9, bytes_accessed=1500 * 10**6, transcendentals=0),
        compiler_params=pltpu.CompilerParams(
            collective_id=0, has_side_effects=True, vmem_limit_bytes=32 << 20
        ),
        name="ring_gather",
    )(own)


def piece_of(half):
    for size in (64, 32, 16):
        if half % size == 0:
            return size


def reduce_kernel(n, shard_lines, left_ref, right_refs, qkv_ref, out_ref, slots, lines, ssem, rsem, out_sem):
    t = lax.axis_index("tensor")
    d, p, right, left = ring_neighbours(n)
    rows = BIG_ROWS // n
    half = rows // 2
    SUB = piece_of(half)
    subs = half // SUB
    ring_barrier(left, right, t)
    qkv_at = BIG_OFF["w_qkv"]
    qkv_rows = dict(BIG)["w_qkv"]

    def own_into(at, put):
        in_qkv = jnp.logical_and(at >= qkv_at, at < qkv_at + qkv_rows)
        which = jnp.int32(0)
        for name, _ in BIG[1:]:
            if name != "w_qkv":
                which = which + jnp.where(at >= BIG_OFF[name], 1, 0)

        @pl.when(in_qkv)
        def _():
            put(qkv_ref[pl.ds(pl.multiple_of(at - qkv_at, SUB), SUB), :].astype(F32))

        @pl.when(jnp.logical_not(in_qkv))
        def _():
            row = jnp.where(at >= qkv_at + qkv_rows, at - qkv_rows, at)
            lt = left_ref[pl.ds(pl.multiple_of(row, SUB), SUB), :]
            put(jnp.dot(lt, right_refs[which], preferred_element_type=F32))

    def owner_of(way, step):
        return ring_dev(lax.rem(p + (n - 1 - step if way == 0 else 1 + step), n), n)

    def copy(way, step, c):
        target = right if way == 0 else left
        return pltpu.make_async_remote_copy(
            src_ref=slots.at[way, step, pl.ds(pl.multiple_of(c * SUB, SUB), SUB)],
            dst_ref=slots.at[way, step + 1, pl.ds(pl.multiple_of(c * SUB, SUB), SUB)],
            send_sem=ssem.at[way, step, c],
            recv_sem=rsem.at[way, step, c],
            device_id=(target, t),
            device_id_type=MESH,
        )

    def run(step):
        @pl.loop(0, subs)
        def _(c):
            here = pl.ds(pl.multiple_of(c * SUB, SUB), SUB)
            for way in (0, 1):
                at = owner_of(way, step) * rows + way * half + c * SUB
                if step > 0:
                    copy(way, step - 1, c).wait_recv()

                def put(value):
                    if step > 0:
                        value = value + slots[way, step, here, :].astype(F32)
                    if step < n - 1:
                        slots[way, step, here, :] = value.astype(BF)
                    else:
                        for j in range(LINES):
                            lines[way, pl.ds(j, SUB, stride=LINES), :] = value[:, j * LANES : (j + 1) * LANES]

                if step == n - 1:

                    @pl.when(c > 0)
                    def _():
                        leave(way, c - 1).wait()

                own_into(at, put)
                if step < n - 1:
                    copy(way, step, c).start()
                else:
                    leave(way, c).start()

    def leave(way, c):
        row = d * rows + way * half + c * SUB
        to = row * LINES + LEAD + jnp.where(row >= FIRST // LINES, SMALL_ROWS, 0) - d * shard_lines + SLACK
        return pltpu.make_async_copy(
            lines.at[way], out_ref.at[pl.ds(to, SUB * LINES), 0], out_sem.at[way]
        )

    for step in range(n):
        run(step)
    for way in (0, 1):
        leave(way, subs - 1).wait()

    @pl.loop(0, subs)
    def _(c):
        for way in (0, 1):
            for step in range(n - 1):
                copy(way, step, c).wait_send()


def ring_reduce(left_t, rights, qkv_grad, n, shard_lines):
    rows = BIG_ROWS // n
    sub = piece_of(rows // 2)
    subs = rows // 2 // sub
    vm = pl.BlockSpec(memory_space=pltpu.VMEM)
    return pl.pallas_call(
        functools.partial(reduce_kernel, n, shard_lines),
        out_shape=jax.ShapeDtypeStruct((shard_lines + 2 * SLACK, 1, LANES), F32),
        in_specs=[vm, vm, vm],
        out_specs=pl.BlockSpec(memory_space=pl.ANY),
        scratch_shapes=[
            pltpu.VMEM((2, n, rows // 2, D), BF),
            pltpu.VMEM((2, sub * LINES, LANES), F32),
            pltpu.SemaphoreType.DMA((2, n - 1, subs)),
            pltpu.SemaphoreType.DMA((2, n - 1, subs)),
            pltpu.SemaphoreType.DMA((2,)),
        ],
        cost_estimate=pl.CostEstimate(flops=10**9, bytes_accessed=1500 * 10**6, transcendentals=0),
        compiler_params=pltpu.CompilerParams(
            collective_id=1, has_side_effects=True, vmem_limit_bytes=67043328
        ),
        name="ring_reduce",
    )(left_t, rights, qkv_grad)


def spread(ref, value):
    rows = value.shape[0]
    for j in range(EI // LANES):
        ref[pl.ds(j, rows, stride=EI // LANES), :] = value[:, j * LANES : (j + 1) * LANES]


def collect(ref, rows):
    return jnp.concatenate(
        [ref[pl.ds(j, rows, stride=EI // LANES), :] for j in range(EI // LANES)], axis=1
    )


SUBL = EI // LANES


def scan_kernel(slots, proj_ref, bc_ref, unit_ref, gate_ref, w_dt_ref, bias_ref, skip_ref, alog_ref,
                gated_ref, step_s, su_s, y_s, rate_s):
    pre = jnp.dot(proj_ref[:, :DTR], w_dt_ref[...], preferred_element_type=F32) + bias_ref[...]
    step = softplus(pre)
    unit = unit_ref[...].astype(F32)
    spread(step_s, step)
    spread(su_s, step * unit)
    rate_s[...] = -jnp.exp(alog_ref[...]) * LOG2E

    def body(t, states):
        new = []
        for m in range(slots):
            r = m * SLOT + t
            row = pl.ds(pl.multiple_of(r * SUBL, SUBL), SUBL)
            st = step_s[row, :]
            su = su_s[row, :]
            y = jnp.zeros((SUBL, LANES), F32)
            for k in range(NSTATE):
                dec = jnp.exp2(rate_s[k * SUBL : (k + 1) * SUBL, :] * st)
                s = dec * states[m * NSTATE + k] + bc_ref[r, k] * su
                y = y + bc_ref[r, NSTATE + k] * s
                new.append(s)
            y_s[row, :] = y
        return tuple(new)

    init = tuple(jnp.zeros((SUBL, LANES), F32) for _ in range(slots * NSTATE))
    lax.fori_loop(0, SLOT, body, init)
    y = collect(y_s, slots * SLOT) + skip_ref[...] * unit
    z = gate_ref[...]
    gated_ref[...] = (y * silu(z)).astype(BF)


def scan_forward(proj, bc, unit, gate, w_dt, dt_bias, d_skip, a_log):
    rows = unit.shape[0]
    vm = pl.BlockSpec(memory_space=pltpu.VMEM)
    sm = pl.BlockSpec(memory_space=pltpu.SMEM)
    return pl.pallas_call(
        functools.partial(scan_kernel, rows // SLOT),
        out_shape=jax.ShapeDtypeStruct((rows, EI), BF),
        in_specs=[vm, sm, vm, vm, vm, vm, vm, vm],
        out_specs=vm,
        scratch_shapes=[
            pltpu.VMEM((rows * SUBL, LANES), F32),
            pltpu.VMEM((rows * SUBL, LANES), F32),
            pltpu.VMEM((rows * SUBL, LANES), F32),
            pltpu.VMEM((NSTATE * SUBL, LANES), F32),
        ],
        compiler_params=pltpu.CompilerParams(vmem_limit_bytes=60 << 20),
        name="scan_forward",
    )(proj, bc, unit, gate, w_dt, dt_bias, d_skip, a_log)


def adjoint_kernel(slots, proj_ref, bc_ref, unit_ref, gate_ref, w_dt_ref, bias_ref, skip_ref, alog_ref,
                   grad_ref, gz_ref, gunit_ref, gproj_ref, gdt_ref, gbias_ref, gskip_ref, galog_ref,
                   step_s, su_s, unit_s, y_s, gy_s, gs_s, lb_s, rate_s, hist, lams):
    rows = slots * SLOT
    pre = jnp.dot(proj_ref[:, :DTR], w_dt_ref[...], preferred_element_type=F32) + bias_ref[...]
    step = softplus(pre)
    unit = unit_ref[...].astype(F32)
    spread(step_s, step)
    spread(unit_s, unit)
    spread(su_s, step * unit)
    z = gate_ref[...]
    sig = jax.nn.sigmoid(z)
    gg = grad_ref[...]
    gy = gg * z * sig
    spread(gy_s, gy)
    rate_s[...] = -jnp.exp(alog_ref[...])
    galog_ref[...] = jnp.zeros_like(galog_ref)
    zero = jnp.zeros((SUBL, LANES), F32)
    span = SLOT + 1

    def hist_at(k, t):
        return pl.ds(pl.multiple_of((k * span + t) * SUBL, SUBL), SUBL)

    def lam_at(k, t):
        return pl.ds(pl.multiple_of((k * SLOT + t) * SUBL, SUBL), SUBL)

    for m in range(slots):
        for k in range(NSTATE):
            hist[hist_at(k, 0), :] = zero

        def forward(t, states):
            r = m * SLOT + t
            row = pl.ds(pl.multiple_of(r * SUBL, SUBL), SUBL)
            st = step_s[row, :] * LOG2E
            su = su_s[row, :]
            y = zero
            new = []
            for k in range(NSTATE):
                dec = jnp.exp2(rate_s[k * SUBL : (k + 1) * SUBL, :] * st)
                s = dec * states[k] + bc_ref[r, k] * su
                y = y + bc_ref[r, NSTATE + k] * s
                hist[hist_at(k, t + 1), :] = s
                new.append(s)
            y_s[row, :] = y
            return tuple(new)

        lax.fori_loop(0, SLOT, forward, tuple(zero for _ in range(NSTATE)))

        def backward(i, carry):
            t = SLOT - 1 - i
            r = m * SLOT + t
            row = pl.ds(pl.multiple_of(r * SUBL, SUBL), SUBL)
            st = step_s[row, :]
            st2 = st * LOG2E
            gyt = gy_s[row, :]
            lb = zero
            gs = zero
            new = []
            for k in range(NSTATE):
                rate = rate_s[k * SUBL : (k + 1) * SUBL, :]
                dec = jnp.exp2(rate * st2)
                lam = bc_ref[r, NSTATE + k] * gyt + carry[k]
                ld = dec * lam
                new.append(ld)
                lams[lam_at(k, t), :] = lam
                lb = lb + bc_ref[r, k] * lam
                x = ld * hist[hist_at(k, t), :]
                gs = gs + rate * x
                at = slice(k * SUBL, (k + 1) * SUBL)
                galog_ref[at, :] = galog_ref[at, :] + st * x
            lb_s[row, :] = lb
            gs_s[row, :] = gs + unit_s[row, :] * lb
            return tuple(new)

        lax.fori_loop(0, SLOT, backward, tuple(zero for _ in range(NSTATE)))
        out = slice(m * SLOT, (m + 1) * SLOT)
        base = m * SLOT * SUBL

        lane = lax.broadcasted_iota(jnp.int32, (SLOT, LANES), 1)

        def reduce_state(k, acc):
            ab = jnp.zeros((SLOT, LANES), F32)
            ac = jnp.zeros((SLOT, LANES), F32)
            for j in range(SUBL):
                cols = slice(j * LANES, (j + 1) * LANES)
                lam = lams[pl.ds(k * SLOT * SUBL + j, SLOT, stride=SUBL), :]
                h = hist[pl.ds((k * span + 1) * SUBL + j, SLOT, stride=SUBL), :]
                sj = su_s[pl.ds(base + j, SLOT, stride=SUBL), :]
                gj = gy_s[pl.ds(base + j, SLOT, stride=SUBL), :]
                ab = ab + lam * sj
                ac = ac + h * gj
            sb = jnp.sum(ab, axis=1, keepdims=True)
            sc = jnp.sum(ac, axis=1, keepdims=True)
            return acc + jnp.where(lane == k, sb, 0.0) + jnp.where(lane == NSTATE + k, sc, 0.0)

        sums = lax.fori_loop(0, NSTATE, reduce_state, jnp.zeros((SLOT, LANES), F32))
        gproj_ref[out, DTR : DTR + LANES] = sums.astype(BF)
    galog_ref[...] = galog_ref[...] * rate_s[...]
    y = collect(y_s, rows) + skip_ref[...] * unit
    gz_ref[...] = (gg * y * sig * (1.0 + z * (1.0 - sig))).astype(BF)
    gunit_ref[...] = gy * skip_ref[...] + step * collect(lb_s, rows)
    gskip_ref[...] = jnp.sum(gy * unit, axis=0, keepdims=True)
    q = collect(gs_s, rows) * jax.nn.sigmoid(pre)
    gbias_ref[...] = jnp.sum(q, axis=0, keepdims=True)
    ql = q.astype(BF)
    gdt_ref[...] = mat_tn(proj_ref[:, :DTR], ql)
    gproj_ref[:, :DTR] = mat_nt(ql, w_dt_ref[...]).astype(BF)


def scan_backward(proj, bc, unit, gate, w_dt, dt_bias, d_skip, a_log, grad):
    rows = unit.shape[0]
    vm = pl.BlockSpec(memory_space=pltpu.VMEM)
    sm = pl.BlockSpec(memory_space=pltpu.SMEM)
    sds = jax.ShapeDtypeStruct
    flat = pltpu.VMEM((rows * SUBL, LANES), F32)
    return pl.pallas_call(
        functools.partial(adjoint_kernel, rows // SLOT),
        out_shape=(
            sds((rows, EI), BF),
            sds((rows, EI), F32),
            sds((rows, DTR + LANES), BF),
            sds((DTR, EI), F32),
            sds((1, EI), F32),
            sds((1, EI), F32),
            sds((NSTATE * SUBL, LANES), F32),
        ),
        in_specs=[vm, sm, vm, vm, vm, vm, vm, vm, vm],
        out_specs=(vm,) * 7,
        scratch_shapes=[flat] * 7
        + [
            pltpu.VMEM((NSTATE * SUBL, LANES), F32),
            pltpu.VMEM((NSTATE * (SLOT + 1) * SUBL, LANES), F32),
            pltpu.VMEM((NSTATE * SLOT * SUBL, LANES), F32),
        ],
        compiler_params=pltpu.CompilerParams(vmem_limit_bytes=60 << 20),
        name="scan_backward",
    )(proj, bc, unit, gate, w_dt, dt_bias, d_skip, a_log, grad)


def rope_tables(length, head_dim):
    half_dim = head_dim // 2
    freq_index = jnp.arange(half_dim, dtype=F32)
    inv_freq = jnp.exp(-math.log(ROPE_BASE) * 2.0 * freq_index / head_dim)
    angles = jnp.arange(length, dtype=F32)[:, None] * inv_freq[None, :]
    return (jnp.cos(angles)[None, :, None, :], jnp.sin(angles)[None, :, None, :])


def rope_apply(values, cosine, sine):
    half_dim = values.shape[-1] // 2
    a = values[..., :half_dim]
    b = values[..., half_dim:]
    return jnp.concatenate([a * cosine - b * sine, b * cosine + a * sine], axis=-1)


def rms_parts(v, g):
    s = lax.rsqrt(jnp.mean(v * v, axis=-1, keepdims=True) + EPS_NORM)
    return s, v * s


def rms_back(v, g, gh):
    s, nrm = rms_parts(v, g)
    gg = jnp.sum(gh * nrm, axis=0)
    gv = s * (gh * g - nrm * jnp.mean(gh * g * nrm, axis=-1, keepdims=True))
    return gv, gg


def total(partial_out):
    return lax.psum(partial_out.astype(BF), "tensor").astype(F32)


def shift_down(v, by):
    if by == 0:
        return v
    return jnp.pad(v, ((0, 0), (by, 0), (0, 0)))[:, : v.shape[1]]


def shift_up(v, by):
    if by == 0:
        return v
    return jnp.pad(v, ((0, 0), (0, by), (0, 0)))[:, by:]


def attend(query, keys, values):
    scale = HEAD_DIM ** (-0.5)
    distance = jnp.arange(SLOT)[:, None] - jnp.arange(SLOT)[None, :]
    allowed = (distance >= 0) & (distance < WINDOW)
    scores = jnp.einsum("mqhd,mkhd->mhqk", query, keys, preferred_element_type=F32) * scale
    scores = jnp.where(allowed, scores, NEG_FILL)
    expo = jnp.exp(scores - jnp.max(scores, axis=-1, keepdims=True))
    return expo / jnp.sum(expo, axis=-1, keepdims=True)


def ffn_forward(h, w_gu, w_down):
    pre = mat_nn(h, w_gu)
    act = (silu(pre[:, :FI]) * pre[:, FI:]).astype(BF)
    return total(mat_nn(act, w_down)), pre, act


def ffn_backward(pre, w_gu, w_down, grad_low):
    gate = pre[:, :FI]
    up = pre[:, FI:]
    ga = mat_nt(grad_low, w_down)
    sig = jax.nn.sigmoid(gate)
    grad_gate = ga * up * sig * (1.0 + gate * (1.0 - sig))
    grad_up = ga * gate * sig
    gp = jnp.concatenate([grad_gate, grad_up], axis=1).astype(BF)
    return total(mat_nt(gp, w_gu)), gp


def layer(x, grad_out, w, small, gains, n):
    rows = x.shape[0]
    m = rows // SLOT
    hr = HW // HEAD_DIM
    cosine, sine = rope_tables(SLOT, HEAD_DIM)
    s1, n1 = rms_parts(x, gains[0])
    h1 = (n1 * gains[0]).astype(BF)
    mixed = mat_nn(h1, w["w_in"])
    mix_x = mixed[:, :EI].reshape(m, SLOT, EI)
    gate_z = mixed[:, EI:]
    conv_w = small["conv_w"].astype(F32)
    pre_conv = small["conv_b"].astype(F32)[None, None, :]
    for j in range(CONV):
        pre_conv = pre_conv + conv_w[j] * shift_down(mix_x, CONV - 1 - j)
    unit = silu(pre_conv).astype(BF).reshape(rows, EI)
    proj = lax.psum(mat_nn(unit, small["w_x"]).astype(BF), "tensor")
    bc = proj[:, DTR:].astype(F32)
    scan_args = (
        proj[:, :DTR],
        bc,
        unit,
        gate_z,
        small["w_dt"],
        small["dt_bias"].astype(F32)[None],
        small["d_skip"].astype(F32)[None],
        small["a_log"].astype(F32).reshape(NSTATE * SUBL, LANES),
    )
    gated = scan_forward(*scan_args)
    x1 = x + total(mat_nn(gated, w["w_out"]))
    h2 = (rms_parts(x1, 0)[1] * gains[1]).astype(BF)
    branch, pre1, act1 = ffn_forward(h2, w["w_gu1"], w["w_down1"])
    x2 = x1 + branch
    h3 = (rms_parts(x2, 0)[1] * gains[2]).astype(BF)
    packed = mat_nn(h3, w["w_qkv"]).reshape(m, SLOT, 3, hr, HEAD_DIM)
    query = rope_apply(packed[:, :, 0], cosine, sine).astype(BF)
    keys = rope_apply(packed[:, :, 1], cosine, sine).astype(BF)
    values = packed[:, :, 2].astype(BF)
    probs = attend(query, keys, values)
    probs_low = probs.astype(BF)
    attended = jnp.einsum("mhqk,mkhd->mqhd", probs_low, values, preferred_element_type=F32)
    attended = attended.reshape(rows, HW).astype(BF)
    x3 = x2 + total(mat_nn(attended, w["w_o"]))
    h4 = (rms_parts(x3, 0)[1] * gains[3]).astype(BF)
    branch, pre2, act2 = ffn_forward(h4, w["w_gu2"], w["w_down2"])
    x4 = x3 + branch

    gb4 = grad_out.astype(BF)
    gh, gp2 = ffn_backward(pre2, w["w_gu2"], w["w_down2"], gb4)
    gv, gg4 = rms_back(x3, gains[3], gh)
    g3 = grad_out + gv
    gb3 = g3.astype(BF)
    gatt = mat_nt(gb3, w["w_o"]).astype(BF).reshape(m, SLOT, hr, HEAD_DIM)
    grad_p = jnp.einsum("mqhd,mkhd->mhqk", gatt, values, preferred_element_type=F32)
    inner = jnp.sum(probs * grad_p, axis=-1, keepdims=True)
    gs = (probs * (grad_p - inner)).astype(BF)
    scale = HEAD_DIM ** (-0.5)
    gq = jnp.einsum("mhqk,mkhd->mqhd", gs, keys, preferred_element_type=F32) * scale
    gk = jnp.einsum("mhqk,mqhd->mkhd", gs, query, preferred_element_type=F32) * scale
    gvv = jnp.einsum("mhqk,mqhd->mkhd", probs_low, gatt, preferred_element_type=F32)
    gpk = (
        jnp.stack([rope_apply(gq, cosine, -sine), rope_apply(gk, cosine, -sine), gvv], axis=2)
        .reshape(rows, 3 * HW)
        .astype(BF)
    )
    gv, gg3 = rms_back(x2, gains[2], total(mat_nt(gpk, w["w_qkv"])))
    g2 = g3 + gv
    gb2 = g2.astype(BF)
    gh, gp1 = ffn_backward(pre1, w["w_gu1"], w["w_down1"], gb2)
    gv, gg2 = rms_back(x1, gains[1], gh)
    g1 = g2 + gv
    gb1 = g1.astype(BF)
    ggated = mat_nt(gb1, w["w_out"])
    gz, gunit, gproj, g_dt, g_bias, g_skip, g_alog = scan_backward(*scan_args, ggated)
    gproj = lax.psum(gproj[:, : DTR + 2 * NSTATE], "tensor")
    g_wx = mat_tn(unit, gproj)
    gu = gunit + mat_nt(gproj, small["w_x"])
    sig = jax.nn.sigmoid(pre_conv)
    gpre = gu.reshape(m, SLOT, EI) * sig * (1.0 + pre_conv * (1.0 - sig))
    g_conv_b = jnp.sum(gpre, axis=(0, 1))
    g_conv_w = jnp.stack(
        [jnp.sum(gpre * shift_down(mix_x, CONV - 1 - j), axis=(0, 1)) for j in range(CONV)]
    )
    gmx = sum(conv_w[j] * shift_up(gpre, CONV - 1 - j) for j in range(CONV))
    gmixed = jnp.concatenate([gmx.reshape(rows, EI).astype(BF), gz], axis=1)
    gv, gg1 = rms_back(x, gains[0], total(mat_nt(gmixed, w["w_in"])))
    g0 = g1 + gv

    left_t = jnp.concatenate([h1, gated, h2, act1, attended, h4, act2], axis=1).T
    rights = jnp.stack([gmixed, gb1, gp1, gb2, gb3, gp2, gb4])
    g_qkv = mat_tn(h3, gpk).astype(BF).reshape(-1, D)
    start = lax.axis_index("tensor") * DG
    g_gain = lax.dynamic_slice_in_dim(jnp.stack([gg1, gg2, gg3, gg4]), start, DG, 1)
    pieces = [g_gain, g_conv_w, g_conv_b, g_bias, g_skip, g_alog, g_wx, g_dt]
    small_grads = jnp.concatenate([p.reshape(-1, LANES).astype(BF) for p in pieces])
    small_grads, left_t = lax.optimization_barrier((small_grads, left_t))
    return x4.astype(BF), g0, (left_t, rights, g_qkv), small_grads


def extents(n, shard_rows):
    slab = BIG_ROWS * LINES // n
    before = 0
    after = 0
    back_before = 0
    back_after = 0
    for d in range(n):
        lo, hi = slab * d, slab * (d + 1) - 1
        qs = [p + LEAD + (SMALL_ROWS if p >= FIRST else 0) - shard_rows * d for p in (lo, hi)]
        before = max(before, -qs[0])
        after = max(after, qs[1] + 1 - shard_rows)
    return before, after


def shift_perm(n, by):
    return [(i, i + by) for i in range(n) if 0 <= i + by < n]


def stack_kernel(n, shard_lines, before, per, top_ref, own_ref, bottom_ref, out_ref, hold, sem):
    d = lax.axis_index("dp")
    i = pl.program_id(0)
    steps = BIG_ROWS // n // per
    size = per * LINES

    def fetch(k, slot):
        row = d * (BIG_ROWS // n) + k * per
        a = row * LINES + LEAD + jnp.where(row >= FIRST // LINES, SMALL_ROWS, 0) - d * shard_lines
        high = a < 0
        low = a + size > shard_lines

        @pl.when(high)
        def _():
            pltpu.make_async_copy(top_ref.at[pl.ds(a + before, size), 0], hold.at[slot], sem.at[slot]).start()

        @pl.when(low)
        def _():
            pltpu.make_async_copy(
                bottom_ref.at[pl.ds(a + size - shard_lines, size), 0], hold.at[slot], sem.at[slot]
            ).start()

        @pl.when(jnp.logical_not(jnp.logical_or(high, low)))
        def _():
            pltpu.make_async_copy(own_ref.at[pl.ds(a, size), 0], hold.at[slot], sem.at[slot]).start()

    @pl.when(i == 0)
    def _():
        for k in range(min(3, steps)):
            fetch(k, k)

    @pl.when(i + 3 < steps)
    def _():
        fetch(i + 3, lax.rem(i + 3, 4))

    slot = lax.rem(i, 4)
    pltpu.make_async_copy(own_ref.at[pl.ds(0, size), 0], hold.at[slot], sem.at[slot]).wait()
    for j in range(LINES):
        out_ref[:, j * LANES : (j + 1) * LANES] = hold[slot, pl.ds(j, per, stride=LINES), :].astype(BF)


def stack_own(lines3, n):
    shard_lines = lines3.shape[0]
    before, after = extents(n, shard_lines)
    rows = BIG_ROWS // n
    per = 64 if rows % 64 == 0 else 32
    size = per * LINES
    nxt = lax.ppermute(lines3[:after], "dp", shift_perm(n, -1))
    prv = lax.ppermute(lines3[shard_lines - before :], "dp", shift_perm(n, 1))
    top = jnp.concatenate([prv, lines3[:size]])
    bottom = jnp.concatenate([lines3[shard_lines - size :], nxt])
    hbm = pl.BlockSpec(memory_space=pl.ANY)
    return pl.pallas_call(
        functools.partial(stack_kernel, n, shard_lines, before, per),
        grid=(rows // per,),
        out_shape=jax.ShapeDtypeStruct((rows, D), BF),
        in_specs=[hbm] * 3,
        out_specs=pl.BlockSpec((per, D), lambda i: (i, 0)),
        scratch_shapes=[pltpu.VMEM((4, size, LANES), F32), pltpu.SemaphoreType.DMA((4,))],
        compiler_params=pltpu.CompilerParams(vmem_limit_bytes=24 << 20),
        name="stack_own",
    )(top, lines3, bottom)


def window(values, shift, size):
    length = values.shape[0]
    s = jnp.clip(shift, 0, length - size)
    got = lax.dynamic_slice_in_dim(values, s, size, 0)
    room = jnp.zeros((3 * size,) + values.shape[1:], values.dtype)
    room = lax.dynamic_update_slice_in_dim(room, got, size + jnp.clip(s - shift, -size, size), 0)
    return room[size : 2 * size]


def moments_kernel(groups, shard, bounds_ref, grad_ref, w_ref, one_ref, two_ref,
                   first_ref, second_ref, grad_out, sums_ref, hold):
    i = pl.program_id(0)
    size = CHUNK * LANES

    @pl.when(i == 0)
    def _():
        @pl.loop(0, 2 * groups)
        def _(g):
            sums_ref[g] = 0.0

    grad = grad_ref[...]
    w = w_ref[...]
    first = BETA_ONE * one_ref[...] + (1.0 - BETA_ONE) * grad
    second = BETA_TWO * two_ref[...] + (1.0 - BETA_TWO) * grad * grad
    first_ref[...] = first
    second_ref[...] = second
    grad_out[...] = grad
    hold[...] = first / (jnp.sqrt(second) + ADAM_EPS) + DECAY_W * w
    d = lax.axis_index("dp")
    start = d * shard + i * size
    stop = jnp.minimum(start + size, (d + 1) * shard)

    @pl.loop(0, groups)
    def _(g):
        low = jnp.maximum(bounds_ref[2 * g], start)
        high = jnp.minimum(bounds_ref[2 * g + 1], stop)

        @pl.when(low < high)
        def _():
            index = start + lax.broadcasted_iota(jnp.int32, (1, size), 1)
            inside = (index >= low) & (index < high)
            wv = w_ref[...]
            rv = hold[...]
            sums_ref[2 * g] = sums_ref[2 * g] + jnp.sum(jnp.where(inside, wv * wv, 0.0))
            sums_ref[2 * g + 1] = sums_ref[2 * g + 1] + jnp.sum(jnp.where(inside, rv * rv, 0.0))


def moments(bounds, lines, master, one, two):
    shard = master.shape[1]
    size = CHUNK * LANES
    groups = bounds.shape[0] // 2
    block = pl.BlockSpec((1, size), lambda i: (0, i))
    ahead = SLACK // CHUNK
    flat = jax.ShapeDtypeStruct((1, shard), F32)
    smem = pl.BlockSpec(memory_space=pltpu.SMEM)
    return pl.pallas_call(
        functools.partial(moments_kernel, groups, shard),
        grid=(pl.cdiv(shard, size),),
        out_shape=(flat, flat, flat, jax.ShapeDtypeStruct((2 * groups,), F32)),
        in_specs=[smem, pl.BlockSpec((1, size), lambda i: (0, i + ahead)), block, block, block],
        out_specs=(block, block, block, smem),
        scratch_shapes=[pltpu.VMEM((1, size), F32)],
        compiler_params=pltpu.CompilerParams(vmem_limit_bytes=40 << 20),
        name="moments",
    )(bounds, lines.reshape(1, -1), master, one, two)


def update_kernel(groups, shard, bounds_ref, trust_ref, w_ref, first_ref, second_ref, new_ref, low_ref, hold):
    i = pl.program_id(0)
    size = CHUNK * LANES
    d = lax.axis_index("dp")
    start = d * shard + i * size
    hold[...] = jnp.zeros_like(hold)

    @pl.loop(0, groups)
    def _(g):
        low = jnp.maximum(bounds_ref[2 * g], start)
        high = jnp.minimum(bounds_ref[2 * g + 1], start + size)

        @pl.when(low < high)
        def _():
            index = start + lax.broadcasted_iota(jnp.int32, (1, size), 1)
            hold[...] = jnp.where((index >= low) & (index < high), trust_ref[g], hold[...])

    w = w_ref[...]
    ratio = first_ref[...] / (jnp.sqrt(second_ref[...]) + ADAM_EPS) + DECAY_W * w
    new = w - LEARN_RATE * hold[...] * ratio
    new_ref[...] = new
    low_ref[...] = new.astype(BF)


def update(bounds, trust, master, first, second):
    shard = master.shape[1]
    size = CHUNK * LANES
    groups = bounds.shape[0] // 2
    block = pl.BlockSpec((1, size), lambda i: (0, i))
    smem = pl.BlockSpec(memory_space=pltpu.SMEM)
    return pl.pallas_call(
        functools.partial(update_kernel, groups, shard),
        grid=(pl.cdiv(shard, size),),
        out_shape=(jax.ShapeDtypeStruct((1, shard), F32), jax.ShapeDtypeStruct((1, shard), BF)),
        in_specs=[smem, smem, block, block, block],
        out_specs=(block, block),
        scratch_shapes=[pltpu.VMEM((1, size), F32)],
        compiler_params=pltpu.CompilerParams(vmem_limit_bytes=40 << 20),
        name="update",
    )(bounds, trust, master, first, second)


def norms_kernel(n, m, own_ref, out_ref, across, along, part, ssem, rsem, ssem2, rsem2):
    d = lax.axis_index("dp")
    t = lax.axis_index("tensor")
    barrier = pltpu.get_barrier_semaphore()
    for k in range(1, m):
        pl.semaphore_signal(barrier, inc=1, device_id=(d, lax.rem(t + k, m)), device_id_type=MESH)

    @pl.loop(1, n)
    def _(k):
        pl.semaphore_signal(barrier, inc=1, device_id=(lax.rem(d + k, n), t), device_id_type=MESH)

    pl.semaphore_wait(barrier, n + m - 2)

    def over_tensor(k):
        return pltpu.make_async_remote_copy(
            src_ref=own_ref,
            dst_ref=across.at[k - 1],
            send_sem=ssem.at[k - 1],
            recv_sem=rsem.at[k - 1],
            device_id=(d, lax.rem(t + k, m)),
            device_id_type=MESH,
        )

    def over_dp(k):
        return pltpu.make_async_remote_copy(
            src_ref=part,
            dst_ref=along.at[k - 1],
            send_sem=ssem2.at[k - 1],
            recv_sem=rsem2.at[k - 1],
            device_id=(lax.rem(d + k, n), t),
            device_id_type=MESH,
        )

    for k in range(1, m):
        over_tensor(k).start()
    total_ = own_ref[...]
    for k in range(1, m):
        over_tensor(k).wait_recv()
    for k in range(1, m):
        total_ = total_ + across[k - 1]
    part[...] = total_

    @pl.loop(1, n)
    def _(k):
        over_dp(k).start()

    @pl.loop(1, n)
    def _(k):
        over_dp(k).wait_recv()

    def add(k, acc):
        return acc + along[k - 1]

    out_ref[...] = lax.fori_loop(1, n, add, part[...])
    for k in range(1, m):
        over_tensor(k).wait_send()

    @pl.loop(1, n)
    def _(k):
        over_dp(k).wait_send()


def sum_everywhere(values, n, m):
    vm = pl.BlockSpec(memory_space=pltpu.VMEM)
    dma = pltpu.SemaphoreType.DMA
    tile = pltpu.VMEM((8, LANES), F32)
    return pl.pallas_call(
        functools.partial(norms_kernel, n, m),
        out_shape=jax.ShapeDtypeStruct((8, LANES), F32),
        in_specs=[vm],
        out_specs=vm,
        scratch_shapes=[
            pltpu.VMEM((m - 1, 8, LANES), F32),
            pltpu.VMEM((n - 1, 8, LANES), F32),
            tile,
            dma((m - 1,)),
            dma((m - 1,)),
            dma((n - 1,)),
            dma((n - 1,)),
        ],
        compiler_params=pltpu.CompilerParams(collective_id=2, has_side_effects=True),
        name="sum_everywhere",
    )(values)


def per_device(n, m, tokens, cotangent, lengths, master, moment_one, moment_two):
    d = lax.axis_index("dp")
    shard = master.shape[1]
    lines = shard // LANES
    lines3 = master.reshape(lines, 1, LANES)
    base = d * lines
    mid = LEAD + FIRST
    small_own = jnp.concatenate(
        [window(lines3, -base, GAIN_ROWS), window(lines3, mid - base, SMALL_ROWS)]
    )
    small_flat = lax.psum(small_own.reshape(-1, LANES).astype(BF), "dp")
    gains = lax.all_gather(small_flat[:GAIN_ROWS].reshape(4, DG), "tensor", axis=1, tiled=True)
    gains = gains.astype(F32)
    small = {}
    at = GAIN_ROWS
    for name, shape in SMALL:
        count = math.prod(shape) // LANES
        small[name] = small_flat[at : at + count].reshape(shape)
        at += count
    weights = ring_gather(stack_own(lines3, n), n)
    w = {}
    for name, rows in BIG:
        w[name] = weights[BIG_OFF[name] : BIG_OFF[name] + rows]
    w["w_qkv"] = w["w_qkv"].reshape(D, 3 * HW)
    x = tokens.astype(F32)
    pos = lax.broadcasted_iota(jnp.int32, (tokens.shape[0] // SLOT, SLOT), 1)
    valid = (pos < lengths[:, None]).astype(F32).reshape(-1, 1)
    grad = cotangent.astype(F32) * valid
    out, grad_in, operands, small_grads = layer(x, grad, w, small, gains, n)
    small_sum = lax.psum(small_grads, "dp").astype(F32).reshape(-1, 1, LANES)
    laid = ring_reduce(*operands, n, lines)

    before, after = extents(n, lines)
    slab_lines = BIG_ROWS * LINES // n

    def local(row):
        return row * LINES + LEAD + jnp.where(row >= FIRST // LINES, SMALL_ROWS, 0) - base

    begin = local(d * (BIG_ROWS // n))
    close = local((d + 1) * (BIG_ROWS // n) - 1) + LINES
    from_prev = lax.ppermute(laid[SLACK + lines : SLACK + lines + after], "dp", shift_perm(n, 1))
    from_next = lax.ppermute(laid[SLACK - before : SLACK], "dp", shift_perm(n, -1))
    line = lax.broadcasted_iota(jnp.int32, (after, 1, 1), 0)
    top = jnp.where(line < begin, from_prev, laid[SLACK : SLACK + after])
    line = lax.broadcasted_iota(jnp.int32, (before, 1, 1), 0) + (lines - before)
    bottom = jnp.where(line >= close, from_next, laid[SLACK + lines - before : SLACK + lines])
    laid = laid.at[SLACK : SLACK + after].set(top)
    laid = laid.at[SLACK + lines - before : SLACK + lines].set(bottom)

    def place(laid, values, at):
        count = values.shape[0]
        return lax.dynamic_update_slice_in_dim(laid, values, SLACK + jnp.clip(at - base, -count, lines), 0)

    laid = place(laid, small_sum[GAIN_ROWS:], mid)
    laid = place(laid, small_sum[:GAIN_ROWS], 0)
    used = LEAD + SMALL_ROWS + BIG_ROWS * LINES
    rest = lines * n - used
    if rest:
        laid = place(laid, jnp.zeros((rest, 1, LANES), F32), used)

    bounds = jnp.asarray([v for pair in group_bounds() for v in pair], jnp.int32)
    first, second, grad_shard, sums = moments(bounds, laid, master, moment_one, moment_two)
    count = sums.shape[0]
    tile = jnp.pad(sums, (0, 8 * LANES - count)).reshape(8, LANES)
    squares = sum_everywhere(tile, n, m).reshape(-1)[:count].reshape(-1, 2)
    trust = jnp.sqrt(squares[:, 0] + TRUST_EPSILON) * lax.rsqrt(squares[:, 1] + TRUST_EPSILON)
    master_new, low = update(bounds, trust, master, first, second)
    return (out, grad_in, master_new, first, second, low, grad_shard, jnp.sqrt(squares))


def solution(mesh):
    row = P("dp", None)
    flat = P("tensor", "dp")
    return jax.shard_map(
        functools.partial(per_device, mesh.shape["dp"], mesh.shape["tensor"]),
        mesh=mesh,
        in_specs=(row, row, P("dp"), flat, flat, flat),
        out_specs=(row, row, flat, flat, flat, flat, flat, P()),
        check_vma=False,
    )
```

```python
import functools
import math

import jax
import jax.numpy as jnp
from jax import lax
from jax.experimental import pallas as pl
from jax.experimental.pallas import tpu as pltpu
from jax.sharding import PartitionSpec as P

D = 2048
INNER = 4096
NSTATE = 16
DTR = 128
HEADS = 32
HEAD_DIM = 64
FF = 4096
CONV = 4
WINDOW = 2048
SLOT = 128
LANES = 128

EPS_NORM = 1e-05
TRUST_EPSILON = 1e-06
ROPE_BASE = 10000.0
BETA_ONE = 0.5
BETA_TWO = 0.55
ADAM_EPS = 1e-06
DECAY_W = 0.01
LEARN_RATE = 0.2
NEG_FILL = -1e30
LOG2E = 1.4426950408889634
MESH = pl.DeviceIdType.MESH
BF = jnp.bfloat16
F32 = jnp.float32

EI = INNER // 4
FI = FF // 4
HW = HEADS * HEAD_DIM // 4
DG = D // 4

SMALL = [
    ("conv_w", (CONV, EI)),
    ("conv_b", (EI,)),
    ("dt_bias", (EI,)),
    ("d_skip", (EI,)),
    ("a_log", (NSTATE, EI)),
    ("w_x", (EI, DTR + 2 * NSTATE)),
    ("w_dt", (DTR, EI)),
]
SMALL_ROWS = sum(math.prod(s) for _, s in SMALL) // LANES
GAIN_ROWS = 4 * DG // LANES
BIG = [
    ("w_in", D),
    ("w_out", EI),
    ("w_gu1", D),
    ("w_down1", FI),
    ("w_qkv", D * 3 * HW // D),
    ("w_o", HW),
    ("w_gu2", D),
    ("w_down2", FI),
]
BIG_OFF = {}
_at = 0
for _name, _rows in BIG:
    BIG_OFF[_name] = _at
    _at += _rows
BIG_ROWS = _at
LINES = D // LANES
FIRST = BIG_OFF["w_out"] * LINES
LEAD = GAIN_ROWS
CHUNK = 1024
SLACK = -(-(SMALL_ROWS + GAIN_ROWS) // CHUNK) * CHUNK


def group_bounds():
    bounds = []
    for k in range(4):
        bounds.append((k * DG, (k + 1) * DG))
    at = 4 * DG
    entries = [("w_in", D * 2 * EI)]
    entries += [(name, math.prod(shape)) for name, shape in SMALL]
    entries += [
        ("w_out", EI * D),
        ("w_gu1", D * 2 * FI),
        ("w_down1", FI * D),
        ("w_qkv", D * 3 * HW),
        ("w_o", HW * D),
        ("w_gu2", D * 2 * FI),
        ("w_down2", FI * D),
    ]
    for _, count in entries:
        bounds.append((at, at + count))
        at += count
    return bounds


def silu(v):
    return v * jax.nn.sigmoid(v)


def softplus(v):
    return jnp.maximum(v, 0.0) + jnp.log1p(jnp.exp(-jnp.abs(v)))


def mat_nn(a, b):
    return jnp.dot(a, b, preferred_element_type=F32)


def mat_tn(a, b):
    return lax.dot_general(a, b, (((0,), (0,)), ((), ())), preferred_element_type=F32)


def mat_nt(a, b):
    return lax.dot_general(a, b, (((1,), (1,)), ((), ())), preferred_element_type=F32)


def ring_pos(d, n):
    return jnp.where(lax.rem(d, 2) == 0, lax.div(d, 2), n - 1 - lax.div(d, 2))


def ring_dev(p, n):
    return jnp.where(p < n // 2, 2 * p, 2 * (n - 1 - p) + 1)


def ring_neighbours(n):
    d = lax.axis_index("dp")
    p = ring_pos(d, n)
    right = ring_dev(lax.rem(p + 1, n), n)
    left = ring_dev(lax.rem(p + n - 1, n), n)
    return d, p, right, left


def ring_barrier(left, right, t):
    barrier = pltpu.get_barrier_semaphore()
    for nb in (left, right):
        pl.semaphore_signal(barrier, inc=1, device_id=(nb, t), device_id_type=MESH)
    pl.semaphore_wait(barrier, 2)


def gather_kernel(n, subs, own_ref, out_ref, hold, local_sem, ssem, rsem):
    t = lax.axis_index("tensor")
    d, p, right, left = ring_neighbours(n)
    rows = own_ref.shape[0]
    half = rows // 2
    sub = half // subs
    fetch = pltpu.make_async_copy(own_ref, hold, local_sem.at[0])
    fetch.start()
    ring_barrier(left, right, t)

    def copy(way, step, c, from_own):
        target = right if way == 0 else left
        owner = ring_dev(lax.rem(p + (n - step if way == 0 else step), n), n)
        at = pl.multiple_of(owner * rows + way * half + c * sub, 8)
        src = own_ref.at[pl.ds(way * half + c * sub, sub)] if from_own else out_ref.at[pl.ds(at, sub)]
        return pltpu.make_async_remote_copy(
            src_ref=src,
            dst_ref=out_ref.at[pl.ds(at, sub)],
            send_sem=ssem.at[way, step, c],
            recv_sem=rsem.at[way, step, c],
            device_id=(target, t),
            device_id_type=MESH,
        )

    for c in range(subs):
        for way in (0, 1):
            copy(way, 0, c, True).start()
    fetch.wait()
    store = pltpu.make_async_copy(
        hold, out_ref.at[pl.ds(pl.multiple_of(d * rows, 8), rows)], local_sem.at[1]
    )
    store.start()
    for step in range(1, n - 1):
        for c in range(subs):
            for way in (0, 1):
                copy(way, step - 1, c, step == 1).wait_recv()
                copy(way, step, c, False).start()
    for c in range(subs):
        for way in (0, 1):
            copy(way, n - 2, c, n == 2).wait_recv()
    store.wait()
    for step in range(n - 1):
        for c in range(subs):
            for way in (0, 1):
                copy(way, step, c, step == 0).wait_send()


def ring_gather(own, n):
    rows, cols = own.shape
    subs = 2
    return pl.pallas_call(
        functools.partial(gather_kernel, n, subs),
        out_shape=jax.ShapeDtypeStruct((n * rows, cols), own.dtype),
        in_specs=[pl.BlockSpec(memory_space=pl.ANY)],
        out_specs=pl.BlockSpec(memory_space=pl.ANY),
        scratch_shapes=[
            pltpu.VMEM((rows, cols), own.dtype),
            pltpu.SemaphoreType.DMA((2,)),
            pltpu.SemaphoreType.DMA((2, n - 1, subs)),
            pltpu.SemaphoreType.DMA((2, n - 1, subs)),
        ],
        cost_estimate=pl.CostEstimate(flops=10**9, bytes_accessed=1500 * 10**6, transcendentals=0),
        compiler_params=pltpu.CompilerParams(
            collective_id=0, has_side_effects=True, vmem_limit_bytes=32 << 20
        ),
        name="ring_gather",
    )(own)


def piece_of(half):
    for size in (64, 32, 16):
        if half % size == 0:
            return size


def reduce_kernel(n, shard_lines, left_ref, right_refs, qkv_ref, out_ref, slots, lines, ssem, rsem, out_sem):
    t = lax.axis_index("tensor")
    d, p, right, left = ring_neighbours(n)
    rows = BIG_ROWS // n
    half = rows // 2
    SUB = piece_of(half)
    subs = half // SUB
    ring_barrier(left, right, t)
    qkv_at = BIG_OFF["w_qkv"]
    qkv_rows = dict(BIG)["w_qkv"]

    def own_into(at, put):
        in_qkv = jnp.logical_and(at >= qkv_at, at < qkv_at + qkv_rows)
        which = jnp.int32(0)
        for name, _ in BIG[1:]:
            if name != "w_qkv":
                which = which + jnp.where(at >= BIG_OFF[name], 1, 0)

        @pl.when(in_qkv)
        def _():
            put(qkv_ref[pl.ds(pl.multiple_of(at - qkv_at, SUB), SUB), :].astype(F32))

        @pl.when(jnp.logical_not(in_qkv))
        def _():
            row = jnp.where(at >= qkv_at + qkv_rows, at - qkv_rows, at)
            lt = left_ref[pl.ds(pl.multiple_of(row, SUB), SUB), :]
            put(jnp.dot(lt, right_refs[which], preferred_element_type=F32))

    def owner_of(way, step):
        return ring_dev(lax.rem(p + (n - 1 - step if way == 0 else 1 + step), n), n)

    def copy(way, step, c):
        target = right if way == 0 else left
        return pltpu.make_async_remote_copy(
            src_ref=slots.at[way, step, pl.ds(pl.multiple_of(c * SUB, SUB), SUB)],
            dst_ref=slots.at[way, step + 1, pl.ds(pl.multiple_of(c * SUB, SUB), SUB)],
            send_sem=ssem.at[way, step, c],
            recv_sem=rsem.at[way, step, c],
            device_id=(target, t),
            device_id_type=MESH,
        )

    def run(step):
        @pl.loop(0, subs)
        def _(c):
            here = pl.ds(pl.multiple_of(c * SUB, SUB), SUB)
            for way in (0, 1):
                at = owner_of(way, step) * rows + way * half + c * SUB
                if step > 0:
                    copy(way, step - 1, c).wait_recv()

                def put(value):
                    if step > 0:
                        value = value + slots[way, step, here, :].astype(F32)
                    if step < n - 1:
                        slots[way, step, here, :] = value.astype(BF)
                    else:
                        for j in range(LINES):
                            lines[way, pl.ds(j, SUB, stride=LINES), :] = value[:, j * LANES : (j + 1) * LANES]

                if step == n - 1:

                    @pl.when(c > 0)
                    def _():
                        leave(way, c - 1).wait()

                own_into(at, put)
                if step < n - 1:
                    copy(way, step, c).start()
                else:
                    leave(way, c).start()

    def leave(way, c):
        row = d * rows + way * half + c * SUB
        to = row * LINES + LEAD + jnp.where(row >= FIRST // LINES, SMALL_ROWS, 0) - d * shard_lines + SLACK
        return pltpu.make_async_copy(
            lines.at[way], out_ref.at[pl.ds(to, SUB * LINES), 0], out_sem.at[way]
        )

    for step in range(n):
        run(step)
    for way in (0, 1):
        leave(way, subs - 1).wait()

    @pl.loop(0, subs)
    def _(c):
        for way in (0, 1):
            for step in range(n - 1):
                copy(way, step, c).wait_send()


def ring_reduce(left_t, rights, qkv_grad, n, shard_lines):
    rows = BIG_ROWS // n
    sub = piece_of(rows // 2)
    subs = rows // 2 // sub
    vm = pl.BlockSpec(memory_space=pltpu.VMEM)
    return pl.pallas_call(
        functools.partial(reduce_kernel, n, shard_lines),
        out_shape=jax.ShapeDtypeStruct((shard_lines + 2 * SLACK, 1, LANES), F32),
        in_specs=[vm, vm, vm],
        out_specs=pl.BlockSpec(memory_space=pl.ANY),
        scratch_shapes=[
            pltpu.VMEM((2, n, rows // 2, D), BF),
            pltpu.VMEM((2, sub * LINES, LANES), F32),
            pltpu.SemaphoreType.DMA((2, n - 1, subs)),
            pltpu.SemaphoreType.DMA((2, n - 1, subs)),
            pltpu.SemaphoreType.DMA((2,)),
        ],
        cost_estimate=pl.CostEstimate(flops=10**9, bytes_accessed=1500 * 10**6, transcendentals=0),
        compiler_params=pltpu.CompilerParams(
            collective_id=1, has_side_effects=True, vmem_limit_bytes=67043328
        ),
        name="ring_reduce",
    )(left_t, rights, qkv_grad)


def pair_kernel(parts, x_ref, out_ref, from_mate, chip, from_far, s1, r1, s2, r2, s3, r3):
    d = lax.axis_index("dp")
    t = lax.axis_index("tensor")
    core = lax.rem(t, 2)
    mate = t + 1 - 2 * core
    far = lax.rem(t + 2, 4)
    half = x_ref.shape[0] // 2
    q = half // parts
    barrier = pltpu.get_barrier_semaphore()
    for peer in (mate, far):
        pl.semaphore_signal(barrier, inc=1, device_id=(d, peer), device_id_type=MESH)
    pl.semaphore_wait(barrier, 2)

    def mine(k):
        return pl.ds(pl.multiple_of(core * half + k * q, 16), q)

    def theirs(k):
        return pl.ds(pl.multiple_of((1 - core) * half + k * q, 16), q)

    def send(src, dst, ssem, rsem, k, peer):
        return pltpu.make_async_remote_copy(
            src_ref=src,
            dst_ref=dst,
            send_sem=ssem.at[k],
            recv_sem=rsem.at[k],
            device_id=(d, peer),
            device_id_type=MESH,
        )

    def one(k):
        here = pl.ds(k * q, q)
        return send(x_ref.at[theirs(k)], from_mate.at[here], s1, r1, k, mate)

    def two(k):
        here = pl.ds(k * q, q)
        return send(chip.at[here], from_far.at[here], s2, r2, k, far)

    def three(k):
        return send(out_ref.at[mine(k)], out_ref.at[mine(k)], s3, r3, k, mate)

    for k in range(parts):
        one(k).start()
    for k in range(parts):
        here = slice(k * q, (k + 1) * q)
        one(k).wait_recv()
        chip[here, :] = (x_ref[mine(k), :].astype(F32) + from_mate[here, :].astype(F32)).astype(BF)
        two(k).start()
    for k in range(parts):
        here = slice(k * q, (k + 1) * q)
        two(k).wait_recv()
        out_ref[mine(k), :] = (chip[here, :].astype(F32) + from_far[here, :].astype(F32)).astype(BF)
        three(k).start()
    for k in range(parts):
        three(k).wait_recv()
    for k in range(parts):
        one(k).wait_send()
        two(k).wait_send()
        three(k).wait_send()


def sum_tensor(value):
    rows, cols = value.shape
    parts = 4 if cols >= 1024 else 1
    vm = pl.BlockSpec(memory_space=pltpu.VMEM)
    dma = pltpu.SemaphoreType.DMA
    part = pltpu.VMEM((rows // 2, cols), BF)
    return pl.pallas_call(
        functools.partial(pair_kernel, parts),
        out_shape=jax.ShapeDtypeStruct((rows, cols), BF),
        in_specs=[vm],
        out_specs=vm,
        scratch_shapes=[part, part, part] + [dma((parts,))] * 6,
        compiler_params=pltpu.CompilerParams(
            collective_id=3 if cols >= 1024 else 4, has_side_effects=True
        ),
        name="sum_tensor",
    )(value)


def sum_proj(value):
    cols = value.shape[1]
    padded = jnp.pad(value, ((0, 0), (0, -cols % LANES)))
    return sum_tensor(padded)[:, :cols]


def spread_kernel(n, x_ref, out_ref, got, s1, r1, s2, r2):
    d = lax.axis_index("dp")
    t = lax.axis_index("tensor")
    q = x_ref.shape[0] // n
    barrier = pltpu.get_barrier_semaphore()

    def peer(k):
        return lax.rem(d + k, n)

    @pl.loop(1, n)
    def _(k):
        pl.semaphore_signal(barrier, inc=1, device_id=(peer(k), t), device_id_type=MESH)

    pl.semaphore_wait(barrier, n - 1)

    def rows(e):
        return pl.ds(pl.multiple_of(e * q, 16), q)

    def one(k):
        return pltpu.make_async_remote_copy(
            src_ref=x_ref.at[rows(peer(k))],
            dst_ref=got.at[k - 1],
            send_sem=s1.at[k - 1],
            recv_sem=r1.at[k - 1],
            device_id=(peer(k), t),
            device_id_type=MESH,
        )

    def two(k):
        return pltpu.make_async_remote_copy(
            src_ref=out_ref.at[rows(d)],
            dst_ref=out_ref.at[rows(d)],
            send_sem=s2.at[k - 1],
            recv_sem=r2.at[k - 1],
            device_id=(peer(k), t),
            device_id_type=MESH,
        )

    @pl.loop(1, n)
    def _(k):
        one(k).start()

    @pl.loop(1, n)
    def _(k):
        one(k).wait_recv()

    def add(k, acc):
        return acc + got[k - 1].astype(F32)

    out_ref[rows(d), :] = lax.fori_loop(1, n, add, x_ref[rows(d), :].astype(F32)).astype(BF)

    @pl.loop(1, n)
    def _(k):
        two(k).start()

    @pl.loop(1, n)
    def _(k):
        two(k).wait_recv()

    @pl.loop(1, n)
    def _(k):
        one(k).wait_send()
        two(k).wait_send()


def sum_dp(value, n):
    count = value.shape[0]
    padded = jnp.pad(value, ((0, -count % (16 * n)), (0, 0)))
    vm = pl.BlockSpec(memory_space=pltpu.VMEM)
    dma = pltpu.SemaphoreType.DMA((n - 1,))
    return pl.pallas_call(
        functools.partial(spread_kernel, n),
        out_shape=jax.ShapeDtypeStruct(padded.shape, BF),
        in_specs=[vm],
        out_specs=vm,
        scratch_shapes=[pltpu.VMEM((n - 1, padded.shape[0] // n, LANES), BF), dma, dma, dma, dma],
        compiler_params=pltpu.CompilerParams(collective_id=5, has_side_effects=True),
        name="sum_dp",
    )(padded)[:count]


def spread(ref, value):
    rows = value.shape[0]
    for j in range(EI // LANES):
        ref[pl.ds(j, rows, stride=EI // LANES), :] = value[:, j * LANES : (j + 1) * LANES]


def collect(ref, rows):
    return jnp.concatenate(
        [ref[pl.ds(j, rows, stride=EI // LANES), :] for j in range(EI // LANES)], axis=1
    )


SUBL = EI // LANES


def scan_kernel(slots, proj_ref, bc_ref, unit_ref, gate_ref, w_dt_ref, bias_ref, skip_ref, alog_ref,
                gated_ref, step_s, su_s, y_s, rate_s):
    pre = jnp.dot(proj_ref[:, :DTR], w_dt_ref[...], preferred_element_type=F32) + bias_ref[...]
    step = softplus(pre)
    unit = unit_ref[...].astype(F32)
    spread(step_s, step)
    spread(su_s, step * unit)
    rate_s[...] = -jnp.exp(alog_ref[...]) * LOG2E

    def body(t, states):
        new = []
        for m in range(slots):
            r = m * SLOT + t
            row = pl.ds(pl.multiple_of(r * SUBL, SUBL), SUBL)
            st = step_s[row, :]
            su = su_s[row, :]
            y = jnp.zeros((SUBL, LANES), F32)
            for k in range(NSTATE):
                dec = jnp.exp2(rate_s[k * SUBL : (k + 1) * SUBL, :] * st)
                s = dec * states[m * NSTATE + k] + bc_ref[r, k] * su
                y = y + bc_ref[r, NSTATE + k] * s
                new.append(s)
            y_s[row, :] = y
        return tuple(new)

    init = tuple(jnp.zeros((SUBL, LANES), F32) for _ in range(slots * NSTATE))
    lax.fori_loop(0, SLOT, body, init)
    y = collect(y_s, slots * SLOT) + skip_ref[...] * unit
    z = gate_ref[...]
    gated_ref[...] = (y * silu(z)).astype(BF)


def scan_forward(proj, bc, unit, gate, w_dt, dt_bias, d_skip, a_log):
    rows = unit.shape[0]
    vm = pl.BlockSpec(memory_space=pltpu.VMEM)
    sm = pl.BlockSpec(memory_space=pltpu.SMEM)
    return pl.pallas_call(
        functools.partial(scan_kernel, rows // SLOT),
        out_shape=jax.ShapeDtypeStruct((rows, EI), BF),
        in_specs=[vm, sm, vm, vm, vm, vm, vm, vm],
        out_specs=vm,
        scratch_shapes=[
            pltpu.VMEM((rows * SUBL, LANES), F32),
            pltpu.VMEM((rows * SUBL, LANES), F32),
            pltpu.VMEM((rows * SUBL, LANES), F32),
            pltpu.VMEM((NSTATE * SUBL, LANES), F32),
        ],
        compiler_params=pltpu.CompilerParams(vmem_limit_bytes=60 << 20),
        name="scan_forward",
    )(proj, bc, unit, gate, w_dt, dt_bias, d_skip, a_log)


def adjoint_kernel(slots, proj_ref, bc_ref, unit_ref, gate_ref, w_dt_ref, bias_ref, skip_ref, alog_ref,
                   grad_ref, gz_ref, gunit_ref, gproj_ref, gdt_ref, gbias_ref, gskip_ref, galog_ref,
                   step_s, su_s, unit_s, y_s, gy_s, gs_s, lb_s, rate_s, hist, lams):
    rows = slots * SLOT
    pre = jnp.dot(proj_ref[:, :DTR], w_dt_ref[...], preferred_element_type=F32) + bias_ref[...]
    step = softplus(pre)
    unit = unit_ref[...].astype(F32)
    spread(step_s, step)
    spread(unit_s, unit)
    spread(su_s, step * unit)
    z = gate_ref[...]
    sig = jax.nn.sigmoid(z)
    gg = grad_ref[...]
    gy = gg * z * sig
    spread(gy_s, gy)
    rate_s[...] = -jnp.exp(alog_ref[...])
    galog_ref[...] = jnp.zeros_like(galog_ref)
    zero = jnp.zeros((SUBL, LANES), F32)
    span = SLOT + 1

    def hist_at(k, t):
        return pl.ds(pl.multiple_of((k * span + t) * SUBL, SUBL), SUBL)

    def lam_at(k, t):
        return pl.ds(pl.multiple_of((k * SLOT + t) * SUBL, SUBL), SUBL)

    for m in range(slots):
        for k in range(NSTATE):
            hist[hist_at(k, 0), :] = zero

        def forward(t, states):
            r = m * SLOT + t
            row = pl.ds(pl.multiple_of(r * SUBL, SUBL), SUBL)
            st = step_s[row, :] * LOG2E
            su = su_s[row, :]
            y = zero
            new = []
            for k in range(NSTATE):
                dec = jnp.exp2(rate_s[k * SUBL : (k + 1) * SUBL, :] * st)
                s = dec * states[k] + bc_ref[r, k] * su
                y = y + bc_ref[r, NSTATE + k] * s
                hist[hist_at(k, t + 1), :] = s
                new.append(s)
            y_s[row, :] = y
            return tuple(new)

        lax.fori_loop(0, SLOT, forward, tuple(zero for _ in range(NSTATE)))

        def backward(i, carry):
            t = SLOT - 1 - i
            r = m * SLOT + t
            row = pl.ds(pl.multiple_of(r * SUBL, SUBL), SUBL)
            st = step_s[row, :]
            st2 = st * LOG2E
            gyt = gy_s[row, :]
            lb = zero
            gs = zero
            new = []
            for k in range(NSTATE):
                rate = rate_s[k * SUBL : (k + 1) * SUBL, :]
                dec = jnp.exp2(rate * st2)
                lam = bc_ref[r, NSTATE + k] * gyt + carry[k]
                ld = dec * lam
                new.append(ld)
                lams[lam_at(k, t), :] = lam
                lb = lb + bc_ref[r, k] * lam
                x = ld * hist[hist_at(k, t), :]
                gs = gs + rate * x
                at = slice(k * SUBL, (k + 1) * SUBL)
                galog_ref[at, :] = galog_ref[at, :] + st * x
            lb_s[row, :] = lb
            gs_s[row, :] = gs + unit_s[row, :] * lb
            return tuple(new)

        lax.fori_loop(0, SLOT, backward, tuple(zero for _ in range(NSTATE)))
        out = slice(m * SLOT, (m + 1) * SLOT)
        base = m * SLOT * SUBL

        lane = lax.broadcasted_iota(jnp.int32, (SLOT, LANES), 1)

        def reduce_state(k, acc):
            ab = jnp.zeros((SLOT, LANES), F32)
            ac = jnp.zeros((SLOT, LANES), F32)
            for j in range(SUBL):
                cols = slice(j * LANES, (j + 1) * LANES)
                lam = lams[pl.ds(k * SLOT * SUBL + j, SLOT, stride=SUBL), :]
                h = hist[pl.ds((k * span + 1) * SUBL + j, SLOT, stride=SUBL), :]
                sj = su_s[pl.ds(base + j, SLOT, stride=SUBL), :]
                gj = gy_s[pl.ds(base + j, SLOT, stride=SUBL), :]
                ab = ab + lam * sj
                ac = ac + h * gj
            sb = jnp.sum(ab, axis=1, keepdims=True)
            sc = jnp.sum(ac, axis=1, keepdims=True)
            return acc + jnp.where(lane == k, sb, 0.0) + jnp.where(lane == NSTATE + k, sc, 0.0)

        sums = lax.fori_loop(0, NSTATE, reduce_state, jnp.zeros((SLOT, LANES), F32))
        gproj_ref[out, DTR : DTR + LANES] = sums.astype(BF)
    galog_ref[...] = galog_ref[...] * rate_s[...]
    y = collect(y_s, rows) + skip_ref[...] * unit
    gz_ref[...] = (gg * y * sig * (1.0 + z * (1.0 - sig))).astype(BF)
    gunit_ref[...] = gy * skip_ref[...] + step * collect(lb_s, rows)
    gskip_ref[...] = jnp.sum(gy * unit, axis=0, keepdims=True)
    q = collect(gs_s, rows) * jax.nn.sigmoid(pre)
    gbias_ref[...] = jnp.sum(q, axis=0, keepdims=True)
    ql = q.astype(BF)
    gdt_ref[...] = mat_tn(proj_ref[:, :DTR], ql)
    gproj_ref[:, :DTR] = mat_nt(ql, w_dt_ref[...]).astype(BF)


def scan_backward(proj, bc, unit, gate, w_dt, dt_bias, d_skip, a_log, grad):
    rows = unit.shape[0]
    vm = pl.BlockSpec(memory_space=pltpu.VMEM)
    sm = pl.BlockSpec(memory_space=pltpu.SMEM)
    sds = jax.ShapeDtypeStruct
    flat = pltpu.VMEM((rows * SUBL, LANES), F32)
    return pl.pallas_call(
        functools.partial(adjoint_kernel, rows // SLOT),
        out_shape=(
            sds((rows, EI), BF),
            sds((rows, EI), F32),
            sds((rows, DTR + LANES), BF),
            sds((DTR, EI), F32),
            sds((1, EI), F32),
            sds((1, EI), F32),
            sds((NSTATE * SUBL, LANES), F32),
        ),
        in_specs=[vm, sm, vm, vm, vm, vm, vm, vm, vm],
        out_specs=(vm,) * 7,
        scratch_shapes=[flat] * 7
        + [
            pltpu.VMEM((NSTATE * SUBL, LANES), F32),
            pltpu.VMEM((NSTATE * (SLOT + 1) * SUBL, LANES), F32),
            pltpu.VMEM((NSTATE * SLOT * SUBL, LANES), F32),
        ],
        compiler_params=pltpu.CompilerParams(vmem_limit_bytes=60 << 20),
        name="scan_backward",
    )(proj, bc, unit, gate, w_dt, dt_bias, d_skip, a_log, grad)


def rope_tables(length, head_dim):
    half_dim = head_dim // 2
    freq_index = jnp.arange(half_dim, dtype=F32)
    inv_freq = jnp.exp(-math.log(ROPE_BASE) * 2.0 * freq_index / head_dim)
    angles = jnp.arange(length, dtype=F32)[:, None] * inv_freq[None, :]
    return (jnp.cos(angles)[None, :, None, :], jnp.sin(angles)[None, :, None, :])


def rope_apply(values, cosine, sine):
    half_dim = values.shape[-1] // 2
    a = values[..., :half_dim]
    b = values[..., half_dim:]
    return jnp.concatenate([a * cosine - b * sine, b * cosine + a * sine], axis=-1)


def rms_parts(v, g):
    s = lax.rsqrt(jnp.mean(v * v, axis=-1, keepdims=True) + EPS_NORM)
    return s, v * s


def rms_back(v, g, gh):
    s, nrm = rms_parts(v, g)
    gg = jnp.sum(gh * nrm, axis=0)
    gv = s * (gh * g - nrm * jnp.mean(gh * g * nrm, axis=-1, keepdims=True))
    return gv, gg


def total(partial_out):
    return sum_tensor(partial_out.astype(BF)).astype(F32)


def shift_down(v, by):
    if by == 0:
        return v
    return jnp.pad(v, ((0, 0), (by, 0), (0, 0)))[:, : v.shape[1]]


def shift_up(v, by):
    if by == 0:
        return v
    return jnp.pad(v, ((0, 0), (0, by), (0, 0)))[:, by:]


def attend(query, keys, values):
    scale = HEAD_DIM ** (-0.5)
    distance = jnp.arange(SLOT)[:, None] - jnp.arange(SLOT)[None, :]
    allowed = (distance >= 0) & (distance < WINDOW)
    scores = jnp.einsum("mqhd,mkhd->mhqk", query, keys, preferred_element_type=F32) * scale
    scores = jnp.where(allowed, scores, NEG_FILL)
    expo = jnp.exp(scores - jnp.max(scores, axis=-1, keepdims=True))
    return expo / jnp.sum(expo, axis=-1, keepdims=True)


def ffn_forward(h, w_gu, w_down):
    pre = mat_nn(h, w_gu)
    act = (silu(pre[:, :FI]) * pre[:, FI:]).astype(BF)
    return total(mat_nn(act, w_down)), pre, act


def ffn_backward(pre, w_gu, w_down, grad_low):
    gate = pre[:, :FI]
    up = pre[:, FI:]
    ga = mat_nt(grad_low, w_down)
    sig = jax.nn.sigmoid(gate)
    grad_gate = ga * up * sig * (1.0 + gate * (1.0 - sig))
    grad_up = ga * gate * sig
    gp = jnp.concatenate([grad_gate, grad_up], axis=1).astype(BF)
    return total(mat_nt(gp, w_gu)), gp


def layer(x, grad_out, w, small, gains, n):
    rows = x.shape[0]
    m = rows // SLOT
    hr = HW // HEAD_DIM
    cosine, sine = rope_tables(SLOT, HEAD_DIM)
    s1, n1 = rms_parts(x, gains[0])
    h1 = (n1 * gains[0]).astype(BF)
    mixed = mat_nn(h1, w["w_in"])
    mix_x = mixed[:, :EI].reshape(m, SLOT, EI)
    gate_z = mixed[:, EI:]
    conv_w = small["conv_w"].astype(F32)
    pre_conv = small["conv_b"].astype(F32)[None, None, :]
    for j in range(CONV):
        pre_conv = pre_conv + conv_w[j] * shift_down(mix_x, CONV - 1 - j)
    unit = silu(pre_conv).astype(BF).reshape(rows, EI)
    proj = sum_proj(mat_nn(unit, small["w_x"]).astype(BF))
    bc = proj[:, DTR:].astype(F32)
    scan_args = (
        proj[:, :DTR],
        bc,
        unit,
        gate_z,
        small["w_dt"],
        small["dt_bias"].astype(F32)[None],
        small["d_skip"].astype(F32)[None],
        small["a_log"].astype(F32).reshape(NSTATE * SUBL, LANES),
    )
    gated = scan_forward(*scan_args)
    x1 = x + total(mat_nn(gated, w["w_out"]))
    h2 = (rms_parts(x1, 0)[1] * gains[1]).astype(BF)
    branch, pre1, act1 = ffn_forward(h2, w["w_gu1"], w["w_down1"])
    x2 = x1 + branch
    h3 = (rms_parts(x2, 0)[1] * gains[2]).astype(BF)
    packed = mat_nn(h3, w["w_qkv"]).reshape(m, SLOT, 3, hr, HEAD_DIM)
    query = rope_apply(packed[:, :, 0], cosine, sine).astype(BF)
    keys = rope_apply(packed[:, :, 1], cosine, sine).astype(BF)
    values = packed[:, :, 2].astype(BF)
    probs = attend(query, keys, values)
    probs_low = probs.astype(BF)
    attended = jnp.einsum("mhqk,mkhd->mqhd", probs_low, values, preferred_element_type=F32)
    attended = attended.reshape(rows, HW).astype(BF)
    x3 = x2 + total(mat_nn(attended, w["w_o"]))
    h4 = (rms_parts(x3, 0)[1] * gains[3]).astype(BF)
    branch, pre2, act2 = ffn_forward(h4, w["w_gu2"], w["w_down2"])
    x4 = x3 + branch

    gb4 = grad_out.astype(BF)
    gh, gp2 = ffn_backward(pre2, w["w_gu2"], w["w_down2"], gb4)
    gv, gg4 = rms_back(x3, gains[3], gh)
    g3 = grad_out + gv
    gb3 = g3.astype(BF)
    gatt = mat_nt(gb3, w["w_o"]).astype(BF).reshape(m, SLOT, hr, HEAD_DIM)
    grad_p = jnp.einsum("mqhd,mkhd->mhqk", gatt, values, preferred_element_type=F32)
    inner = jnp.sum(probs * grad_p, axis=-1, keepdims=True)
    gs = (probs * (grad_p - inner)).astype(BF)
    scale = HEAD_DIM ** (-0.5)
    gq = jnp.einsum("mhqk,mkhd->mqhd", gs, keys, preferred_element_type=F32) * scale
    gk = jnp.einsum("mhqk,mqhd->mkhd", gs, query, preferred_element_type=F32) * scale
    gvv = jnp.einsum("mhqk,mqhd->mkhd", probs_low, gatt, preferred_element_type=F32)
    gpk = (
        jnp.stack([rope_apply(gq, cosine, -sine), rope_apply(gk, cosine, -sine), gvv], axis=2)
        .reshape(rows, 3 * HW)
        .astype(BF)
    )
    gv, gg3 = rms_back(x2, gains[2], total(mat_nt(gpk, w["w_qkv"])))
    g2 = g3 + gv
    gb2 = g2.astype(BF)
    gh, gp1 = ffn_backward(pre1, w["w_gu1"], w["w_down1"], gb2)
    gv, gg2 = rms_back(x1, gains[1], gh)
    g1 = g2 + gv
    gb1 = g1.astype(BF)
    ggated = mat_nt(gb1, w["w_out"])
    gz, gunit, gproj, g_dt, g_bias, g_skip, g_alog = scan_backward(*scan_args, ggated)
    gproj = sum_tensor(gproj)[:, : DTR + 2 * NSTATE]
    g_wx = mat_tn(unit, gproj)
    gu = gunit + mat_nt(gproj, small["w_x"])
    sig = jax.nn.sigmoid(pre_conv)
    gpre = gu.reshape(m, SLOT, EI) * sig * (1.0 + pre_conv * (1.0 - sig))
    g_conv_b = jnp.sum(gpre, axis=(0, 1))
    g_conv_w = jnp.stack(
        [jnp.sum(gpre * shift_down(mix_x, CONV - 1 - j), axis=(0, 1)) for j in range(CONV)]
    )
    gmx = sum(conv_w[j] * shift_up(gpre, CONV - 1 - j) for j in range(CONV))
    gmixed = jnp.concatenate([gmx.reshape(rows, EI).astype(BF), gz], axis=1)
    gv, gg1 = rms_back(x, gains[0], total(mat_nt(gmixed, w["w_in"])))
    g0 = g1 + gv

    left_t = jnp.concatenate([h1, gated, h2, act1, attended, h4, act2], axis=1).T
    rights = jnp.stack([gmixed, gb1, gp1, gb2, gb3, gp2, gb4])
    g_qkv = mat_tn(h3, gpk).astype(BF).reshape(-1, D)
    start = lax.axis_index("tensor") * DG
    g_gain = lax.dynamic_slice_in_dim(jnp.stack([gg1, gg2, gg3, gg4]), start, DG, 1)
    pieces = [g_gain, g_conv_w, g_conv_b, g_bias, g_skip, g_alog, g_wx, g_dt]
    small_grads = jnp.concatenate([p.reshape(-1, LANES).astype(BF) for p in pieces])
    small_sum = sum_dp(small_grads, n)
    g0, small_sum, left_t = lax.optimization_barrier((g0, small_sum, left_t))
    return x4.astype(BF), g0, (left_t, rights, g_qkv), small_sum


def extents(n, shard_rows):
    slab = BIG_ROWS * LINES // n
    before = 0
    after = 0
    back_before = 0
    back_after = 0
    for d in range(n):
        lo, hi = slab * d, slab * (d + 1) - 1
        qs = [p + LEAD + (SMALL_ROWS if p >= FIRST else 0) - shard_rows * d for p in (lo, hi)]
        before = max(before, -qs[0])
        after = max(after, qs[1] + 1 - shard_rows)
    return before, after


def shift_perm(n, by):
    return [(i, i + by) for i in range(n) if 0 <= i + by < n]


def stack_kernel(n, shard_lines, before, per, top_ref, own_ref, bottom_ref, out_ref, hold, sem):
    d = lax.axis_index("dp")
    i = pl.program_id(0)
    steps = BIG_ROWS // n // per
    size = per * LINES

    def fetch(k, slot):
        row = d * (BIG_ROWS // n) + k * per
        a = row * LINES + LEAD + jnp.where(row >= FIRST // LINES, SMALL_ROWS, 0) - d * shard_lines
        high = a < 0
        low = a + size > shard_lines

        @pl.when(high)
        def _():
            pltpu.make_async_copy(top_ref.at[pl.ds(a + before, size), 0], hold.at[slot], sem.at[slot]).start()

        @pl.when(low)
        def _():
            pltpu.make_async_copy(
                bottom_ref.at[pl.ds(a + size - shard_lines, size), 0], hold.at[slot], sem.at[slot]
            ).start()

        @pl.when(jnp.logical_not(jnp.logical_or(high, low)))
        def _():
            pltpu.make_async_copy(own_ref.at[pl.ds(a, size), 0], hold.at[slot], sem.at[slot]).start()

    @pl.when(i == 0)
    def _():
        for k in range(min(3, steps)):
            fetch(k, k)

    @pl.when(i + 3 < steps)
    def _():
        fetch(i + 3, lax.rem(i + 3, 4))

    slot = lax.rem(i, 4)
    pltpu.make_async_copy(own_ref.at[pl.ds(0, size), 0], hold.at[slot], sem.at[slot]).wait()
    for j in range(LINES):
        out_ref[:, j * LANES : (j + 1) * LANES] = hold[slot, pl.ds(j, per, stride=LINES), :].astype(BF)


def stack_own(lines3, n):
    shard_lines = lines3.shape[0]
    before, after = extents(n, shard_lines)
    rows = BIG_ROWS // n
    per = 64 if rows % 64 == 0 else 32
    size = per * LINES
    nxt = lax.ppermute(lines3[:after], "dp", shift_perm(n, -1))
    prv = lax.ppermute(lines3[shard_lines - before :], "dp", shift_perm(n, 1))
    top = jnp.concatenate([prv, lines3[:size]])
    bottom = jnp.concatenate([lines3[shard_lines - size :], nxt])
    hbm = pl.BlockSpec(memory_space=pl.ANY)
    return pl.pallas_call(
        functools.partial(stack_kernel, n, shard_lines, before, per),
        grid=(rows // per,),
        out_shape=jax.ShapeDtypeStruct((rows, D), BF),
        in_specs=[hbm] * 3,
        out_specs=pl.BlockSpec((per, D), lambda i: (i, 0)),
        scratch_shapes=[pltpu.VMEM((4, size, LANES), F32), pltpu.SemaphoreType.DMA((4,))],
        compiler_params=pltpu.CompilerParams(vmem_limit_bytes=24 << 20),
        name="stack_own",
    )(top, lines3, bottom)


def window(values, shift, size):
    length = values.shape[0]
    s = jnp.clip(shift, 0, length - size)
    got = lax.dynamic_slice_in_dim(values, s, size, 0)
    room = jnp.zeros((3 * size,) + values.shape[1:], values.dtype)
    room = lax.dynamic_update_slice_in_dim(room, got, size + jnp.clip(s - shift, -size, size), 0)
    return room[size : 2 * size]


STRIP = 8192


def lone_group(groups, bounds_ref, start, stop):
    def look(g, found):
        holds = jnp.logical_and(bounds_ref[2 * g] <= start, bounds_ref[2 * g + 1] >= stop)
        return jnp.where(holds, g, found)

    return lax.fori_loop(0, groups, look, jnp.int32(-1))


def moments_kernel(groups, shard, bounds_ref, grad_ref, w_ref, one_ref, two_ref,
                   first_ref, second_ref, grad_out, sums_ref, hold):
    i = pl.program_id(0)
    size = CHUNK * LANES
    lanes = STRIP // 8

    @pl.when(i == 0)
    def _():
        @pl.loop(0, 2 * groups)
        def _(g):
            sums_ref[g] = 0.0

    def strip(k, carry):
        here = pl.ds(pl.multiple_of(k * STRIP, STRIP), STRIP)
        grad = grad_ref[:, here]
        w = w_ref[:, here]
        first = BETA_ONE * one_ref[:, here] + (1.0 - BETA_ONE) * grad
        second = BETA_TWO * two_ref[:, here] + (1.0 - BETA_TWO) * grad * grad
        ratio = first / (jnp.sqrt(second) + ADAM_EPS) + DECAY_W * w
        first_ref[:, here] = first
        second_ref[:, here] = second
        grad_out[:, here] = grad
        hold[:, here] = ratio
        wsq, rsq = carry
        for j in range(8):
            part = slice(j * lanes, (j + 1) * lanes)
            wsq = wsq + w[:, part] * w[:, part]
            rsq = rsq + ratio[:, part] * ratio[:, part]
        return wsq, rsq

    zero = jnp.zeros((1, lanes), F32)
    wsq, rsq = lax.fori_loop(0, size // STRIP, strip, (zero, zero))
    d = lax.axis_index("dp")
    start = d * shard + i * size
    limit = (d + 1) * shard
    alone = lone_group(groups, bounds_ref, start, start + size)
    alone = jnp.where(start + size <= limit, alone, -1)

    @pl.when(alone >= 0)
    def _():
        sums_ref[2 * alone] = sums_ref[2 * alone] + jnp.sum(wsq)
        sums_ref[2 * alone + 1] = sums_ref[2 * alone + 1] + jnp.sum(rsq)

    @pl.when(alone < 0)
    def _():
        @pl.loop(0, groups)
        def _(g):
            low = jnp.maximum(bounds_ref[2 * g], start)
            high = jnp.minimum(bounds_ref[2 * g + 1], jnp.minimum(start + size, limit))

            @pl.when(low < high)
            def _():
                def masked(k, carry):
                    at = pl.multiple_of(k * lanes, lanes)
                    here = pl.ds(at, lanes)
                    index = start + at + lax.broadcasted_iota(jnp.int32, (1, lanes), 1)
                    inside = (index >= low) & (index < high)
                    wv = w_ref[:, here]
                    rv = hold[:, here]
                    return (
                        carry[0] + jnp.where(inside, wv * wv, 0.0),
                        carry[1] + jnp.where(inside, rv * rv, 0.0),
                    )

                k0 = (low - start) // lanes
                k1 = (high - start + lanes - 1) // lanes
                wv, rv = lax.fori_loop(k0, k1, masked, (zero, zero))
                sums_ref[2 * g] = sums_ref[2 * g] + jnp.sum(wv)
                sums_ref[2 * g + 1] = sums_ref[2 * g + 1] + jnp.sum(rv)


def moments(bounds, lines, master, one, two):
    shard = master.shape[1]
    size = CHUNK * LANES
    groups = bounds.shape[0] // 2
    block = pl.BlockSpec((1, size), lambda i: (0, i))
    ahead = SLACK // CHUNK
    flat = jax.ShapeDtypeStruct((1, shard), F32)
    smem = pl.BlockSpec(memory_space=pltpu.SMEM)
    return pl.pallas_call(
        functools.partial(moments_kernel, groups, shard),
        grid=(pl.cdiv(shard, size),),
        out_shape=(flat, flat, flat, jax.ShapeDtypeStruct((2 * groups,), F32)),
        in_specs=[smem, pl.BlockSpec((1, size), lambda i: (0, i + ahead)), block, block, block],
        out_specs=(block, block, block, smem),
        scratch_shapes=[pltpu.VMEM((1, size), F32)],
        compiler_params=pltpu.CompilerParams(vmem_limit_bytes=40 << 20),
        name="moments",
    )(bounds, lines.reshape(1, -1), master, one, two)


def update_kernel(groups, shard, bounds_ref, trust_ref, w_ref, first_ref, second_ref, new_ref, low_ref, hold):
    i = pl.program_id(0)
    size = CHUNK * LANES
    lanes = STRIP // 8
    start = lax.axis_index("dp") * shard + i * size
    alone = lone_group(groups, bounds_ref, start, start + size)

    def step(trust_of):
        @pl.loop(0, size // STRIP)
        def _(k):
            here = pl.ds(pl.multiple_of(k * STRIP, STRIP), STRIP)
            w = w_ref[:, here]
            ratio = first_ref[:, here] / (jnp.sqrt(second_ref[:, here]) + ADAM_EPS) + DECAY_W * w
            new = w - LEARN_RATE * trust_of(here) * ratio
            new_ref[:, here] = new
            low_ref[:, here] = new.astype(BF)

    @pl.when(alone >= 0)
    def _():
        trust = trust_ref[jnp.maximum(alone, 0)]
        step(lambda here: trust)

    @pl.when(alone < 0)
    def _():
        hold[...] = jnp.zeros_like(hold)

        @pl.loop(0, groups)
        def _(g):
            low = jnp.maximum(bounds_ref[2 * g], start)
            high = jnp.minimum(bounds_ref[2 * g + 1], start + size)

            @pl.when(low < high)
            def _():
                @pl.loop((low - start) // lanes, (high - start + lanes - 1) // lanes)
                def _(k):
                    at = pl.multiple_of(k * lanes, lanes)
                    here = pl.ds(at, lanes)
                    index = start + at + lax.broadcasted_iota(jnp.int32, (1, lanes), 1)
                    hold[:, here] = jnp.where((index >= low) & (index < high), trust_ref[g], hold[:, here])

        step(lambda here: hold[:, here])


def update(bounds, trust, master, first, second):
    shard = master.shape[1]
    size = CHUNK * LANES
    groups = bounds.shape[0] // 2
    block = pl.BlockSpec((1, size), lambda i: (0, i))
    smem = pl.BlockSpec(memory_space=pltpu.SMEM)
    return pl.pallas_call(
        functools.partial(update_kernel, groups, shard),
        grid=(pl.cdiv(shard, size),),
        out_shape=(jax.ShapeDtypeStruct((1, shard), F32), jax.ShapeDtypeStruct((1, shard), BF)),
        in_specs=[smem, smem, block, block, block],
        out_specs=(block, block),
        scratch_shapes=[pltpu.VMEM((1, size), F32)],
        compiler_params=pltpu.CompilerParams(vmem_limit_bytes=40 << 20),
        name="update",
    )(bounds, trust, master, first, second)


def norms_kernel(n, m, own_ref, out_ref, across, along, part, ssem, rsem, ssem2, rsem2):
    d = lax.axis_index("dp")
    t = lax.axis_index("tensor")
    barrier = pltpu.get_barrier_semaphore()
    for k in range(1, m):
        pl.semaphore_signal(barrier, inc=1, device_id=(d, lax.rem(t + k, m)), device_id_type=MESH)

    @pl.loop(1, n)
    def _(k):
        pl.semaphore_signal(barrier, inc=1, device_id=(lax.rem(d + k, n), t), device_id_type=MESH)

    pl.semaphore_wait(barrier, n + m - 2)

    def over_tensor(k):
        return pltpu.make_async_remote_copy(
            src_ref=own_ref,
            dst_ref=across.at[k - 1],
            send_sem=ssem.at[k - 1],
            recv_sem=rsem.at[k - 1],
            device_id=(d, lax.rem(t + k, m)),
            device_id_type=MESH,
        )

    def over_dp(k):
        return pltpu.make_async_remote_copy(
            src_ref=part,
            dst_ref=along.at[k - 1],
            send_sem=ssem2.at[k - 1],
            recv_sem=rsem2.at[k - 1],
            device_id=(lax.rem(d + k, n), t),
            device_id_type=MESH,
        )

    for k in range(1, m):
        over_tensor(k).start()
    total_ = own_ref[...]
    for k in range(1, m):
        over_tensor(k).wait_recv()
    for k in range(1, m):
        total_ = total_ + across[k - 1]
    part[...] = total_

    @pl.loop(1, n)
    def _(k):
        over_dp(k).start()

    @pl.loop(1, n)
    def _(k):
        over_dp(k).wait_recv()

    def add(k, acc):
        return acc + along[k - 1]

    out_ref[...] = lax.fori_loop(1, n, add, part[...])
    for k in range(1, m):
        over_tensor(k).wait_send()

    @pl.loop(1, n)
    def _(k):
        over_dp(k).wait_send()


def sum_everywhere(values, n, m):
    vm = pl.BlockSpec(memory_space=pltpu.VMEM)
    dma = pltpu.SemaphoreType.DMA
    tile = pltpu.VMEM((8, LANES), F32)
    return pl.pallas_call(
        functools.partial(norms_kernel, n, m),
        out_shape=jax.ShapeDtypeStruct((8, LANES), F32),
        in_specs=[vm],
        out_specs=vm,
        scratch_shapes=[
            pltpu.VMEM((m - 1, 8, LANES), F32),
            pltpu.VMEM((n - 1, 8, LANES), F32),
            tile,
            dma((m - 1,)),
            dma((m - 1,)),
            dma((n - 1,)),
            dma((n - 1,)),
        ],
        compiler_params=pltpu.CompilerParams(collective_id=2, has_side_effects=True),
        name="sum_everywhere",
    )(values)


def per_device(n, m, tokens, cotangent, lengths, master, moment_one, moment_two):
    d = lax.axis_index("dp")
    shard = master.shape[1]
    lines = shard // LANES
    lines3 = master.reshape(lines, 1, LANES)
    base = d * lines
    mid = LEAD + FIRST
    small_own = jnp.concatenate(
        [window(lines3, -base, GAIN_ROWS), window(lines3, mid - base, SMALL_ROWS)]
    )
    small_own = lax.optimization_barrier(small_own)
    small_flat = sum_dp(small_own.reshape(-1, LANES).astype(BF), n)
    gains = lax.all_gather(small_flat[:GAIN_ROWS].reshape(4, DG), "tensor", axis=1, tiled=True)
    gains = gains.astype(F32)
    small = {}
    at = GAIN_ROWS
    for name, shape in SMALL:
        count = math.prod(shape) // LANES
        small[name] = small_flat[at : at + count].reshape(shape)
        at += count
    weights = ring_gather(stack_own(lines3, n), n)
    w = {}
    for name, rows in BIG:
        w[name] = weights[BIG_OFF[name] : BIG_OFF[name] + rows]
    w["w_qkv"] = w["w_qkv"].reshape(D, 3 * HW)
    x = tokens.astype(F32)
    pos = lax.broadcasted_iota(jnp.int32, (tokens.shape[0] // SLOT, SLOT), 1)
    valid = (pos < lengths[:, None]).astype(F32).reshape(-1, 1)
    grad = cotangent.astype(F32) * valid
    out, grad_in, operands, small_grads = layer(x, grad, w, small, gains, n)
    small_sum = small_grads.astype(F32).reshape(-1, 1, LANES)
    laid = ring_reduce(*operands, n, lines)

    before, after = extents(n, lines)
    slab_lines = BIG_ROWS * LINES // n

    def local(row):
        return row * LINES + LEAD + jnp.where(row >= FIRST // LINES, SMALL_ROWS, 0) - base

    begin = local(d * (BIG_ROWS // n))
    close = local((d + 1) * (BIG_ROWS // n) - 1) + LINES
    tail, head, laid = lax.optimization_barrier(
        (laid[SLACK + lines : SLACK + lines + after], laid[SLACK - before : SLACK], laid)
    )
    from_prev = lax.ppermute(tail, "dp", shift_perm(n, 1))
    from_next = lax.ppermute(head, "dp", shift_perm(n, -1))
    line = lax.broadcasted_iota(jnp.int32, (after, 1, 1), 0)
    top = jnp.where(line < begin, from_prev, laid[SLACK : SLACK + after])
    line = lax.broadcasted_iota(jnp.int32, (before, 1, 1), 0) + (lines - before)
    bottom = jnp.where(line >= close, from_next, laid[SLACK + lines - before : SLACK + lines])
    laid = laid.at[SLACK : SLACK + after].set(top)
    laid = laid.at[SLACK + lines - before : SLACK + lines].set(bottom)

    def place(laid, values, at):
        count = values.shape[0]
        return lax.dynamic_update_slice_in_dim(laid, values, SLACK + jnp.clip(at - base, -count, lines), 0)

    laid = place(laid, small_sum[GAIN_ROWS:], mid)
    laid = place(laid, small_sum[:GAIN_ROWS], 0)
    used = LEAD + SMALL_ROWS + BIG_ROWS * LINES
    rest = lines * n - used
    if rest:
        laid = place(laid, jnp.zeros((rest, 1, LANES), F32), used)

    bounds = jnp.asarray([v for pair in group_bounds() for v in pair], jnp.int32)
    first, second, grad_shard, sums = moments(bounds, laid, master, moment_one, moment_two)
    count = sums.shape[0]
    tile = jnp.pad(sums, (0, 8 * LANES - count)).reshape(8, LANES)
    squares = sum_everywhere(tile, n, m).reshape(-1)[:count].reshape(-1, 2)
    trust = jnp.sqrt(squares[:, 0] + TRUST_EPSILON) * lax.rsqrt(squares[:, 1] + TRUST_EPSILON)
    master_new, low = update(bounds, trust, master, first, second)
    return (out, grad_in, master_new, first, second, low, grad_shard, jnp.sqrt(squares))


def solution(mesh):
    row = P("dp", None)
    flat = P("tensor", "dp")
    return jax.shard_map(
        functools.partial(per_device, mesh.shape["dp"], mesh.shape["tensor"]),
        mesh=mesh,
        in_specs=(row, row, P("dp"), flat, flat, flat),
        out_specs=(row, row, flat, flat, flat, flat, flat, P()),
        check_vma=False,
    )
```

```python
import functools
import math

import jax
import jax.numpy as jnp
from jax import lax
from jax.experimental import pallas as pl
from jax.experimental.pallas import tpu as pltpu
from jax.sharding import PartitionSpec as P

D = 2048
INNER = 4096
NSTATE = 16
DTR = 128
HEADS = 32
HEAD_DIM = 64
FF = 4096
CONV = 4
WINDOW = 2048
SLOT = 128
LANES = 128

EPS_NORM = 1e-05
TRUST_EPSILON = 1e-06
ROPE_BASE = 10000.0
BETA_ONE = 0.5
BETA_TWO = 0.55
ADAM_EPS = 1e-06
DECAY_W = 0.01
LEARN_RATE = 0.2
NEG_FILL = -1e30
LOG2E = 1.4426950408889634
MESH = pl.DeviceIdType.MESH
BF = jnp.bfloat16
F32 = jnp.float32

EI = INNER // 4
FI = FF // 4
HW = HEADS * HEAD_DIM // 4
DG = D // 4

SMALL = [
    ("conv_w", (CONV, EI)),
    ("conv_b", (EI,)),
    ("dt_bias", (EI,)),
    ("d_skip", (EI,)),
    ("a_log", (NSTATE, EI)),
    ("w_x", (EI, DTR + 2 * NSTATE)),
    ("w_dt", (DTR, EI)),
]
SMALL_ROWS = sum(math.prod(s) for _, s in SMALL) // LANES
GAIN_ROWS = 4 * DG // LANES
BIG = [
    ("w_in", D),
    ("w_out", EI),
    ("w_gu1", D),
    ("w_down1", FI),
    ("w_qkv", D * 3 * HW // D),
    ("w_o", HW),
    ("w_gu2", D),
    ("w_down2", FI),
]
BIG_OFF = {}
_at = 0
for _name, _rows in BIG:
    BIG_OFF[_name] = _at
    _at += _rows
BIG_ROWS = _at
LINES = D // LANES
FIRST = BIG_OFF["w_out"] * LINES
LEAD = GAIN_ROWS
CHUNK = 1024
SLACK = -(-(SMALL_ROWS + GAIN_ROWS) // CHUNK) * CHUNK


def group_bounds():
    bounds = []
    for k in range(4):
        bounds.append((k * DG, (k + 1) * DG))
    at = 4 * DG
    entries = [("w_in", D * 2 * EI)]
    entries += [(name, math.prod(shape)) for name, shape in SMALL]
    entries += [
        ("w_out", EI * D),
        ("w_gu1", D * 2 * FI),
        ("w_down1", FI * D),
        ("w_qkv", D * 3 * HW),
        ("w_o", HW * D),
        ("w_gu2", D * 2 * FI),
        ("w_down2", FI * D),
    ]
    for _, count in entries:
        bounds.append((at, at + count))
        at += count
    return bounds


def silu(v):
    return v * jax.nn.sigmoid(v)


def softplus(v):
    return jnp.maximum(v, 0.0) + jnp.log1p(jnp.exp(-jnp.abs(v)))


def mat_nn(a, b):
    return jnp.dot(a, b, preferred_element_type=F32)


def mat_tn(a, b):
    return lax.dot_general(a, b, (((0,), (0,)), ((), ())), preferred_element_type=F32)


def mat_nt(a, b):
    return lax.dot_general(a, b, (((1,), (1,)), ((), ())), preferred_element_type=F32)


def ring_pos(d, n):
    return jnp.where(lax.rem(d, 2) == 0, lax.div(d, 2), n - 1 - lax.div(d, 2))


def ring_dev(p, n):
    return jnp.where(p < n // 2, 2 * p, 2 * (n - 1 - p) + 1)


def ring_neighbours(n):
    d = lax.axis_index("dp")
    p = ring_pos(d, n)
    right = ring_dev(lax.rem(p + 1, n), n)
    left = ring_dev(lax.rem(p + n - 1, n), n)
    return d, p, right, left


def ring_barrier(left, right, t):
    barrier = pltpu.get_barrier_semaphore()
    for nb in (left, right):
        pl.semaphore_signal(barrier, inc=1, device_id=(nb, t), device_id_type=MESH)
    pl.semaphore_wait(barrier, 2)


def gather_kernel(n, subs, own_ref, out_ref, hold, local_sem, ssem, rsem):
    t = lax.axis_index("tensor")
    d, p, right, left = ring_neighbours(n)
    rows = own_ref.shape[0]
    half = rows // 2
    sub = half // subs
    fetch = pltpu.make_async_copy(own_ref, hold, local_sem.at[0])
    fetch.start()
    ring_barrier(left, right, t)

    def copy(way, step, c, from_own):
        target = right if way == 0 else left
        owner = ring_dev(lax.rem(p + (n - step if way == 0 else step), n), n)
        at = pl.multiple_of(owner * rows + way * half + c * sub, 8)
        src = own_ref.at[pl.ds(way * half + c * sub, sub)] if from_own else out_ref.at[pl.ds(at, sub)]
        return pltpu.make_async_remote_copy(
            src_ref=src,
            dst_ref=out_ref.at[pl.ds(at, sub)],
            send_sem=ssem.at[way, step, c],
            recv_sem=rsem.at[way, step, c],
            device_id=(target, t),
            device_id_type=MESH,
        )

    for c in range(subs):
        for way in (0, 1):
            copy(way, 0, c, True).start()
    fetch.wait()
    store = pltpu.make_async_copy(
        hold, out_ref.at[pl.ds(pl.multiple_of(d * rows, 8), rows)], local_sem.at[1]
    )
    store.start()
    for step in range(1, n - 1):
        for c in range(subs):
            for way in (0, 1):
                copy(way, step - 1, c, step == 1).wait_recv()
                copy(way, step, c, False).start()
    for c in range(subs):
        for way in (0, 1):
            copy(way, n - 2, c, n == 2).wait_recv()
    store.wait()
    for step in range(n - 1):
        for c in range(subs):
            for way in (0, 1):
                copy(way, step, c, step == 0).wait_send()


def ring_gather(own, n):
    rows, cols = own.shape
    subs = 2
    return pl.pallas_call(
        functools.partial(gather_kernel, n, subs),
        out_shape=jax.ShapeDtypeStruct((n * rows, cols), own.dtype),
        in_specs=[pl.BlockSpec(memory_space=pl.ANY)],
        out_specs=pl.BlockSpec(memory_space=pl.ANY),
        scratch_shapes=[
            pltpu.VMEM((rows, cols), own.dtype),
            pltpu.SemaphoreType.DMA((2,)),
            pltpu.SemaphoreType.DMA((2, n - 1, subs)),
            pltpu.SemaphoreType.DMA((2, n - 1, subs)),
        ],
        cost_estimate=pl.CostEstimate(flops=10**9, bytes_accessed=1500 * 10**6, transcendentals=0),
        compiler_params=pltpu.CompilerParams(
            collective_id=0, has_side_effects=True, vmem_limit_bytes=32 << 20
        ),
        name="ring_gather",
    )(own)


def piece_of(half):
    for size in (64, 32, 16):
        if half % size == 0:
            return size


def reduce_kernel(n, shard_lines, left_ref, right_refs, qkv_ref, out_ref, slots, lines, ssem, rsem, out_sem):
    t = lax.axis_index("tensor")
    d, p, right, left = ring_neighbours(n)
    rows = BIG_ROWS // n
    half = rows // 2
    SUB = piece_of(half)
    subs = half // SUB
    ring_barrier(left, right, t)
    qkv_at = BIG_OFF["w_qkv"]
    qkv_rows = dict(BIG)["w_qkv"]

    def own_into(at, put):
        in_qkv = jnp.logical_and(at >= qkv_at, at < qkv_at + qkv_rows)
        which = jnp.int32(0)
        for name, _ in BIG[1:]:
            if name != "w_qkv":
                which = which + jnp.where(at >= BIG_OFF[name], 1, 0)

        @pl.when(in_qkv)
        def _():
            put(qkv_ref[pl.ds(pl.multiple_of(at - qkv_at, SUB), SUB), :].astype(F32))

        @pl.when(jnp.logical_not(in_qkv))
        def _():
            row = jnp.where(at >= qkv_at + qkv_rows, at - qkv_rows, at)
            lt = left_ref[pl.ds(pl.multiple_of(row, SUB), SUB), :]
            put(jnp.dot(lt, right_refs[which], preferred_element_type=F32))

    def owner_of(way, step):
        return ring_dev(lax.rem(p + (n - 1 - step if way == 0 else 1 + step), n), n)

    def copy(way, step, c):
        target = right if way == 0 else left
        return pltpu.make_async_remote_copy(
            src_ref=slots.at[way, step, pl.ds(pl.multiple_of(c * SUB, SUB), SUB)],
            dst_ref=slots.at[way, step + 1, pl.ds(pl.multiple_of(c * SUB, SUB), SUB)],
            send_sem=ssem.at[way, step, c],
            recv_sem=rsem.at[way, step, c],
            device_id=(target, t),
            device_id_type=MESH,
        )

    def run(step):
        @pl.loop(0, subs)
        def _(c):
            here = pl.ds(pl.multiple_of(c * SUB, SUB), SUB)
            for way in (0, 1):
                at = owner_of(way, step) * rows + way * half + c * SUB
                if step > 0:
                    copy(way, step - 1, c).wait_recv()

                def put(value):
                    if step > 0:
                        value = value + slots[way, step, here, :].astype(F32)
                    if step < n - 1:
                        slots[way, step, here, :] = value.astype(BF)
                    else:
                        for j in range(LINES):
                            lines[way, pl.ds(j, SUB, stride=LINES), :] = value[:, j * LANES : (j + 1) * LANES]

                if step == n - 1:

                    @pl.when(c > 0)
                    def _():
                        leave(way, c - 1).wait()

                own_into(at, put)
                if step < n - 1:
                    copy(way, step, c).start()
                else:
                    leave(way, c).start()

    def leave(way, c):
        row = d * rows + way * half + c * SUB
        to = row * LINES + LEAD + jnp.where(row >= FIRST // LINES, SMALL_ROWS, 0) - d * shard_lines + SLACK
        return pltpu.make_async_copy(
            lines.at[way], out_ref.at[pl.ds(to, SUB * LINES), 0], out_sem.at[way]
        )

    for step in range(n):
        run(step)
    for way in (0, 1):
        leave(way, subs - 1).wait()

    @pl.loop(0, subs)
    def _(c):
        for way in (0, 1):
            for step in range(n - 1):
                copy(way, step, c).wait_send()


def ring_reduce(left_t, rights, qkv_grad, n, shard_lines):
    rows = BIG_ROWS // n
    sub = piece_of(rows // 2)
    subs = rows // 2 // sub
    vm = pl.BlockSpec(memory_space=pltpu.VMEM)
    return pl.pallas_call(
        functools.partial(reduce_kernel, n, shard_lines),
        out_shape=jax.ShapeDtypeStruct((shard_lines + 2 * SLACK, 1, LANES), F32),
        in_specs=[vm, vm, vm],
        out_specs=pl.BlockSpec(memory_space=pl.ANY),
        scratch_shapes=[
            pltpu.VMEM((2, n, rows // 2, D), BF),
            pltpu.VMEM((2, sub * LINES, LANES), F32),
            pltpu.SemaphoreType.DMA((2, n - 1, subs)),
            pltpu.SemaphoreType.DMA((2, n - 1, subs)),
            pltpu.SemaphoreType.DMA((2,)),
        ],
        cost_estimate=pl.CostEstimate(flops=10**9, bytes_accessed=1500 * 10**6, transcendentals=0),
        compiler_params=pltpu.CompilerParams(
            collective_id=1, has_side_effects=True, vmem_limit_bytes=67043328
        ),
        name="ring_reduce",
    )(left_t, rights, qkv_grad)


def pair_kernel(parts, x_ref, out_ref, from_mate, chip, from_far, s1, r1, s2, r2, s3, r3):
    d = lax.axis_index("dp")
    t = lax.axis_index("tensor")
    core = lax.rem(t, 2)
    mate = t + 1 - 2 * core
    far = lax.rem(t + 2, 4)
    half = x_ref.shape[0] // 2
    q = half // parts
    barrier = pltpu.get_barrier_semaphore()
    for peer in (mate, far):
        pl.semaphore_signal(barrier, inc=1, device_id=(d, peer), device_id_type=MESH)
    pl.semaphore_wait(barrier, 2)

    def mine(k):
        return pl.ds(pl.multiple_of(core * half + k * q, 16), q)

    def theirs(k):
        return pl.ds(pl.multiple_of((1 - core) * half + k * q, 16), q)

    def send(src, dst, ssem, rsem, k, peer):
        return pltpu.make_async_remote_copy(
            src_ref=src,
            dst_ref=dst,
            send_sem=ssem.at[k],
            recv_sem=rsem.at[k],
            device_id=(d, peer),
            device_id_type=MESH,
        )

    def one(k):
        here = pl.ds(k * q, q)
        return send(x_ref.at[theirs(k)], from_mate.at[here], s1, r1, k, mate)

    def two(k):
        here = pl.ds(k * q, q)
        return send(chip.at[here], from_far.at[here], s2, r2, k, far)

    def three(k):
        return send(out_ref.at[mine(k)], out_ref.at[mine(k)], s3, r3, k, mate)

    for k in range(parts):
        one(k).start()
    for k in range(parts):
        here = slice(k * q, (k + 1) * q)
        one(k).wait_recv()
        chip[here, :] = (x_ref[mine(k), :].astype(F32) + from_mate[here, :].astype(F32)).astype(BF)
        two(k).start()
    for k in range(parts):
        here = slice(k * q, (k + 1) * q)
        two(k).wait_recv()
        out_ref[mine(k), :] = (chip[here, :].astype(F32) + from_far[here, :].astype(F32)).astype(BF)
        three(k).start()
    for k in range(parts):
        three(k).wait_recv()
    for k in range(parts):
        one(k).wait_send()
        two(k).wait_send()
        three(k).wait_send()


def sum_tensor(value):
    rows, cols = value.shape
    parts = 4 if cols >= 1024 else 1
    vm = pl.BlockSpec(memory_space=pltpu.VMEM)
    dma = pltpu.SemaphoreType.DMA
    part = pltpu.VMEM((rows // 2, cols), BF)
    return pl.pallas_call(
        functools.partial(pair_kernel, parts),
        out_shape=jax.ShapeDtypeStruct((rows, cols), BF),
        in_specs=[vm],
        out_specs=vm,
        scratch_shapes=[part, part, part] + [dma((parts,))] * 6,
        compiler_params=pltpu.CompilerParams(
            collective_id=3 if cols >= 1024 else 4, has_side_effects=True
        ),
        name="sum_tensor",
    )(value)


def sum_proj(value):
    cols = value.shape[1]
    padded = jnp.pad(value, ((0, 0), (0, -cols % LANES)))
    return sum_tensor(padded)[:, :cols]


def spread_kernel(n, x_ref, out_ref, got, s1, r1, s2, r2):
    d = lax.axis_index("dp")
    t = lax.axis_index("tensor")
    q = x_ref.shape[0] // n
    barrier = pltpu.get_barrier_semaphore()

    def peer(k):
        return lax.rem(d + k, n)

    @pl.loop(1, n)
    def _(k):
        pl.semaphore_signal(barrier, inc=1, device_id=(peer(k), t), device_id_type=MESH)

    pl.semaphore_wait(barrier, n - 1)

    def rows(e):
        return pl.ds(pl.multiple_of(e * q, 16), q)

    def one(k):
        return pltpu.make_async_remote_copy(
            src_ref=x_ref.at[rows(peer(k))],
            dst_ref=got.at[k - 1],
            send_sem=s1.at[k - 1],
            recv_sem=r1.at[k - 1],
            device_id=(peer(k), t),
            device_id_type=MESH,
        )

    def two(k):
        return pltpu.make_async_remote_copy(
            src_ref=out_ref.at[rows(d)],
            dst_ref=out_ref.at[rows(d)],
            send_sem=s2.at[k - 1],
            recv_sem=r2.at[k - 1],
            device_id=(peer(k), t),
            device_id_type=MESH,
        )

    @pl.loop(1, n)
    def _(k):
        one(k).start()

    @pl.loop(1, n)
    def _(k):
        one(k).wait_recv()

    def add(k, acc):
        return acc + got[k - 1].astype(F32)

    out_ref[rows(d), :] = lax.fori_loop(1, n, add, x_ref[rows(d), :].astype(F32)).astype(BF)

    @pl.loop(1, n)
    def _(k):
        two(k).start()

    @pl.loop(1, n)
    def _(k):
        two(k).wait_recv()

    @pl.loop(1, n)
    def _(k):
        one(k).wait_send()
        two(k).wait_send()


def sum_dp(value, n):
    count = value.shape[0]
    padded = jnp.pad(value, ((0, -count % (16 * n)), (0, 0)))
    vm = pl.BlockSpec(memory_space=pltpu.VMEM)
    dma = pltpu.SemaphoreType.DMA((n - 1,))
    return pl.pallas_call(
        functools.partial(spread_kernel, n),
        out_shape=jax.ShapeDtypeStruct(padded.shape, BF),
        in_specs=[vm],
        out_specs=vm,
        scratch_shapes=[pltpu.VMEM((n - 1, padded.shape[0] // n, LANES), BF), dma, dma, dma, dma],
        compiler_params=pltpu.CompilerParams(collective_id=5, has_side_effects=True),
        name="sum_dp",
    )(padded)[:count]


def rows_kernel(src, dst, src_ref, out_ref, inn, out):
    wide = src_ref.shape[1] // LANES
    thin = out_ref.shape[1] // LANES
    groups = src_ref.shape[0] // src
    for b in range(wide):
        inn[b] = src_ref[:, b * LANES : (b + 1) * LANES].astype(F32)
    for q in range(src * wide):
        a, b = divmod(q, wide)
        j, c = divmod(q, thin)
        out[c, pl.ds(j, groups, stride=dst), :] = inn[b, pl.ds(a, groups, stride=src), :]
    for c in range(thin):
        out_ref[:, c * LANES : (c + 1) * LANES] = out[c].astype(BF)


def change_rows(value, start, count, width):
    cols = value.shape[1]
    unit = math.gcd(cols, width)
    src, dst = width // unit, cols // unit
    block = 32 * src
    first = start // block
    return pl.pallas_call(
        functools.partial(rows_kernel, src, dst),
        grid=(count // block,),
        out_shape=jax.ShapeDtypeStruct((count * cols // width, width), BF),
        in_specs=[pl.BlockSpec((block, cols), lambda i: (i + first, 0))],
        out_specs=pl.BlockSpec((32 * dst, width), lambda i: (i, 0)),
        scratch_shapes=[
            pltpu.VMEM((cols // LANES, block, LANES), F32),
            pltpu.VMEM((width // LANES, 32 * dst, LANES), F32),
        ],
        compiler_params=pltpu.CompilerParams(vmem_limit_bytes=24 << 20),
        name="change_rows",
    )(value)


def spread(ref, value):
    rows = value.shape[0]
    for j in range(EI // LANES):
        ref[pl.ds(j, rows, stride=EI // LANES), :] = value[:, j * LANES : (j + 1) * LANES]


def collect(ref, rows):
    return jnp.concatenate(
        [ref[pl.ds(j, rows, stride=EI // LANES), :] for j in range(EI // LANES)], axis=1
    )


SUBL = EI // LANES


def scan_kernel(slots, proj_ref, bc_ref, unit_ref, gate_ref, w_dt_ref, bias_ref, skip_ref, alog_ref,
                gated_ref, step_s, su_s, y_s, rate_s):
    pre = jnp.dot(proj_ref[:, :DTR], w_dt_ref[...], preferred_element_type=F32) + bias_ref[...]
    step = softplus(pre)
    unit = unit_ref[...].astype(F32)
    spread(step_s, step)
    spread(su_s, step * unit)
    rate_s[...] = -jnp.exp(alog_ref[...]) * LOG2E

    def body(t, states):
        new = []
        for m in range(slots):
            r = m * SLOT + t
            row = pl.ds(pl.multiple_of(r * SUBL, SUBL), SUBL)
            st = step_s[row, :]
            su = su_s[row, :]
            y = jnp.zeros((SUBL, LANES), F32)
            for k in range(NSTATE):
                dec = jnp.exp2(rate_s[k * SUBL : (k + 1) * SUBL, :] * st)
                s = dec * states[m * NSTATE + k] + bc_ref[r, k] * su
                y = y + bc_ref[r, NSTATE + k] * s
                new.append(s)
            y_s[row, :] = y
        return tuple(new)

    init = tuple(jnp.zeros((SUBL, LANES), F32) for _ in range(slots * NSTATE))
    lax.fori_loop(0, SLOT, body, init)
    y = collect(y_s, slots * SLOT) + skip_ref[...] * unit
    z = gate_ref[...]
    gated_ref[...] = (y * silu(z)).astype(BF)


def scan_forward(proj, bc, unit, gate, w_dt, dt_bias, d_skip, a_log):
    rows = unit.shape[0]
    vm = pl.BlockSpec(memory_space=pltpu.VMEM)
    sm = pl.BlockSpec(memory_space=pltpu.SMEM)
    return pl.pallas_call(
        functools.partial(scan_kernel, rows // SLOT),
        out_shape=jax.ShapeDtypeStruct((rows, EI), BF),
        in_specs=[vm, sm, vm, vm, vm, vm, vm, vm],
        out_specs=vm,
        scratch_shapes=[
            pltpu.VMEM((rows * SUBL, LANES), F32),
            pltpu.VMEM((rows * SUBL, LANES), F32),
            pltpu.VMEM((rows * SUBL, LANES), F32),
            pltpu.VMEM((NSTATE * SUBL, LANES), F32),
        ],
        compiler_params=pltpu.CompilerParams(vmem_limit_bytes=60 << 20),
        name="scan_forward",
    )(proj, bc, unit, gate, w_dt, dt_bias, d_skip, a_log)


def adjoint_kernel(slots, proj_ref, bc_ref, unit_ref, gate_ref, w_dt_ref, bias_ref, skip_ref, alog_ref,
                   grad_ref, gz_ref, gunit_ref, gproj_ref, gdt_ref, gbias_ref, gskip_ref, galog_ref,
                   step_s, su_s, unit_s, y_s, gy_s, gs_s, lb_s, rate_s, hist, lams):
    rows = slots * SLOT
    pre = jnp.dot(proj_ref[:, :DTR], w_dt_ref[...], preferred_element_type=F32) + bias_ref[...]
    step = softplus(pre)
    unit = unit_ref[...].astype(F32)
    spread(step_s, step)
    spread(unit_s, unit)
    spread(su_s, step * unit)
    z = gate_ref[...]
    sig = jax.nn.sigmoid(z)
    gg = grad_ref[...]
    gy = gg * z * sig
    spread(gy_s, gy)
    rate_s[...] = -jnp.exp(alog_ref[...])
    galog_ref[...] = jnp.zeros_like(galog_ref)
    zero = jnp.zeros((SUBL, LANES), F32)
    span = SLOT + 1

    def hist_at(k, t):
        return pl.ds(pl.multiple_of((k * span + t) * SUBL, SUBL), SUBL)

    def lam_at(k, t):
        return pl.ds(pl.multiple_of((k * SLOT + t) * SUBL, SUBL), SUBL)

    for m in range(slots):
        for k in range(NSTATE):
            hist[hist_at(k, 0), :] = zero

        def forward(t, states):
            r = m * SLOT + t
            row = pl.ds(pl.multiple_of(r * SUBL, SUBL), SUBL)
            st = step_s[row, :] * LOG2E
            su = su_s[row, :]
            y = zero
            new = []
            for k in range(NSTATE):
                dec = jnp.exp2(rate_s[k * SUBL : (k + 1) * SUBL, :] * st)
                s = dec * states[k] + bc_ref[r, k] * su
                y = y + bc_ref[r, NSTATE + k] * s
                hist[hist_at(k, t + 1), :] = s
                new.append(s)
            y_s[row, :] = y
            return tuple(new)

        lax.fori_loop(0, SLOT, forward, tuple(zero for _ in range(NSTATE)))

        def backward(i, carry):
            t = SLOT - 1 - i
            r = m * SLOT + t
            row = pl.ds(pl.multiple_of(r * SUBL, SUBL), SUBL)
            st = step_s[row, :]
            st2 = st * LOG2E
            gyt = gy_s[row, :]
            lb = zero
            gs = zero
            new = []
            for k in range(NSTATE):
                rate = rate_s[k * SUBL : (k + 1) * SUBL, :]
                dec = jnp.exp2(rate * st2)
                lam = bc_ref[r, NSTATE + k] * gyt + carry[k]
                ld = dec * lam
                new.append(ld)
                lams[lam_at(k, t), :] = lam
                lb = lb + bc_ref[r, k] * lam
                x = ld * hist[hist_at(k, t), :]
                gs = gs + rate * x
                at = slice(k * SUBL, (k + 1) * SUBL)
                galog_ref[at, :] = galog_ref[at, :] + st * x
            lb_s[row, :] = lb
            gs_s[row, :] = gs + unit_s[row, :] * lb
            return tuple(new)

        lax.fori_loop(0, SLOT, backward, tuple(zero for _ in range(NSTATE)))
        out = slice(m * SLOT, (m + 1) * SLOT)
        base = m * SLOT * SUBL

        lane = lax.broadcasted_iota(jnp.int32, (SLOT, LANES), 1)

        def reduce_state(k, acc):
            ab = jnp.zeros((SLOT, LANES), F32)
            ac = jnp.zeros((SLOT, LANES), F32)
            for j in range(SUBL):
                cols = slice(j * LANES, (j + 1) * LANES)
                lam = lams[pl.ds(k * SLOT * SUBL + j, SLOT, stride=SUBL), :]
                h = hist[pl.ds((k * span + 1) * SUBL + j, SLOT, stride=SUBL), :]
                sj = su_s[pl.ds(base + j, SLOT, stride=SUBL), :]
                gj = gy_s[pl.ds(base + j, SLOT, stride=SUBL), :]
                ab = ab + lam * sj
                ac = ac + h * gj
            sb = jnp.sum(ab, axis=1, keepdims=True)
            sc = jnp.sum(ac, axis=1, keepdims=True)
            return acc + jnp.where(lane == k, sb, 0.0) + jnp.where(lane == NSTATE + k, sc, 0.0)

        sums = lax.fori_loop(0, NSTATE, reduce_state, jnp.zeros((SLOT, LANES), F32))
        gproj_ref[out, DTR : DTR + LANES] = sums.astype(BF)
    galog_ref[...] = galog_ref[...] * rate_s[...]
    y = collect(y_s, rows) + skip_ref[...] * unit
    gz_ref[...] = (gg * y * sig * (1.0 + z * (1.0 - sig))).astype(BF)
    gunit_ref[...] = gy * skip_ref[...] + step * collect(lb_s, rows)
    gskip_ref[...] = jnp.sum(gy * unit, axis=0, keepdims=True)
    q = collect(gs_s, rows) * jax.nn.sigmoid(pre)
    gbias_ref[...] = jnp.sum(q, axis=0, keepdims=True)
    ql = q.astype(BF)
    gdt_ref[...] = mat_tn(proj_ref[:, :DTR], ql)
    gproj_ref[:, :DTR] = mat_nt(ql, w_dt_ref[...]).astype(BF)


def scan_backward(proj, bc, unit, gate, w_dt, dt_bias, d_skip, a_log, grad):
    rows = unit.shape[0]
    vm = pl.BlockSpec(memory_space=pltpu.VMEM)
    sm = pl.BlockSpec(memory_space=pltpu.SMEM)
    sds = jax.ShapeDtypeStruct
    flat = pltpu.VMEM((rows * SUBL, LANES), F32)
    return pl.pallas_call(
        functools.partial(adjoint_kernel, rows // SLOT),
        out_shape=(
            sds((rows, EI), BF),
            sds((rows, EI), F32),
            sds((rows, DTR + LANES), BF),
            sds((DTR, EI), F32),
            sds((1, EI), F32),
            sds((1, EI), F32),
            sds((NSTATE * SUBL, LANES), F32),
        ),
        in_specs=[vm, sm, vm, vm, vm, vm, vm, vm, vm],
        out_specs=(vm,) * 7,
        scratch_shapes=[flat] * 7
        + [
            pltpu.VMEM((NSTATE * SUBL, LANES), F32),
            pltpu.VMEM((NSTATE * (SLOT + 1) * SUBL, LANES), F32),
            pltpu.VMEM((NSTATE * SLOT * SUBL, LANES), F32),
        ],
        compiler_params=pltpu.CompilerParams(vmem_limit_bytes=60 << 20),
        name="scan_backward",
    )(proj, bc, unit, gate, w_dt, dt_bias, d_skip, a_log, grad)


def rope_tables(length, head_dim):
    half_dim = head_dim // 2
    freq_index = jnp.arange(half_dim, dtype=F32)
    inv_freq = jnp.exp(-math.log(ROPE_BASE) * 2.0 * freq_index / head_dim)
    angles = jnp.arange(length, dtype=F32)[:, None] * inv_freq[None, :]
    return (jnp.cos(angles)[None, :, None, :], jnp.sin(angles)[None, :, None, :])


def rope_apply(values, cosine, sine):
    half_dim = values.shape[-1] // 2
    a = values[..., :half_dim]
    b = values[..., half_dim:]
    return jnp.concatenate([a * cosine - b * sine, b * cosine + a * sine], axis=-1)


def rms_parts(v, g):
    s = lax.rsqrt(jnp.mean(v * v, axis=-1, keepdims=True) + EPS_NORM)
    return s, v * s


def rms_back(v, g, gh):
    s, nrm = rms_parts(v, g)
    gg = jnp.sum(gh * nrm, axis=0)
    gv = s * (gh * g - nrm * jnp.mean(gh * g * nrm, axis=-1, keepdims=True))
    return gv, gg


def total(partial_out):
    return sum_tensor(partial_out.astype(BF)).astype(F32)


def shift_down(v, by):
    if by == 0:
        return v
    return jnp.pad(v, ((0, 0), (by, 0), (0, 0)))[:, : v.shape[1]]


def shift_up(v, by):
    if by == 0:
        return v
    return jnp.pad(v, ((0, 0), (0, by), (0, 0)))[:, by:]


def attend(query, keys, values):
    scale = HEAD_DIM ** (-0.5)
    distance = jnp.arange(SLOT)[:, None] - jnp.arange(SLOT)[None, :]
    allowed = (distance >= 0) & (distance < WINDOW)
    scores = jnp.einsum("mqhd,mkhd->mhqk", query, keys, preferred_element_type=F32) * scale
    scores = jnp.where(allowed, scores, NEG_FILL)
    expo = jnp.exp(scores - jnp.max(scores, axis=-1, keepdims=True))
    return expo / jnp.sum(expo, axis=-1, keepdims=True)


def ffn_forward(h, w_gu, w_down):
    pre = mat_nn(h, w_gu)
    act = (silu(pre[:, :FI]) * pre[:, FI:]).astype(BF)
    return total(mat_nn(act, w_down)), pre, act


def ffn_backward(pre, w_gu, w_down, grad_low):
    gate = pre[:, :FI]
    up = pre[:, FI:]
    ga = mat_nt(grad_low, w_down)
    sig = jax.nn.sigmoid(gate)
    grad_gate = ga * up * sig * (1.0 + gate * (1.0 - sig))
    grad_up = ga * gate * sig
    gp = jnp.concatenate([grad_gate, grad_up], axis=1).astype(BF)
    return total(mat_nt(gp, w_gu)), gp


def layer(x, grad_out, w, small, gains, n):
    rows = x.shape[0]
    m = rows // SLOT
    hr = HW // HEAD_DIM
    cosine, sine = rope_tables(SLOT, HEAD_DIM)
    s1, n1 = rms_parts(x, gains[0])
    h1 = (n1 * gains[0]).astype(BF)
    mixed = mat_nn(h1, w["w_in"])
    mix_x = mixed[:, :EI].reshape(m, SLOT, EI)
    gate_z = mixed[:, EI:]
    conv_w = small["conv_w"].astype(F32)
    pre_conv = small["conv_b"].astype(F32)[None, None, :]
    for j in range(CONV):
        pre_conv = pre_conv + conv_w[j] * shift_down(mix_x, CONV - 1 - j)
    unit = silu(pre_conv).astype(BF).reshape(rows, EI)
    proj = sum_proj(mat_nn(unit, small["w_x"]).astype(BF))
    bc = proj[:, DTR:].astype(F32)
    scan_args = (
        proj[:, :DTR],
        bc,
        unit,
        gate_z,
        small["w_dt"],
        small["dt_bias"].astype(F32)[None],
        small["d_skip"].astype(F32)[None],
        small["a_log"].astype(F32).reshape(NSTATE * SUBL, LANES),
    )
    gated = scan_forward(*scan_args)
    x1 = x + total(mat_nn(gated, w["w_out"]))
    h2 = (rms_parts(x1, 0)[1] * gains[1]).astype(BF)
    branch, pre1, act1 = ffn_forward(h2, w["w_gu1"], w["w_down1"])
    x2 = x1 + branch
    h3 = (rms_parts(x2, 0)[1] * gains[2]).astype(BF)
    packed = mat_nn(h3, w["w_qkv"]).reshape(m, SLOT, 3, hr, HEAD_DIM)
    query = rope_apply(packed[:, :, 0], cosine, sine).astype(BF)
    keys = rope_apply(packed[:, :, 1], cosine, sine).astype(BF)
    values = packed[:, :, 2].astype(BF)
    probs = attend(query, keys, values)
    probs_low = probs.astype(BF)
    attended = jnp.einsum("mhqk,mkhd->mqhd", probs_low, values, preferred_element_type=F32)
    attended = attended.reshape(rows, HW).astype(BF)
    x3 = x2 + total(mat_nn(attended, w["w_o"]))
    h4 = (rms_parts(x3, 0)[1] * gains[3]).astype(BF)
    branch, pre2, act2 = ffn_forward(h4, w["w_gu2"], w["w_down2"])
    x4 = x3 + branch

    gb4 = grad_out.astype(BF)
    gh, gp2 = ffn_backward(pre2, w["w_gu2"], w["w_down2"], gb4)
    gv, gg4 = rms_back(x3, gains[3], gh)
    g3 = grad_out + gv
    gb3 = g3.astype(BF)
    gatt = mat_nt(gb3, w["w_o"]).astype(BF).reshape(m, SLOT, hr, HEAD_DIM)
    grad_p = jnp.einsum("mqhd,mkhd->mhqk", gatt, values, preferred_element_type=F32)
    inner = jnp.sum(probs * grad_p, axis=-1, keepdims=True)
    gs = (probs * (grad_p - inner)).astype(BF)
    scale = HEAD_DIM ** (-0.5)
    gq = jnp.einsum("mhqk,mkhd->mqhd", gs, keys, preferred_element_type=F32) * scale
    gk = jnp.einsum("mhqk,mqhd->mkhd", gs, query, preferred_element_type=F32) * scale
    gvv = jnp.einsum("mhqk,mqhd->mkhd", probs_low, gatt, preferred_element_type=F32)
    gpk = (
        jnp.stack([rope_apply(gq, cosine, -sine), rope_apply(gk, cosine, -sine), gvv], axis=2)
        .reshape(rows, 3 * HW)
        .astype(BF)
    )
    gv, gg3 = rms_back(x2, gains[2], total(mat_nt(gpk, w["w_qkv"])))
    g2 = g3 + gv
    gb2 = g2.astype(BF)
    gh, gp1 = ffn_backward(pre1, w["w_gu1"], w["w_down1"], gb2)
    gv, gg2 = rms_back(x1, gains[1], gh)
    g1 = g2 + gv
    gb1 = g1.astype(BF)
    ggated = mat_nt(gb1, w["w_out"])
    gz, gunit, gproj, g_dt, g_bias, g_skip, g_alog = scan_backward(*scan_args, ggated)
    gproj = sum_tensor(gproj)[:, : DTR + 2 * NSTATE]
    g_wx = mat_tn(unit, gproj)
    gu = gunit + mat_nt(gproj, small["w_x"])
    sig = jax.nn.sigmoid(pre_conv)
    gpre = gu.reshape(m, SLOT, EI) * sig * (1.0 + pre_conv * (1.0 - sig))
    g_conv_b = jnp.sum(gpre, axis=(0, 1))
    g_conv_w = jnp.stack(
        [jnp.sum(gpre * shift_down(mix_x, CONV - 1 - j), axis=(0, 1)) for j in range(CONV)]
    )
    gmx = sum(conv_w[j] * shift_up(gpre, CONV - 1 - j) for j in range(CONV))
    gmixed = jnp.concatenate([gmx.reshape(rows, EI).astype(BF), gz], axis=1)
    gv, gg1 = rms_back(x, gains[0], total(mat_nt(gmixed, w["w_in"])))
    g0 = g1 + gv

    left_t = jnp.concatenate([h1, gated, h2, act1, attended, h4, act2], axis=1).T
    rights = jnp.stack([gmixed, gb1, gp1, gb2, gb3, gp2, gb4])
    g_qkv = mat_tn(h3, gpk).astype(BF)
    g_qkv = change_rows(g_qkv, 0, D, D)
    start = lax.axis_index("tensor") * DG
    g_gain = lax.dynamic_slice_in_dim(jnp.stack([gg1, gg2, gg3, gg4]), start, DG, 1)
    pieces = [g_gain, g_conv_w, g_conv_b, g_bias, g_skip, g_alog, g_wx, g_dt]
    small_grads = jnp.concatenate([p.reshape(-1, LANES).astype(BF) for p in pieces])
    small_sum = sum_dp(small_grads, n)
    g0, small_sum, left_t = lax.optimization_barrier((g0, small_sum, left_t))
    return x4.astype(BF), g0, (left_t, rights, g_qkv), small_sum


def extents(n, shard_rows):
    slab = BIG_ROWS * LINES // n
    before = 0
    after = 0
    back_before = 0
    back_after = 0
    for d in range(n):
        lo, hi = slab * d, slab * (d + 1) - 1
        qs = [p + LEAD + (SMALL_ROWS if p >= FIRST else 0) - shard_rows * d for p in (lo, hi)]
        before = max(before, -qs[0])
        after = max(after, qs[1] + 1 - shard_rows)
    return before, after


def shift_perm(n, by):
    return [(i, i + by) for i in range(n) if 0 <= i + by < n]


def stack_kernel(n, shard_lines, before, per, top_ref, own_ref, bottom_ref, out_ref, hold, sem):
    d = lax.axis_index("dp")
    i = pl.program_id(0)
    steps = BIG_ROWS // n // per
    size = per * LINES

    def fetch(k, slot):
        row = d * (BIG_ROWS // n) + k * per
        a = row * LINES + LEAD + jnp.where(row >= FIRST // LINES, SMALL_ROWS, 0) - d * shard_lines
        high = a < 0
        low = a + size > shard_lines

        @pl.when(high)
        def _():
            pltpu.make_async_copy(top_ref.at[pl.ds(a + before, size), 0], hold.at[slot], sem.at[slot]).start()

        @pl.when(low)
        def _():
            pltpu.make_async_copy(
                bottom_ref.at[pl.ds(a + size - shard_lines, size), 0], hold.at[slot], sem.at[slot]
            ).start()

        @pl.when(jnp.logical_not(jnp.logical_or(high, low)))
        def _():
            pltpu.make_async_copy(own_ref.at[pl.ds(a, size), 0], hold.at[slot], sem.at[slot]).start()

    @pl.when(i == 0)
    def _():
        for k in range(min(3, steps)):
            fetch(k, k)

    @pl.when(i + 3 < steps)
    def _():
        fetch(i + 3, lax.rem(i + 3, 4))

    slot = lax.rem(i, 4)
    pltpu.make_async_copy(own_ref.at[pl.ds(0, size), 0], hold.at[slot], sem.at[slot]).wait()
    for j in range(LINES):
        out_ref[:, j * LANES : (j + 1) * LANES] = hold[slot, pl.ds(j, per, stride=LINES), :].astype(BF)


def stack_own(lines3, n):
    shard_lines = lines3.shape[0]
    before, after = extents(n, shard_lines)
    rows = BIG_ROWS // n
    per = 64 if rows % 64 == 0 else 32
    size = per * LINES
    nxt = lax.ppermute(lines3[:after], "dp", shift_perm(n, -1))
    prv = lax.ppermute(lines3[shard_lines - before :], "dp", shift_perm(n, 1))
    top = jnp.concatenate([prv, lines3[:size]])
    bottom = jnp.concatenate([lines3[shard_lines - size :], nxt])
    hbm = pl.BlockSpec(memory_space=pl.ANY)
    return pl.pallas_call(
        functools.partial(stack_kernel, n, shard_lines, before, per),
        grid=(rows // per,),
        out_shape=jax.ShapeDtypeStruct((rows, D), BF),
        in_specs=[hbm] * 3,
        out_specs=pl.BlockSpec((per, D), lambda i: (i, 0)),
        scratch_shapes=[pltpu.VMEM((4, size, LANES), F32), pltpu.SemaphoreType.DMA((4,))],
        compiler_params=pltpu.CompilerParams(vmem_limit_bytes=24 << 20),
        name="stack_own",
    )(top, lines3, bottom)


def window(values, shift, size):
    length = values.shape[0]
    s = jnp.clip(shift, 0, length - size)
    got = lax.dynamic_slice_in_dim(values, s, size, 0)
    room = jnp.zeros((3 * size,) + values.shape[1:], values.dtype)
    room = lax.dynamic_update_slice_in_dim(room, got, size + jnp.clip(s - shift, -size, size), 0)
    return room[size : 2 * size]


STRIP = 8192


def lone_group(groups, bounds_ref, start, stop):
    def look(g, found):
        holds = jnp.logical_and(bounds_ref[2 * g] <= start, bounds_ref[2 * g + 1] >= stop)
        return jnp.where(holds, g, found)

    return lax.fori_loop(0, groups, look, jnp.int32(-1))


def moments_kernel(groups, shard, bounds_ref, grad_ref, w_ref, one_ref, two_ref,
                   first_ref, second_ref, grad_out, sums_ref, hold):
    i = pl.program_id(0)
    size = CHUNK * LANES
    lanes = STRIP // 8

    @pl.when(i == 0)
    def _():
        @pl.loop(0, 2 * groups)
        def _(g):
            sums_ref[g] = 0.0

    def strip(k, carry):
        here = pl.ds(pl.multiple_of(k * STRIP, STRIP), STRIP)
        grad = grad_ref[:, here]
        w = w_ref[:, here]
        first = BETA_ONE * one_ref[:, here] + (1.0 - BETA_ONE) * grad
        second = BETA_TWO * two_ref[:, here] + (1.0 - BETA_TWO) * grad * grad
        ratio = first / (jnp.sqrt(second) + ADAM_EPS) + DECAY_W * w
        first_ref[:, here] = first
        second_ref[:, here] = second
        grad_out[:, here] = grad
        hold[:, here] = ratio
        wsq, rsq = carry
        for j in range(8):
            part = slice(j * lanes, (j + 1) * lanes)
            wsq = wsq + w[:, part] * w[:, part]
            rsq = rsq + ratio[:, part] * ratio[:, part]
        return wsq, rsq

    zero = jnp.zeros((1, lanes), F32)
    wsq, rsq = lax.fori_loop(0, size // STRIP, strip, (zero, zero))
    d = lax.axis_index("dp")
    start = d * shard + i * size
    limit = (d + 1) * shard
    alone = lone_group(groups, bounds_ref, start, start + size)
    alone = jnp.where(start + size <= limit, alone, -1)

    @pl.when(alone >= 0)
    def _():
        sums_ref[2 * alone] = sums_ref[2 * alone] + jnp.sum(wsq)
        sums_ref[2 * alone + 1] = sums_ref[2 * alone + 1] + jnp.sum(rsq)

    @pl.when(alone < 0)
    def _():
        @pl.loop(0, groups)
        def _(g):
            low = jnp.maximum(bounds_ref[2 * g], start)
            high = jnp.minimum(bounds_ref[2 * g + 1], jnp.minimum(start + size, limit))

            @pl.when(low < high)
            def _():
                def masked(k, carry):
                    at = pl.multiple_of(k * lanes, lanes)
                    here = pl.ds(at, lanes)
                    index = start + at + lax.broadcasted_iota(jnp.int32, (1, lanes), 1)
                    inside = (index >= low) & (index < high)
                    wv = w_ref[:, here]
                    rv = hold[:, here]
                    return (
                        carry[0] + jnp.where(inside, wv * wv, 0.0),
                        carry[1] + jnp.where(inside, rv * rv, 0.0),
                    )

                k0 = (low - start) // lanes
                k1 = (high - start + lanes - 1) // lanes
                wv, rv = lax.fori_loop(k0, k1, masked, (zero, zero))
                sums_ref[2 * g] = sums_ref[2 * g] + jnp.sum(wv)
                sums_ref[2 * g + 1] = sums_ref[2 * g + 1] + jnp.sum(rv)


def moments(bounds, lines, master, one, two):
    shard = master.shape[1]
    size = CHUNK * LANES
    groups = bounds.shape[0] // 2
    block = pl.BlockSpec((1, size), lambda i: (0, i))
    ahead = SLACK // CHUNK
    flat = jax.ShapeDtypeStruct((1, shard), F32)
    smem = pl.BlockSpec(memory_space=pltpu.SMEM)
    return pl.pallas_call(
        functools.partial(moments_kernel, groups, shard),
        grid=(pl.cdiv(shard, size),),
        out_shape=(flat, flat, flat, jax.ShapeDtypeStruct((2 * groups,), F32)),
        in_specs=[smem, pl.BlockSpec((1, size), lambda i: (0, i + ahead)), block, block, block],
        out_specs=(block, block, block, smem),
        scratch_shapes=[pltpu.VMEM((1, size), F32)],
        compiler_params=pltpu.CompilerParams(vmem_limit_bytes=40 << 20),
        name="moments",
    )(bounds, lines.reshape(1, -1), master, one, two)


def update_kernel(groups, shard, bounds_ref, trust_ref, w_ref, first_ref, second_ref, new_ref, low_ref, hold):
    i = pl.program_id(0)
    size = CHUNK * LANES
    lanes = STRIP // 8
    start = lax.axis_index("dp") * shard + i * size
    alone = lone_group(groups, bounds_ref, start, start + size)

    def step(trust_of):
        @pl.loop(0, size // STRIP)
        def _(k):
            here = pl.ds(pl.multiple_of(k * STRIP, STRIP), STRIP)
            w = w_ref[:, here]
            ratio = first_ref[:, here] / (jnp.sqrt(second_ref[:, here]) + ADAM_EPS) + DECAY_W * w
            new = w - LEARN_RATE * trust_of(here) * ratio
            new_ref[:, here] = new
            low_ref[:, here] = new.astype(BF)

    @pl.when(alone >= 0)
    def _():
        trust = trust_ref[jnp.maximum(alone, 0)]
        step(lambda here: trust)

    @pl.when(alone < 0)
    def _():
        hold[...] = jnp.zeros_like(hold)

        @pl.loop(0, groups)
        def _(g):
            low = jnp.maximum(bounds_ref[2 * g], start)
            high = jnp.minimum(bounds_ref[2 * g + 1], start + size)

            @pl.when(low < high)
            def _():
                @pl.loop((low - start) // lanes, (high - start + lanes - 1) // lanes)
                def _(k):
                    at = pl.multiple_of(k * lanes, lanes)
                    here = pl.ds(at, lanes)
                    index = start + at + lax.broadcasted_iota(jnp.int32, (1, lanes), 1)
                    hold[:, here] = jnp.where((index >= low) & (index < high), trust_ref[g], hold[:, here])

        step(lambda here: hold[:, here])


def update(bounds, trust, master, first, second):
    shard = master.shape[1]
    size = CHUNK * LANES
    groups = bounds.shape[0] // 2
    block = pl.BlockSpec((1, size), lambda i: (0, i))
    smem = pl.BlockSpec(memory_space=pltpu.SMEM)
    return pl.pallas_call(
        functools.partial(update_kernel, groups, shard),
        grid=(pl.cdiv(shard, size),),
        out_shape=(jax.ShapeDtypeStruct((1, shard), F32), jax.ShapeDtypeStruct((1, shard), BF)),
        in_specs=[smem, smem, block, block, block],
        out_specs=(block, block),
        scratch_shapes=[pltpu.VMEM((1, size), F32)],
        compiler_params=pltpu.CompilerParams(vmem_limit_bytes=40 << 20),
        name="update",
    )(bounds, trust, master, first, second)


def norms_kernel(n, m, own_ref, out_ref, across, along, part, ssem, rsem, ssem2, rsem2):
    d = lax.axis_index("dp")
    t = lax.axis_index("tensor")
    barrier = pltpu.get_barrier_semaphore()
    for k in range(1, m):
        pl.semaphore_signal(barrier, inc=1, device_id=(d, lax.rem(t + k, m)), device_id_type=MESH)

    @pl.loop(1, n)
    def _(k):
        pl.semaphore_signal(barrier, inc=1, device_id=(lax.rem(d + k, n), t), device_id_type=MESH)

    pl.semaphore_wait(barrier, n + m - 2)

    def over_tensor(k):
        return pltpu.make_async_remote_copy(
            src_ref=own_ref,
            dst_ref=across.at[k - 1],
            send_sem=ssem.at[k - 1],
            recv_sem=rsem.at[k - 1],
            device_id=(d, lax.rem(t + k, m)),
            device_id_type=MESH,
        )

    def over_dp(k):
        return pltpu.make_async_remote_copy(
            src_ref=part,
            dst_ref=along.at[k - 1],
            send_sem=ssem2.at[k - 1],
            recv_sem=rsem2.at[k - 1],
            device_id=(lax.rem(d + k, n), t),
            device_id_type=MESH,
        )

    for k in range(1, m):
        over_tensor(k).start()
    total_ = own_ref[...]
    for k in range(1, m):
        over_tensor(k).wait_recv()
    for k in range(1, m):
        total_ = total_ + across[k - 1]
    part[...] = total_

    @pl.loop(1, n)
    def _(k):
        over_dp(k).start()

    @pl.loop(1, n)
    def _(k):
        over_dp(k).wait_recv()

    def add(k, acc):
        return acc + along[k - 1]

    out_ref[...] = lax.fori_loop(1, n, add, part[...])
    for k in range(1, m):
        over_tensor(k).wait_send()

    @pl.loop(1, n)
    def _(k):
        over_dp(k).wait_send()


def sum_everywhere(values, n, m):
    vm = pl.BlockSpec(memory_space=pltpu.VMEM)
    dma = pltpu.SemaphoreType.DMA
    tile = pltpu.VMEM((8, LANES), F32)
    return pl.pallas_call(
        functools.partial(norms_kernel, n, m),
        out_shape=jax.ShapeDtypeStruct((8, LANES), F32),
        in_specs=[vm],
        out_specs=vm,
        scratch_shapes=[
            pltpu.VMEM((m - 1, 8, LANES), F32),
            pltpu.VMEM((n - 1, 8, LANES), F32),
            tile,
            dma((m - 1,)),
            dma((m - 1,)),
            dma((n - 1,)),
            dma((n - 1,)),
        ],
        compiler_params=pltpu.CompilerParams(collective_id=2, has_side_effects=True),
        name="sum_everywhere",
    )(values)


def per_device(n, m, tokens, cotangent, lengths, master, moment_one, moment_two):
    d = lax.axis_index("dp")
    shard = master.shape[1]
    lines = shard // LANES
    lines3 = master.reshape(lines, 1, LANES)
    base = d * lines
    mid = LEAD + FIRST
    small_own = jnp.concatenate(
        [window(lines3, -base, GAIN_ROWS), window(lines3, mid - base, SMALL_ROWS)]
    )
    small_own = lax.optimization_barrier(small_own)
    small_flat = lax.psum(small_own.reshape(-1, LANES).astype(BF), "dp")
    weights = ring_gather(stack_own(lines3, n), n)
    weights, small_flat = lax.optimization_barrier((weights, small_flat))
    gains = lax.all_gather(small_flat[:GAIN_ROWS].reshape(4, DG), "tensor", axis=1, tiled=True)
    gains = gains.astype(F32)
    small = {}
    at = GAIN_ROWS
    for name, shape in SMALL:
        count = math.prod(shape) // LANES
        small[name] = small_flat[at : at + count].reshape(shape)
        at += count
    w = {}
    for name, rows in BIG:
        w[name] = weights[BIG_OFF[name] : BIG_OFF[name] + rows]
    w["w_qkv"] = change_rows(weights, BIG_OFF["w_qkv"], dict(BIG)["w_qkv"], 3 * HW)
    x = tokens.astype(F32)
    pos = lax.broadcasted_iota(jnp.int32, (tokens.shape[0] // SLOT, SLOT), 1)
    valid = (pos < lengths[:, None]).astype(F32).reshape(-1, 1)
    grad = cotangent.astype(F32) * valid
    out, grad_in, operands, small_grads = layer(x, grad, w, small, gains, n)
    small_sum = small_grads.astype(F32).reshape(-1, 1, LANES)
    laid = ring_reduce(*operands, n, lines)

    before, after = extents(n, lines)
    slab_lines = BIG_ROWS * LINES // n

    def local(row):
        return row * LINES + LEAD + jnp.where(row >= FIRST // LINES, SMALL_ROWS, 0) - base

    begin = local(d * (BIG_ROWS // n))
    close = local((d + 1) * (BIG_ROWS // n) - 1) + LINES
    tail, head, laid = lax.optimization_barrier(
        (laid[SLACK + lines : SLACK + lines + after], laid[SLACK - before : SLACK], laid)
    )
    from_prev = lax.ppermute(tail, "dp", shift_perm(n, 1))
    from_next = lax.ppermute(head, "dp", shift_perm(n, -1))
    line = lax.broadcasted_iota(jnp.int32, (after, 1, 1), 0)
    top = jnp.where(line < begin, from_prev, laid[SLACK : SLACK + after])
    line = lax.broadcasted_iota(jnp.int32, (before, 1, 1), 0) + (lines - before)
    bottom = jnp.where(line >= close, from_next, laid[SLACK + lines - before : SLACK + lines])
    laid = laid.at[SLACK : SLACK + after].set(top)
    laid = laid.at[SLACK + lines - before : SLACK + lines].set(bottom)

    def place(laid, values, at):
        count = values.shape[0]
        return lax.dynamic_update_slice_in_dim(laid, values, SLACK + jnp.clip(at - base, -count, lines), 0)

    laid = place(laid, small_sum[GAIN_ROWS:], mid)
    laid = place(laid, small_sum[:GAIN_ROWS], 0)
    used = LEAD + SMALL_ROWS + BIG_ROWS * LINES
    rest = lines * n - used
    if rest:
        laid = place(laid, jnp.zeros((rest, 1, LANES), F32), used)

    bounds = jnp.asarray([v for pair in group_bounds() for v in pair], jnp.int32)
    first, second, grad_shard, sums = moments(bounds, laid, master, moment_one, moment_two)
    count = sums.shape[0]
    tile = jnp.pad(sums, (0, 8 * LANES - count)).reshape(8, LANES)
    squares = sum_everywhere(tile, n, m).reshape(-1)[:count].reshape(-1, 2)
    trust = jnp.sqrt(squares[:, 0] + TRUST_EPSILON) * lax.rsqrt(squares[:, 1] + TRUST_EPSILON)
    master_new, low = update(bounds, trust, master, first, second)
    return (out, grad_in, master_new, first, second, low, grad_shard, jnp.sqrt(squares))


def solution(mesh):
    row = P("dp", None)
    flat = P("tensor", "dp")
    return jax.shard_map(
        functools.partial(per_device, mesh.shape["dp"], mesh.shape["tensor"]),
        mesh=mesh,
        in_specs=(row, row, P("dp"), flat, flat, flat),
        out_specs=(row, row, flat, flat, flat, flat, flat, P()),
        check_vma=False,
    )
```

```python
import functools
import math

import jax
import jax.numpy as jnp
from jax import lax
from jax.experimental import pallas as pl
from jax.experimental.pallas import tpu as pltpu
from jax.sharding import PartitionSpec as P

D = 2048
INNER = 4096
NSTATE = 16
DTR = 128
HEADS = 32
HEAD_DIM = 64
FF = 4096
CONV = 4
WINDOW = 2048
SLOT = 128
LANES = 128

EPS_NORM = 1e-05
TRUST_EPSILON = 1e-06
ROPE_BASE = 10000.0
BETA_ONE = 0.5
BETA_TWO = 0.55
ADAM_EPS = 1e-06
DECAY_W = 0.01
LEARN_RATE = 0.2
NEG_FILL = -1e30
LOG2E = 1.4426950408889634
MESH = pl.DeviceIdType.MESH
BF = jnp.bfloat16
F32 = jnp.float32

EI = INNER // 4
FI = FF // 4
HW = HEADS * HEAD_DIM // 4
DG = D // 4

SMALL = [
    ("conv_w", (CONV, EI)),
    ("conv_b", (EI,)),
    ("dt_bias", (EI,)),
    ("d_skip", (EI,)),
    ("a_log", (NSTATE, EI)),
    ("w_x", (EI, DTR + 2 * NSTATE)),
    ("w_dt", (DTR, EI)),
]
SMALL_ROWS = sum(math.prod(s) for _, s in SMALL) // LANES
GAIN_ROWS = 4 * DG // LANES
BIG = [
    ("w_in", D),
    ("w_out", EI),
    ("w_gu1", D),
    ("w_down1", FI),
    ("w_qkv", D * 3 * HW // D),
    ("w_o", HW),
    ("w_gu2", D),
    ("w_down2", FI),
]
BIG_OFF = {}
_at = 0
for _name, _rows in BIG:
    BIG_OFF[_name] = _at
    _at += _rows
BIG_ROWS = _at
LINES = D // LANES
FIRST = BIG_OFF["w_out"] * LINES
LEAD = GAIN_ROWS
CHUNK = 1024
SLACK = -(-(SMALL_ROWS + GAIN_ROWS) // CHUNK) * CHUNK


def group_bounds():
    bounds = []
    for k in range(4):
        bounds.append((k * DG, (k + 1) * DG))
    at = 4 * DG
    entries = [("w_in", D * 2 * EI)]
    entries += [(name, math.prod(shape)) for name, shape in SMALL]
    entries += [
        ("w_out", EI * D),
        ("w_gu1", D * 2 * FI),
        ("w_down1", FI * D),
        ("w_qkv", D * 3 * HW),
        ("w_o", HW * D),
        ("w_gu2", D * 2 * FI),
        ("w_down2", FI * D),
    ]
    for _, count in entries:
        bounds.append((at, at + count))
        at += count
    return bounds


def silu(v):
    return v * jax.nn.sigmoid(v)


def softplus(v):
    return jnp.maximum(v, 0.0) + jnp.log1p(jnp.exp(-jnp.abs(v)))


def mat_nn(a, b):
    return jnp.dot(a, b, preferred_element_type=F32)


def mat_tn(a, b):
    return lax.dot_general(a, b, (((0,), (0,)), ((), ())), preferred_element_type=F32)


def mat_nt(a, b):
    return lax.dot_general(a, b, (((1,), (1,)), ((), ())), preferred_element_type=F32)


def ring_pos(d, n):
    return jnp.where(lax.rem(d, 2) == 0, lax.div(d, 2), n - 1 - lax.div(d, 2))


def ring_dev(p, n):
    return jnp.where(p < n // 2, 2 * p, 2 * (n - 1 - p) + 1)


def ring_neighbours(n):
    d = lax.axis_index("dp")
    p = ring_pos(d, n)
    right = ring_dev(lax.rem(p + 1, n), n)
    left = ring_dev(lax.rem(p + n - 1, n), n)
    return d, p, right, left


def ring_barrier(left, right, t):
    barrier = pltpu.get_barrier_semaphore()
    for nb in (left, right):
        pl.semaphore_signal(barrier, inc=1, device_id=(nb, t), device_id_type=MESH)
    pl.semaphore_wait(barrier, 2)


def gather_kernel(n, subs, own_ref, out_ref, hold, local_sem, ssem, rsem):
    t = lax.axis_index("tensor")
    d, p, right, left = ring_neighbours(n)
    rows = own_ref.shape[0]
    half = rows // 2
    sub = half // subs
    fetch = pltpu.make_async_copy(own_ref, hold, local_sem.at[0])
    fetch.start()
    ring_barrier(left, right, t)

    def copy(way, step, c, from_own):
        target = right if way == 0 else left
        owner = ring_dev(lax.rem(p + (n - step if way == 0 else step), n), n)
        at = pl.multiple_of(owner * rows + way * half + c * sub, 8)
        src = own_ref.at[pl.ds(way * half + c * sub, sub)] if from_own else out_ref.at[pl.ds(at, sub)]
        return pltpu.make_async_remote_copy(
            src_ref=src,
            dst_ref=out_ref.at[pl.ds(at, sub)],
            send_sem=ssem.at[way, step, c],
            recv_sem=rsem.at[way, step, c],
            device_id=(target, t),
            device_id_type=MESH,
        )

    for c in range(subs):
        for way in (0, 1):
            copy(way, 0, c, True).start()
    fetch.wait()
    store = pltpu.make_async_copy(
        hold, out_ref.at[pl.ds(pl.multiple_of(d * rows, 8), rows)], local_sem.at[1]
    )
    store.start()
    for step in range(1, n - 1):
        for c in range(subs):
            for way in (0, 1):
                copy(way, step - 1, c, step == 1).wait_recv()
                copy(way, step, c, False).start()
    for c in range(subs):
        for way in (0, 1):
            copy(way, n - 2, c, n == 2).wait_recv()
    store.wait()
    for step in range(n - 1):
        for c in range(subs):
            for way in (0, 1):
                copy(way, step, c, step == 0).wait_send()


def ring_gather(own, n):
    rows, cols = own.shape
    subs = 2
    return pl.pallas_call(
        functools.partial(gather_kernel, n, subs),
        out_shape=jax.ShapeDtypeStruct((n * rows, cols), own.dtype),
        in_specs=[pl.BlockSpec(memory_space=pl.ANY)],
        out_specs=pl.BlockSpec(memory_space=pl.ANY),
        scratch_shapes=[
            pltpu.VMEM((rows, cols), own.dtype),
            pltpu.SemaphoreType.DMA((2,)),
            pltpu.SemaphoreType.DMA((2, n - 1, subs)),
            pltpu.SemaphoreType.DMA((2, n - 1, subs)),
        ],
        cost_estimate=pl.CostEstimate(flops=10**9, bytes_accessed=1500 * 10**6, transcendentals=0),
        compiler_params=pltpu.CompilerParams(
            collective_id=0, has_side_effects=True, vmem_limit_bytes=32 << 20
        ),
        name="ring_gather",
    )(own)


def piece_of(half):
    for size in (64, 32, 16):
        if half % size == 0:
            return size


def reduce_kernel(n, shard_lines, left_ref, right_refs, qkv_ref, out_ref, slots, lines, ssem, rsem, out_sem):
    t = lax.axis_index("tensor")
    d, p, right, left = ring_neighbours(n)
    rows = BIG_ROWS // n
    half = rows // 2
    SUB = piece_of(half)
    subs = half // SUB
    ring_barrier(left, right, t)
    qkv_at = BIG_OFF["w_qkv"]
    qkv_rows = dict(BIG)["w_qkv"]

    def own_into(at, put):
        in_qkv = jnp.logical_and(at >= qkv_at, at < qkv_at + qkv_rows)
        which = jnp.int32(0)
        for name, _ in BIG[1:]:
            if name != "w_qkv":
                which = which + jnp.where(at >= BIG_OFF[name], 1, 0)

        @pl.when(in_qkv)
        def _():
            put(qkv_ref[pl.ds(pl.multiple_of(at - qkv_at, SUB), SUB), :].astype(F32))

        @pl.when(jnp.logical_not(in_qkv))
        def _():
            row = jnp.where(at >= qkv_at + qkv_rows, at - qkv_rows, at)
            lt = left_ref[pl.ds(pl.multiple_of(row, SUB), SUB), :]
            put(jnp.dot(lt, right_refs[which], preferred_element_type=F32))

    def owner_of(way, step):
        return ring_dev(lax.rem(p + (n - 1 - step if way == 0 else 1 + step), n), n)

    def copy(way, step, c):
        target = right if way == 0 else left
        return pltpu.make_async_remote_copy(
            src_ref=slots.at[way, step, pl.ds(pl.multiple_of(c * SUB, SUB), SUB)],
            dst_ref=slots.at[way, step + 1, pl.ds(pl.multiple_of(c * SUB, SUB), SUB)],
            send_sem=ssem.at[way, step, c],
            recv_sem=rsem.at[way, step, c],
            device_id=(target, t),
            device_id_type=MESH,
        )

    def run(step):
        @pl.loop(0, subs)
        def _(c):
            here = pl.ds(pl.multiple_of(c * SUB, SUB), SUB)
            for way in (0, 1):
                at = owner_of(way, step) * rows + way * half + c * SUB
                if step > 0:
                    copy(way, step - 1, c).wait_recv()

                def put(value):
                    if step > 0:
                        value = value + slots[way, step, here, :].astype(F32)
                    if step < n - 1:
                        slots[way, step, here, :] = value.astype(BF)
                    else:
                        for j in range(LINES):
                            lines[way, pl.ds(j, SUB, stride=LINES), :] = value[:, j * LANES : (j + 1) * LANES]

                if step == n - 1:

                    @pl.when(c > 0)
                    def _():
                        leave(way, c - 1).wait()

                own_into(at, put)
                if step < n - 1:
                    copy(way, step, c).start()
                else:
                    leave(way, c).start()

    def leave(way, c):
        row = d * rows + way * half + c * SUB
        to = row * LINES + LEAD + jnp.where(row >= FIRST // LINES, SMALL_ROWS, 0) - d * shard_lines + SLACK
        return pltpu.make_async_copy(
            lines.at[way], out_ref.at[pl.ds(to, SUB * LINES), 0], out_sem.at[way]
        )

    for step in range(n):
        run(step)
    for way in (0, 1):
        leave(way, subs - 1).wait()

    @pl.loop(0, subs)
    def _(c):
        for way in (0, 1):
            for step in range(n - 1):
                copy(way, step, c).wait_send()


def ring_reduce(left_t, rights, qkv_grad, n, shard_lines):
    rows = BIG_ROWS // n
    sub = piece_of(rows // 2)
    subs = rows // 2 // sub
    vm = pl.BlockSpec(memory_space=pltpu.VMEM)
    return pl.pallas_call(
        functools.partial(reduce_kernel, n, shard_lines),
        out_shape=jax.ShapeDtypeStruct((shard_lines + 2 * SLACK, 1, LANES), F32),
        in_specs=[vm, vm, vm],
        out_specs=pl.BlockSpec(memory_space=pl.ANY),
        scratch_shapes=[
            pltpu.VMEM((2, n, rows // 2, D), BF),
            pltpu.VMEM((2, sub * LINES, LANES), F32),
            pltpu.SemaphoreType.DMA((2, n - 1, subs)),
            pltpu.SemaphoreType.DMA((2, n - 1, subs)),
            pltpu.SemaphoreType.DMA((2,)),
        ],
        cost_estimate=pl.CostEstimate(flops=10**9, bytes_accessed=1500 * 10**6, transcendentals=0),
        compiler_params=pltpu.CompilerParams(
            collective_id=1, has_side_effects=True, vmem_limit_bytes=67043328
        ),
        name="ring_reduce",
    )(left_t, rights, qkv_grad)


def pair_kernel(parts, x_ref, out_ref, from_mate, chip, from_far, s1, r1, s2, r2, s3, r3):
    d = lax.axis_index("dp")
    t = lax.axis_index("tensor")
    core = lax.rem(t, 2)
    mate = t + 1 - 2 * core
    far = lax.rem(t + 2, 4)
    half = x_ref.shape[0] // 2
    q = half // parts
    barrier = pltpu.get_barrier_semaphore()
    for peer in (mate, far):
        pl.semaphore_signal(barrier, inc=1, device_id=(d, peer), device_id_type=MESH)
    pl.semaphore_wait(barrier, 2)

    def mine(k):
        return pl.ds(pl.multiple_of(core * half + k * q, 16), q)

    def theirs(k):
        return pl.ds(pl.multiple_of((1 - core) * half + k * q, 16), q)

    def send(src, dst, ssem, rsem, k, peer):
        return pltpu.make_async_remote_copy(
            src_ref=src,
            dst_ref=dst,
            send_sem=ssem.at[k],
            recv_sem=rsem.at[k],
            device_id=(d, peer),
            device_id_type=MESH,
        )

    def one(k):
        here = pl.ds(k * q, q)
        return send(x_ref.at[theirs(k)], from_mate.at[here], s1, r1, k, mate)

    def two(k):
        here = pl.ds(k * q, q)
        return send(chip.at[here], from_far.at[here], s2, r2, k, far)

    def three(k):
        return send(out_ref.at[mine(k)], out_ref.at[mine(k)], s3, r3, k, mate)

    for k in range(parts):
        one(k).start()
    for k in range(parts):
        here = slice(k * q, (k + 1) * q)
        one(k).wait_recv()
        chip[here, :] = (x_ref[mine(k), :].astype(F32) + from_mate[here, :].astype(F32)).astype(BF)
        two(k).start()
    for k in range(parts):
        here = slice(k * q, (k + 1) * q)
        two(k).wait_recv()
        out_ref[mine(k), :] = (chip[here, :].astype(F32) + from_far[here, :].astype(F32)).astype(BF)
        three(k).start()
    for k in range(parts):
        three(k).wait_recv()
    for k in range(parts):
        one(k).wait_send()
        two(k).wait_send()
        three(k).wait_send()


def sum_tensor(value):
    rows, cols = value.shape
    parts = 4 if cols >= 1024 else 1
    vm = pl.BlockSpec(memory_space=pltpu.VMEM)
    dma = pltpu.SemaphoreType.DMA
    part = pltpu.VMEM((rows // 2, cols), BF)
    return pl.pallas_call(
        functools.partial(pair_kernel, parts),
        out_shape=jax.ShapeDtypeStruct((rows, cols), BF),
        in_specs=[vm],
        out_specs=vm,
        scratch_shapes=[part, part, part] + [dma((parts,))] * 6,
        compiler_params=pltpu.CompilerParams(
            collective_id=3 if cols >= 1024 else 4, has_side_effects=True
        ),
        name="sum_tensor",
    )(value)


def sum_proj(value):
    cols = value.shape[1]
    padded = jnp.pad(value, ((0, 0), (0, -cols % LANES)))
    return sum_tensor(padded)[:, :cols]


def rows_kernel(src, dst, src_ref, out_ref, inn, out):
    wide = src_ref.shape[1] // LANES
    thin = out_ref.shape[1] // LANES
    groups = src_ref.shape[0] // src
    for b in range(wide):
        inn[b] = src_ref[:, b * LANES : (b + 1) * LANES].astype(F32)
    for q in range(src * wide):
        a, b = divmod(q, wide)
        j, c = divmod(q, thin)
        out[c, pl.ds(j, groups, stride=dst), :] = inn[b, pl.ds(a, groups, stride=src), :]
    for c in range(thin):
        out_ref[:, c * LANES : (c + 1) * LANES] = out[c].astype(BF)


def change_rows(value, start, count, width):
    cols = value.shape[1]
    unit = math.gcd(cols, width)
    src, dst = width // unit, cols // unit
    block = 32 * src
    first = start // block
    return pl.pallas_call(
        functools.partial(rows_kernel, src, dst),
        grid=(count // block,),
        out_shape=jax.ShapeDtypeStruct((count * cols // width, width), BF),
        in_specs=[pl.BlockSpec((block, cols), lambda i: (i + first, 0))],
        out_specs=pl.BlockSpec((32 * dst, width), lambda i: (i, 0)),
        scratch_shapes=[
            pltpu.VMEM((cols // LANES, block, LANES), F32),
            pltpu.VMEM((width // LANES, 32 * dst, LANES), F32),
        ],
        compiler_params=pltpu.CompilerParams(vmem_limit_bytes=24 << 20),
        name="change_rows",
    )(value)


def spread(ref, value):
    rows = value.shape[0]
    for j in range(EI // LANES):
        ref[pl.ds(j, rows, stride=EI // LANES), :] = value[:, j * LANES : (j + 1) * LANES]


def collect(ref, rows):
    return jnp.concatenate(
        [ref[pl.ds(j, rows, stride=EI // LANES), :] for j in range(EI // LANES)], axis=1
    )


SUBL = EI // LANES


def scan_kernel(slots, proj_ref, bc_ref, unit_ref, gate_ref, w_dt_ref, bias_ref, skip_ref, alog_ref,
                gated_ref, step_s, su_s, y_s, rate_s):
    pre = jnp.dot(proj_ref[:, :DTR], w_dt_ref[...], preferred_element_type=F32) + bias_ref[...]
    step = softplus(pre)
    unit = unit_ref[...].astype(F32)
    spread(step_s, step)
    spread(su_s, step * unit)
    rate_s[...] = -jnp.exp(alog_ref[...]) * LOG2E

    def body(t, states):
        new = []
        for m in range(slots):
            r = m * SLOT + t
            row = pl.ds(pl.multiple_of(r * SUBL, SUBL), SUBL)
            st = step_s[row, :]
            su = su_s[row, :]
            y = jnp.zeros((SUBL, LANES), F32)
            for k in range(NSTATE):
                dec = jnp.exp2(rate_s[k * SUBL : (k + 1) * SUBL, :] * st)
                s = dec * states[m * NSTATE + k] + bc_ref[r, k] * su
                y = y + bc_ref[r, NSTATE + k] * s
                new.append(s)
            y_s[row, :] = y
        return tuple(new)

    init = tuple(jnp.zeros((SUBL, LANES), F32) for _ in range(slots * NSTATE))
    lax.fori_loop(0, SLOT, body, init)
    y = collect(y_s, slots * SLOT) + skip_ref[...] * unit
    z = gate_ref[...]
    gated_ref[...] = (y * silu(z)).astype(BF)


def scan_forward(proj, bc, unit, gate, w_dt, dt_bias, d_skip, a_log):
    rows = unit.shape[0]
    vm = pl.BlockSpec(memory_space=pltpu.VMEM)
    sm = pl.BlockSpec(memory_space=pltpu.SMEM)
    return pl.pallas_call(
        functools.partial(scan_kernel, rows // SLOT),
        out_shape=jax.ShapeDtypeStruct((rows, EI), BF),
        in_specs=[vm, sm, vm, vm, vm, vm, vm, vm],
        out_specs=vm,
        scratch_shapes=[
            pltpu.VMEM((rows * SUBL, LANES), F32),
            pltpu.VMEM((rows * SUBL, LANES), F32),
            pltpu.VMEM((rows * SUBL, LANES), F32),
            pltpu.VMEM((NSTATE * SUBL, LANES), F32),
        ],
        compiler_params=pltpu.CompilerParams(vmem_limit_bytes=60 << 20),
        name="scan_forward",
    )(proj, bc, unit, gate, w_dt, dt_bias, d_skip, a_log)


def adjoint_kernel(slots, proj_ref, bc_ref, unit_ref, gate_ref, w_dt_ref, bias_ref, skip_ref, alog_ref,
                   grad_ref, gz_ref, gunit_ref, gproj_ref, gdt_ref, gbias_ref, gskip_ref, galog_ref,
                   step_s, su_s, unit_s, y_s, gy_s, gs_s, lb_s, rate_s, hist, lams):
    rows = slots * SLOT
    pre = jnp.dot(proj_ref[:, :DTR], w_dt_ref[...], preferred_element_type=F32) + bias_ref[...]
    step = softplus(pre)
    unit = unit_ref[...].astype(F32)
    spread(step_s, step)
    spread(unit_s, unit)
    spread(su_s, step * unit)
    z = gate_ref[...]
    sig = jax.nn.sigmoid(z)
    gg = grad_ref[...]
    gy = gg * z * sig
    spread(gy_s, gy)
    rate_s[...] = -jnp.exp(alog_ref[...])
    galog_ref[...] = jnp.zeros_like(galog_ref)
    zero = jnp.zeros((SUBL, LANES), F32)
    span = SLOT + 1

    def hist_at(k, t):
        return pl.ds(pl.multiple_of((k * span + t) * SUBL, SUBL), SUBL)

    def lam_at(k, t):
        return pl.ds(pl.multiple_of((k * SLOT + t) * SUBL, SUBL), SUBL)

    for m in range(slots):
        for k in range(NSTATE):
            hist[hist_at(k, 0), :] = zero

        def forward(t, states):
            r = m * SLOT + t
            row = pl.ds(pl.multiple_of(r * SUBL, SUBL), SUBL)
            st = step_s[row, :] * LOG2E
            su = su_s[row, :]
            y = zero
            new = []
            for k in range(NSTATE):
                dec = jnp.exp2(rate_s[k * SUBL : (k + 1) * SUBL, :] * st)
                s = dec * states[k] + bc_ref[r, k] * su
                y = y + bc_ref[r, NSTATE + k] * s
                hist[hist_at(k, t + 1), :] = s
                new.append(s)
            y_s[row, :] = y
            return tuple(new)

        lax.fori_loop(0, SLOT, forward, tuple(zero for _ in range(NSTATE)))

        def backward(i, carry):
            t = SLOT - 1 - i
            r = m * SLOT + t
            row = pl.ds(pl.multiple_of(r * SUBL, SUBL), SUBL)
            st = step_s[row, :]
            st2 = st * LOG2E
            gyt = gy_s[row, :]
            lb = zero
            gs = zero
            new = []
            for k in range(NSTATE):
                rate = rate_s[k * SUBL : (k + 1) * SUBL, :]
                dec = jnp.exp2(rate * st2)
                lam = bc_ref[r, NSTATE + k] * gyt + carry[k]
                ld = dec * lam
                new.append(ld)
                lams[lam_at(k, t), :] = lam
                lb = lb + bc_ref[r, k] * lam
                x = ld * hist[hist_at(k, t), :]
                gs = gs + rate * x
                at = slice(k * SUBL, (k + 1) * SUBL)
                galog_ref[at, :] = galog_ref[at, :] + st * x
            lb_s[row, :] = lb
            gs_s[row, :] = gs + unit_s[row, :] * lb
            return tuple(new)

        lax.fori_loop(0, SLOT, backward, tuple(zero for _ in range(NSTATE)))
        out = slice(m * SLOT, (m + 1) * SLOT)
        base = m * SLOT * SUBL

        lane = lax.broadcasted_iota(jnp.int32, (SLOT, LANES), 1)

        def reduce_state(k, acc):
            ab = jnp.zeros((SLOT, LANES), F32)
            ac = jnp.zeros((SLOT, LANES), F32)
            for j in range(SUBL):
                cols = slice(j * LANES, (j + 1) * LANES)
                lam = lams[pl.ds(k * SLOT * SUBL + j, SLOT, stride=SUBL), :]
                h = hist[pl.ds((k * span + 1) * SUBL + j, SLOT, stride=SUBL), :]
                sj = su_s[pl.ds(base + j, SLOT, stride=SUBL), :]
                gj = gy_s[pl.ds(base + j, SLOT, stride=SUBL), :]
                ab = ab + lam * sj
                ac = ac + h * gj
            sb = jnp.sum(ab, axis=1, keepdims=True)
            sc = jnp.sum(ac, axis=1, keepdims=True)
            return acc + jnp.where(lane == k, sb, 0.0) + jnp.where(lane == NSTATE + k, sc, 0.0)

        sums = lax.fori_loop(0, NSTATE, reduce_state, jnp.zeros((SLOT, LANES), F32))
        gproj_ref[out, DTR : DTR + LANES] = sums.astype(BF)
    galog_ref[...] = galog_ref[...] * rate_s[...]
    y = collect(y_s, rows) + skip_ref[...] * unit
    gz_ref[...] = (gg * y * sig * (1.0 + z * (1.0 - sig))).astype(BF)
    gunit_ref[...] = gy * skip_ref[...] + step * collect(lb_s, rows)
    gskip_ref[...] = jnp.sum(gy * unit, axis=0, keepdims=True)
    q = collect(gs_s, rows) * jax.nn.sigmoid(pre)
    gbias_ref[...] = jnp.sum(q, axis=0, keepdims=True)
    ql = q.astype(BF)
    gdt_ref[...] = mat_tn(proj_ref[:, :DTR], ql)
    gproj_ref[:, :DTR] = mat_nt(ql, w_dt_ref[...]).astype(BF)


def scan_backward(proj, bc, unit, gate, w_dt, dt_bias, d_skip, a_log, grad):
    rows = unit.shape[0]
    vm = pl.BlockSpec(memory_space=pltpu.VMEM)
    sm = pl.BlockSpec(memory_space=pltpu.SMEM)
    sds = jax.ShapeDtypeStruct
    flat = pltpu.VMEM((rows * SUBL, LANES), F32)
    return pl.pallas_call(
        functools.partial(adjoint_kernel, rows // SLOT),
        out_shape=(
            sds((rows, EI), BF),
            sds((rows, EI), F32),
            sds((rows, DTR + LANES), BF),
            sds((DTR, EI), F32),
            sds((1, EI), F32),
            sds((1, EI), F32),
            sds((NSTATE * SUBL, LANES), F32),
        ),
        in_specs=[vm, sm, vm, vm, vm, vm, vm, vm, vm],
        out_specs=(vm,) * 7,
        scratch_shapes=[flat] * 7
        + [
            pltpu.VMEM((NSTATE * SUBL, LANES), F32),
            pltpu.VMEM((NSTATE * (SLOT + 1) * SUBL, LANES), F32),
            pltpu.VMEM((NSTATE * SLOT * SUBL, LANES), F32),
        ],
        compiler_params=pltpu.CompilerParams(vmem_limit_bytes=60 << 20),
        name="scan_backward",
    )(proj, bc, unit, gate, w_dt, dt_bias, d_skip, a_log, grad)


def rope_tables(length, head_dim):
    half_dim = head_dim // 2
    freq_index = jnp.arange(half_dim, dtype=F32)
    inv_freq = jnp.exp(-math.log(ROPE_BASE) * 2.0 * freq_index / head_dim)
    angles = jnp.arange(length, dtype=F32)[:, None] * inv_freq[None, :]
    return (jnp.cos(angles)[None, :, None, :], jnp.sin(angles)[None, :, None, :])


def rope_apply(values, cosine, sine):
    half_dim = values.shape[-1] // 2
    a = values[..., :half_dim]
    b = values[..., half_dim:]
    return jnp.concatenate([a * cosine - b * sine, b * cosine + a * sine], axis=-1)


def rms_parts(v, g):
    s = lax.rsqrt(jnp.mean(v * v, axis=-1, keepdims=True) + EPS_NORM)
    return s, v * s


def rms_back(v, g, gh):
    s, nrm = rms_parts(v, g)
    gg = jnp.sum(gh * nrm, axis=0)
    gv = s * (gh * g - nrm * jnp.mean(gh * g * nrm, axis=-1, keepdims=True))
    return gv, gg


def total(partial_out):
    return sum_tensor(partial_out.astype(BF)).astype(F32)


def shift_down(v, by):
    if by == 0:
        return v
    return jnp.pad(v, ((0, 0), (by, 0), (0, 0)))[:, : v.shape[1]]


def shift_up(v, by):
    if by == 0:
        return v
    return jnp.pad(v, ((0, 0), (0, by), (0, 0)))[:, by:]


def attend(query, keys, values):
    scale = HEAD_DIM ** (-0.5)
    distance = jnp.arange(SLOT)[:, None] - jnp.arange(SLOT)[None, :]
    allowed = (distance >= 0) & (distance < WINDOW)
    scores = jnp.einsum("mqhd,mkhd->mhqk", query, keys, preferred_element_type=F32) * scale
    scores = jnp.where(allowed, scores, NEG_FILL)
    expo = jnp.exp(scores - jnp.max(scores, axis=-1, keepdims=True))
    return expo / jnp.sum(expo, axis=-1, keepdims=True)


def ffn_forward(h, w_gu, w_down):
    pre = mat_nn(h, w_gu)
    act = (silu(pre[:, :FI]) * pre[:, FI:]).astype(BF)
    return total(mat_nn(act, w_down)), pre, act


def ffn_backward(pre, w_gu, w_down, grad_low):
    gate = pre[:, :FI]
    up = pre[:, FI:]
    ga = mat_nt(grad_low, w_down)
    sig = jax.nn.sigmoid(gate)
    grad_gate = ga * up * sig * (1.0 + gate * (1.0 - sig))
    grad_up = ga * gate * sig
    gp = jnp.concatenate([grad_gate, grad_up], axis=1).astype(BF)
    return total(mat_nt(gp, w_gu)), gp


def layer(x, grad_out, w, small, gains, n):
    rows = x.shape[0]
    m = rows // SLOT
    hr = HW // HEAD_DIM
    cosine, sine = rope_tables(SLOT, HEAD_DIM)
    s1, n1 = rms_parts(x, gains[0])
    h1 = (n1 * gains[0]).astype(BF)
    mixed = mat_nn(h1, w["w_in"])
    mix_x = mixed[:, :EI].reshape(m, SLOT, EI)
    gate_z = mixed[:, EI:]
    conv_w = small["conv_w"].astype(F32)
    pre_conv = small["conv_b"].astype(F32)[None, None, :]
    for j in range(CONV):
        pre_conv = pre_conv + conv_w[j] * shift_down(mix_x, CONV - 1 - j)
    unit = silu(pre_conv).astype(BF).reshape(rows, EI)
    proj = sum_proj(mat_nn(unit, small["w_x"]).astype(BF))
    bc = proj[:, DTR:].astype(F32)
    scan_args = (
        proj[:, :DTR],
        bc,
        unit,
        gate_z,
        small["w_dt"],
        small["dt_bias"].astype(F32)[None],
        small["d_skip"].astype(F32)[None],
        small["a_log"].astype(F32).reshape(NSTATE * SUBL, LANES),
    )
    gated = scan_forward(*scan_args)
    x1 = x + total(mat_nn(gated, w["w_out"]))
    h2 = (rms_parts(x1, 0)[1] * gains[1]).astype(BF)
    branch, pre1, act1 = ffn_forward(h2, w["w_gu1"], w["w_down1"])
    x2 = x1 + branch
    h3 = (rms_parts(x2, 0)[1] * gains[2]).astype(BF)
    packed = mat_nn(h3, w["w_qkv"]).reshape(m, SLOT, 3, hr, HEAD_DIM)
    query = rope_apply(packed[:, :, 0], cosine, sine).astype(BF)
    keys = rope_apply(packed[:, :, 1], cosine, sine).astype(BF)
    values = packed[:, :, 2].astype(BF)
    probs = attend(query, keys, values)
    probs_low = probs.astype(BF)
    attended = jnp.einsum("mhqk,mkhd->mqhd", probs_low, values, preferred_element_type=F32)
    attended = attended.reshape(rows, HW).astype(BF)
    x3 = x2 + total(mat_nn(attended, w["w_o"]))
    h4 = (rms_parts(x3, 0)[1] * gains[3]).astype(BF)
    branch, pre2, act2 = ffn_forward(h4, w["w_gu2"], w["w_down2"])
    x4 = x3 + branch

    gb4 = grad_out.astype(BF)
    gh, gp2 = ffn_backward(pre2, w["w_gu2"], w["w_down2"], gb4)
    gv, gg4 = rms_back(x3, gains[3], gh)
    g3 = grad_out + gv
    gb3 = g3.astype(BF)
    gatt = mat_nt(gb3, w["w_o"]).astype(BF).reshape(m, SLOT, hr, HEAD_DIM)
    grad_p = jnp.einsum("mqhd,mkhd->mhqk", gatt, values, preferred_element_type=F32)
    inner = jnp.sum(probs * grad_p, axis=-1, keepdims=True)
    gs = (probs * (grad_p - inner)).astype(BF)
    scale = HEAD_DIM ** (-0.5)
    gq = jnp.einsum("mhqk,mkhd->mqhd", gs, keys, preferred_element_type=F32) * scale
    gk = jnp.einsum("mhqk,mqhd->mkhd", gs, query, preferred_element_type=F32) * scale
    gvv = jnp.einsum("mhqk,mqhd->mkhd", probs_low, gatt, preferred_element_type=F32)
    gpk = (
        jnp.stack([rope_apply(gq, cosine, -sine), rope_apply(gk, cosine, -sine), gvv], axis=2)
        .reshape(rows, 3 * HW)
        .astype(BF)
    )
    gv, gg3 = rms_back(x2, gains[2], total(mat_nt(gpk, w["w_qkv"])))
    g2 = g3 + gv
    gb2 = g2.astype(BF)
    gh, gp1 = ffn_backward(pre1, w["w_gu1"], w["w_down1"], gb2)
    gv, gg2 = rms_back(x1, gains[1], gh)
    g1 = g2 + gv
    gb1 = g1.astype(BF)
    ggated = mat_nt(gb1, w["w_out"])
    gz, gunit, gproj, g_dt, g_bias, g_skip, g_alog = scan_backward(*scan_args, ggated)
    gproj = sum_tensor(gproj)[:, : DTR + 2 * NSTATE]
    g_wx = mat_tn(unit, gproj)
    gu = gunit + mat_nt(gproj, small["w_x"])
    sig = jax.nn.sigmoid(pre_conv)
    gpre = gu.reshape(m, SLOT, EI) * sig * (1.0 + pre_conv * (1.0 - sig))
    g_conv_b = jnp.sum(gpre, axis=(0, 1))
    g_conv_w = jnp.stack(
        [jnp.sum(gpre * shift_down(mix_x, CONV - 1 - j), axis=(0, 1)) for j in range(CONV)]
    )
    gmx = sum(conv_w[j] * shift_up(gpre, CONV - 1 - j) for j in range(CONV))
    gmixed = jnp.concatenate([gmx.reshape(rows, EI).astype(BF), gz], axis=1)
    gv, gg1 = rms_back(x, gains[0], total(mat_nt(gmixed, w["w_in"])))
    g0 = g1 + gv

    left_t = jnp.concatenate([h1, gated, h2, act1, attended, h4, act2], axis=1).T
    rights = jnp.stack([gmixed, gb1, gp1, gb2, gb3, gp2, gb4])
    g_qkv = mat_tn(h3, gpk).astype(BF)
    g_qkv = change_rows(g_qkv, 0, D, D)
    start = lax.axis_index("tensor") * DG
    g_gain = lax.dynamic_slice_in_dim(jnp.stack([gg1, gg2, gg3, gg4]), start, DG, 1)
    pieces = [g_gain, g_conv_w, g_conv_b, g_bias, g_skip, g_alog, g_wx, g_dt]
    small_grads = jnp.concatenate([p.reshape(-1, LANES).astype(BF) for p in pieces])
    g0, small_grads, left_t = lax.optimization_barrier((g0, small_grads, left_t))
    return x4.astype(BF), g0, (left_t, rights, g_qkv), small_grads


def extents(n, shard_rows):
    slab = BIG_ROWS * LINES // n
    before = 0
    after = 0
    back_before = 0
    back_after = 0
    for d in range(n):
        lo, hi = slab * d, slab * (d + 1) - 1
        qs = [p + LEAD + (SMALL_ROWS if p >= FIRST else 0) - shard_rows * d for p in (lo, hi)]
        before = max(before, -qs[0])
        after = max(after, qs[1] + 1 - shard_rows)
    return before, after


def shift_perm(n, by):
    return [(i, i + by) for i in range(n) if 0 <= i + by < n]


def stack_kernel(n, shard_lines, before, per, top_ref, own_ref, bottom_ref, out_ref, hold, sem):
    d = lax.axis_index("dp")
    i = pl.program_id(0)
    steps = BIG_ROWS // n // per
    size = per * LINES

    def fetch(k, slot):
        row = d * (BIG_ROWS // n) + k * per
        a = row * LINES + LEAD + jnp.where(row >= FIRST // LINES, SMALL_ROWS, 0) - d * shard_lines
        high = a < 0
        low = a + size > shard_lines

        @pl.when(high)
        def _():
            pltpu.make_async_copy(top_ref.at[pl.ds(a + before, size), 0], hold.at[slot], sem.at[slot]).start()

        @pl.when(low)
        def _():
            pltpu.make_async_copy(
                bottom_ref.at[pl.ds(a + size - shard_lines, size), 0], hold.at[slot], sem.at[slot]
            ).start()

        @pl.when(jnp.logical_not(jnp.logical_or(high, low)))
        def _():
            pltpu.make_async_copy(own_ref.at[pl.ds(a, size), 0], hold.at[slot], sem.at[slot]).start()

    @pl.when(i == 0)
    def _():
        for k in range(min(3, steps)):
            fetch(k, k)

    @pl.when(i + 3 < steps)
    def _():
        fetch(i + 3, lax.rem(i + 3, 4))

    slot = lax.rem(i, 4)
    pltpu.make_async_copy(own_ref.at[pl.ds(0, size), 0], hold.at[slot], sem.at[slot]).wait()
    for j in range(LINES):
        out_ref[:, j * LANES : (j + 1) * LANES] = hold[slot, pl.ds(j, per, stride=LINES), :].astype(BF)


def stack_own(lines3, n):
    shard_lines = lines3.shape[0]
    before, after = extents(n, shard_lines)
    rows = BIG_ROWS // n
    per = 64 if rows % 64 == 0 else 32
    size = per * LINES
    nxt = lax.ppermute(lines3[:after], "dp", shift_perm(n, -1))
    prv = lax.ppermute(lines3[shard_lines - before :], "dp", shift_perm(n, 1))
    top = jnp.concatenate([prv, lines3[:size]])
    bottom = jnp.concatenate([lines3[shard_lines - size :], nxt])
    hbm = pl.BlockSpec(memory_space=pl.ANY)
    return pl.pallas_call(
        functools.partial(stack_kernel, n, shard_lines, before, per),
        grid=(rows // per,),
        out_shape=jax.ShapeDtypeStruct((rows, D), BF),
        in_specs=[hbm] * 3,
        out_specs=pl.BlockSpec((per, D), lambda i: (i, 0)),
        scratch_shapes=[pltpu.VMEM((4, size, LANES), F32), pltpu.SemaphoreType.DMA((4,))],
        compiler_params=pltpu.CompilerParams(vmem_limit_bytes=24 << 20),
        name="stack_own",
    )(top, lines3, bottom)


def low_kernel(x_ref, out_ref):
    out_ref[...] = x_ref[:, 0, :].astype(BF)


def to_low(value):
    vm = pl.BlockSpec(memory_space=pltpu.VMEM)
    return pl.pallas_call(
        low_kernel,
        out_shape=jax.ShapeDtypeStruct((value.shape[0], LANES), BF),
        in_specs=[vm],
        out_specs=vm,
        name="to_low",
    )(value)


def window(values, shift, size):
    length = values.shape[0]
    s = jnp.clip(shift, 0, length - size)
    got = lax.dynamic_slice_in_dim(values, s, size, 0)
    room = jnp.zeros((3 * size,) + values.shape[1:], values.dtype)
    room = lax.dynamic_update_slice_in_dim(room, got, size + jnp.clip(s - shift, -size, size), 0)
    return room[size : 2 * size]


STRIP = 8192


def lone_group(groups, bounds_ref, start, stop):
    def look(g, found):
        holds = jnp.logical_and(bounds_ref[2 * g] <= start, bounds_ref[2 * g + 1] >= stop)
        return jnp.where(holds, g, found)

    return lax.fori_loop(0, groups, look, jnp.int32(-1))


def moments_kernel(groups, shard, bounds_ref, grad_ref, w_ref, one_ref, two_ref,
                   first_ref, second_ref, grad_out, sums_ref, hold):
    i = pl.program_id(0)
    size = CHUNK * LANES
    lanes = STRIP // 8

    @pl.when(i == 0)
    def _():
        @pl.loop(0, 2 * groups)
        def _(g):
            sums_ref[g] = 0.0

    def strip(k, carry):
        here = pl.ds(pl.multiple_of(k * STRIP, STRIP), STRIP)
        grad = grad_ref[:, here]
        w = w_ref[:, here]
        first = BETA_ONE * one_ref[:, here] + (1.0 - BETA_ONE) * grad
        second = BETA_TWO * two_ref[:, here] + (1.0 - BETA_TWO) * grad * grad
        ratio = first / (jnp.sqrt(second) + ADAM_EPS) + DECAY_W * w
        first_ref[:, here] = first
        second_ref[:, here] = second
        grad_out[:, here] = grad
        hold[:, here] = ratio
        wsq, rsq = carry
        for j in range(8):
            part = slice(j * lanes, (j + 1) * lanes)
            wsq = wsq + w[:, part] * w[:, part]
            rsq = rsq + ratio[:, part] * ratio[:, part]
        return wsq, rsq

    zero = jnp.zeros((1, lanes), F32)
    wsq, rsq = lax.fori_loop(0, size // STRIP, strip, (zero, zero))
    d = lax.axis_index("dp")
    start = d * shard + i * size
    limit = (d + 1) * shard
    alone = lone_group(groups, bounds_ref, start, start + size)
    alone = jnp.where(start + size <= limit, alone, -1)

    @pl.when(alone >= 0)
    def _():
        sums_ref[2 * alone] = sums_ref[2 * alone] + jnp.sum(wsq)
        sums_ref[2 * alone + 1] = sums_ref[2 * alone + 1] + jnp.sum(rsq)

    @pl.when(alone < 0)
    def _():
        @pl.loop(0, groups)
        def _(g):
            low = jnp.maximum(bounds_ref[2 * g], start)
            high = jnp.minimum(bounds_ref[2 * g + 1], jnp.minimum(start + size, limit))

            @pl.when(low < high)
            def _():
                def masked(k, carry):
                    at = pl.multiple_of(k * lanes, lanes)
                    here = pl.ds(at, lanes)
                    index = start + at + lax.broadcasted_iota(jnp.int32, (1, lanes), 1)
                    inside = (index >= low) & (index < high)
                    wv = w_ref[:, here]
                    rv = hold[:, here]
                    return (
                        carry[0] + jnp.where(inside, wv * wv, 0.0),
                        carry[1] + jnp.where(inside, rv * rv, 0.0),
                    )

                k0 = (low - start) // lanes
                k1 = (high - start + lanes - 1) // lanes
                wv, rv = lax.fori_loop(k0, k1, masked, (zero, zero))
                sums_ref[2 * g] = sums_ref[2 * g] + jnp.sum(wv)
                sums_ref[2 * g + 1] = sums_ref[2 * g + 1] + jnp.sum(rv)


def moments(bounds, lines, master, one, two):
    shard = master.shape[1]
    size = CHUNK * LANES
    groups = bounds.shape[0] // 2
    block = pl.BlockSpec((1, size), lambda i: (0, i))
    ahead = SLACK // CHUNK
    flat = jax.ShapeDtypeStruct((1, shard), F32)
    smem = pl.BlockSpec(memory_space=pltpu.SMEM)
    return pl.pallas_call(
        functools.partial(moments_kernel, groups, shard),
        grid=(pl.cdiv(shard, size),),
        out_shape=(flat, flat, flat, jax.ShapeDtypeStruct((2 * groups,), F32)),
        in_specs=[smem, pl.BlockSpec((1, size), lambda i: (0, i + ahead)), block, block, block],
        out_specs=(block, block, block, smem),
        scratch_shapes=[pltpu.VMEM((1, size), F32)],
        compiler_params=pltpu.CompilerParams(vmem_limit_bytes=40 << 20),
        name="moments",
    )(bounds, lines.reshape(1, -1), master, one, two)


def update_kernel(groups, shard, bounds_ref, trust_ref, w_ref, first_ref, second_ref, new_ref, low_ref, hold):
    i = pl.program_id(0)
    size = CHUNK * LANES
    lanes = STRIP // 8
    start = lax.axis_index("dp") * shard + i * size
    alone = lone_group(groups, bounds_ref, start, start + size)

    def step(trust_of):
        @pl.loop(0, size // STRIP)
        def _(k):
            here = pl.ds(pl.multiple_of(k * STRIP, STRIP), STRIP)
            w = w_ref[:, here]
            ratio = first_ref[:, here] / (jnp.sqrt(second_ref[:, here]) + ADAM_EPS) + DECAY_W * w
            new = w - LEARN_RATE * trust_of(here) * ratio
            new_ref[:, here] = new
            low_ref[:, here] = new.astype(BF)

    @pl.when(alone >= 0)
    def _():
        trust = trust_ref[jnp.maximum(alone, 0)]
        step(lambda here: trust)

    @pl.when(alone < 0)
    def _():
        hold[...] = jnp.zeros_like(hold)

        @pl.loop(0, groups)
        def _(g):
            low = jnp.maximum(bounds_ref[2 * g], start)
            high = jnp.minimum(bounds_ref[2 * g + 1], start + size)

            @pl.when(low < high)
            def _():
                @pl.loop((low - start) // lanes, (high - start + lanes - 1) // lanes)
                def _(k):
                    at = pl.multiple_of(k * lanes, lanes)
                    here = pl.ds(at, lanes)
                    index = start + at + lax.broadcasted_iota(jnp.int32, (1, lanes), 1)
                    hold[:, here] = jnp.where((index >= low) & (index < high), trust_ref[g], hold[:, here])

        step(lambda here: hold[:, here])


def update(bounds, trust, master, first, second):
    shard = master.shape[1]
    size = CHUNK * LANES
    groups = bounds.shape[0] // 2
    block = pl.BlockSpec((1, size), lambda i: (0, i))
    smem = pl.BlockSpec(memory_space=pltpu.SMEM)
    return pl.pallas_call(
        functools.partial(update_kernel, groups, shard),
        grid=(pl.cdiv(shard, size),),
        out_shape=(jax.ShapeDtypeStruct((1, shard), F32), jax.ShapeDtypeStruct((1, shard), BF)),
        in_specs=[smem, smem, block, block, block],
        out_specs=(block, block),
        scratch_shapes=[pltpu.VMEM((1, size), F32)],
        compiler_params=pltpu.CompilerParams(vmem_limit_bytes=40 << 20),
        name="update",
    )(bounds, trust, master, first, second)


def norms_kernel(n, m, own_ref, out_ref, across, along, part, ssem, rsem, ssem2, rsem2):
    d = lax.axis_index("dp")
    t = lax.axis_index("tensor")
    barrier = pltpu.get_barrier_semaphore()
    for k in range(1, m):
        pl.semaphore_signal(barrier, inc=1, device_id=(d, lax.rem(t + k, m)), device_id_type=MESH)

    @pl.loop(1, n)
    def _(k):
        pl.semaphore_signal(barrier, inc=1, device_id=(lax.rem(d + k, n), t), device_id_type=MESH)

    pl.semaphore_wait(barrier, n + m - 2)

    def over_tensor(k):
        return pltpu.make_async_remote_copy(
            src_ref=own_ref,
            dst_ref=across.at[k - 1],
            send_sem=ssem.at[k - 1],
            recv_sem=rsem.at[k - 1],
            device_id=(d, lax.rem(t + k, m)),
            device_id_type=MESH,
        )

    def over_dp(k):
        return pltpu.make_async_remote_copy(
            src_ref=part,
            dst_ref=along.at[k - 1],
            send_sem=ssem2.at[k - 1],
            recv_sem=rsem2.at[k - 1],
            device_id=(lax.rem(d + k, n), t),
            device_id_type=MESH,
        )

    for k in range(1, m):
        over_tensor(k).start()
    total_ = own_ref[...]
    for k in range(1, m):
        over_tensor(k).wait_recv()
    for k in range(1, m):
        total_ = total_ + across[k - 1]
    part[...] = total_

    @pl.loop(1, n)
    def _(k):
        over_dp(k).start()

    @pl.loop(1, n)
    def _(k):
        over_dp(k).wait_recv()

    def add(k, acc):
        return acc + along[k - 1]

    out_ref[...] = lax.fori_loop(1, n, add, part[...])
    for k in range(1, m):
        over_tensor(k).wait_send()

    @pl.loop(1, n)
    def _(k):
        over_dp(k).wait_send()


def sum_everywhere(values, n, m):
    vm = pl.BlockSpec(memory_space=pltpu.VMEM)
    dma = pltpu.SemaphoreType.DMA
    tile = pltpu.VMEM((8, LANES), F32)
    return pl.pallas_call(
        functools.partial(norms_kernel, n, m),
        out_shape=jax.ShapeDtypeStruct((8, LANES), F32),
        in_specs=[vm],
        out_specs=vm,
        scratch_shapes=[
            pltpu.VMEM((m - 1, 8, LANES), F32),
            pltpu.VMEM((n - 1, 8, LANES), F32),
            tile,
            dma((m - 1,)),
            dma((m - 1,)),
            dma((n - 1,)),
            dma((n - 1,)),
        ],
        compiler_params=pltpu.CompilerParams(collective_id=2, has_side_effects=True),
        name="sum_everywhere",
    )(values)


def per_device(n, m, tokens, cotangent, lengths, master, moment_one, moment_two):
    d = lax.axis_index("dp")
    shard = master.shape[1]
    lines = shard // LANES
    lines3 = master.reshape(lines, 1, LANES)
    base = d * lines
    mid = LEAD + FIRST
    small_own = jnp.concatenate(
        [window(lines3, -base, GAIN_ROWS), window(lines3, mid - base, SMALL_ROWS)]
    )
    small_flat = lax.psum(to_low(small_own), "dp")
    weights = ring_gather(stack_own(lines3, n), n)
    weights, small_flat = lax.optimization_barrier((weights, small_flat))
    gains = lax.all_gather(small_flat[:GAIN_ROWS].reshape(4, DG), "tensor", axis=1, tiled=True)
    gains = gains.astype(F32)
    small = {}
    at = GAIN_ROWS
    for name, shape in SMALL:
        count = math.prod(shape) // LANES
        small[name] = small_flat[at : at + count].reshape(shape)
        at += count
    w = {}
    for name, rows in BIG:
        w[name] = weights[BIG_OFF[name] : BIG_OFF[name] + rows]
    w["w_qkv"] = change_rows(weights, BIG_OFF["w_qkv"], dict(BIG)["w_qkv"], 3 * HW)
    x = tokens.astype(F32)
    pos = lax.broadcasted_iota(jnp.int32, (tokens.shape[0] // SLOT, SLOT), 1)
    valid = (pos < lengths[:, None]).astype(F32).reshape(-1, 1)
    grad = cotangent.astype(F32) * valid
    out, grad_in, operands, small_grads = layer(x, grad, w, small, gains, n)
    small_sum = lax.psum(small_grads, "dp")
    laid = ring_reduce(*operands, n, lines)
    laid, small_sum = lax.optimization_barrier((laid, small_sum))
    small_sum = small_sum.astype(F32).reshape(-1, 1, LANES)

    before, after = extents(n, lines)
    slab_lines = BIG_ROWS * LINES // n

    def local(row):
        return row * LINES + LEAD + jnp.where(row >= FIRST // LINES, SMALL_ROWS, 0) - base

    begin = local(d * (BIG_ROWS // n))
    close = local((d + 1) * (BIG_ROWS // n) - 1) + LINES
    tail, head, laid = lax.optimization_barrier(
        (laid[SLACK + lines : SLACK + lines + after], laid[SLACK - before : SLACK], laid)
    )
    from_prev = lax.ppermute(tail, "dp", shift_perm(n, 1))
    from_next = lax.ppermute(head, "dp", shift_perm(n, -1))
    line = lax.broadcasted_iota(jnp.int32, (after, 1, 1), 0)
    top = jnp.where(line < begin, from_prev, laid[SLACK : SLACK + after])
    line = lax.broadcasted_iota(jnp.int32, (before, 1, 1), 0) + (lines - before)
    bottom = jnp.where(line >= close, from_next, laid[SLACK + lines - before : SLACK + lines])
    laid = laid.at[SLACK : SLACK + after].set(top)
    laid = laid.at[SLACK + lines - before : SLACK + lines].set(bottom)

    def place(laid, values, at):
        count = values.shape[0]
        return lax.dynamic_update_slice_in_dim(laid, values, SLACK + jnp.clip(at - base, -count, lines), 0)

    laid = place(laid, small_sum[GAIN_ROWS:], mid)
    laid = place(laid, small_sum[:GAIN_ROWS], 0)
    used = LEAD + SMALL_ROWS + BIG_ROWS * LINES
    rest = lines * n - used
    if rest:
        laid = place(laid, jnp.zeros((rest, 1, LANES), F32), used)

    bounds = jnp.asarray([v for pair in group_bounds() for v in pair], jnp.int32)
    first, second, grad_shard, sums = moments(bounds, laid, master, moment_one, moment_two)
    count = sums.shape[0]
    tile = jnp.pad(sums, (0, 8 * LANES - count)).reshape(8, LANES)
    squares = sum_everywhere(tile, n, m).reshape(-1)[:count].reshape(-1, 2)
    trust = jnp.sqrt(squares[:, 0] + TRUST_EPSILON) * lax.rsqrt(squares[:, 1] + TRUST_EPSILON)
    master_new, low = update(bounds, trust, master, first, second)
    return (out, grad_in, master_new, first, second, low, grad_shard, jnp.sqrt(squares))


def solution(mesh):
    row = P("dp", None)
    flat = P("tensor", "dp")
    return jax.shard_map(
        functools.partial(per_device, mesh.shape["dp"], mesh.shape["tensor"]),
        mesh=mesh,
        in_specs=(row, row, P("dp"), flat, flat, flat),
        out_specs=(row, row, flat, flat, flat, flat, flat, P()),
        check_vma=False,
    )
```

```python
import functools
import math

import jax
import jax.numpy as jnp
from jax import lax
from jax.experimental import pallas as pl
from jax.experimental.pallas import tpu as pltpu
from jax.sharding import PartitionSpec as P

D = 2048
INNER = 4096
NSTATE = 16
DTR = 128
HEADS = 32
HEAD_DIM = 64
FF = 4096
CONV = 4
WINDOW = 2048
SLOT = 128
LANES = 128

EPS_NORM = 1e-05
TRUST_EPSILON = 1e-06
ROPE_BASE = 10000.0
BETA_ONE = 0.5
BETA_TWO = 0.55
ADAM_EPS = 1e-06
DECAY_W = 0.01
LEARN_RATE = 0.2
NEG_FILL = -1e30
LOG2E = 1.4426950408889634
MESH = pl.DeviceIdType.MESH
BF = jnp.bfloat16
F32 = jnp.float32

EI = INNER // 4
FI = FF // 4
HW = HEADS * HEAD_DIM // 4
DG = D // 4

SMALL = [
    ("conv_w", (CONV, EI)),
    ("conv_b", (EI,)),
    ("dt_bias", (EI,)),
    ("d_skip", (EI,)),
    ("a_log", (NSTATE, EI)),
    ("w_x", (EI, DTR + 2 * NSTATE)),
    ("w_dt", (DTR, EI)),
]
SMALL_ROWS = sum(math.prod(s) for _, s in SMALL) // LANES
GAIN_ROWS = 4 * DG // LANES
BIG = [
    ("w_in", D),
    ("w_out", EI),
    ("w_gu1", D),
    ("w_down1", FI),
    ("w_qkv", D * 3 * HW // D),
    ("w_o", HW),
    ("w_gu2", D),
    ("w_down2", FI),
]
BIG_OFF = {}
_at = 0
for _name, _rows in BIG:
    BIG_OFF[_name] = _at
    _at += _rows
BIG_ROWS = _at
LINES = D // LANES
FIRST = BIG_OFF["w_out"] * LINES
LEAD = GAIN_ROWS
CHUNK = 1024
SLACK = -(-(SMALL_ROWS + GAIN_ROWS) // CHUNK) * CHUNK


def group_bounds():
    bounds = []
    for k in range(4):
        bounds.append((k * DG, (k + 1) * DG))
    at = 4 * DG
    entries = [("w_in", D * 2 * EI)]
    entries += [(name, math.prod(shape)) for name, shape in SMALL]
    entries += [
        ("w_out", EI * D),
        ("w_gu1", D * 2 * FI),
        ("w_down1", FI * D),
        ("w_qkv", D * 3 * HW),
        ("w_o", HW * D),
        ("w_gu2", D * 2 * FI),
        ("w_down2", FI * D),
    ]
    for _, count in entries:
        bounds.append((at, at + count))
        at += count
    return bounds


def silu(v):
    return v * jax.nn.sigmoid(v)


def softplus(v):
    return jnp.maximum(v, 0.0) + jnp.log1p(jnp.exp(-jnp.abs(v)))


def mat_nn(a, b):
    return jnp.dot(a, b, preferred_element_type=F32)


def mat_tn(a, b):
    return lax.dot_general(a, b, (((0,), (0,)), ((), ())), preferred_element_type=F32)


def mat_nt(a, b):
    return lax.dot_general(a, b, (((1,), (1,)), ((), ())), preferred_element_type=F32)


def ring_pos(d, n):
    return jnp.where(lax.rem(d, 2) == 0, lax.div(d, 2), n - 1 - lax.div(d, 2))


def ring_dev(p, n):
    return jnp.where(p < n // 2, 2 * p, 2 * (n - 1 - p) + 1)


def ring_neighbours(n):
    d = lax.axis_index("dp")
    p = ring_pos(d, n)
    right = ring_dev(lax.rem(p + 1, n), n)
    left = ring_dev(lax.rem(p + n - 1, n), n)
    return d, p, right, left


def ring_barrier(left, right, t):
    barrier = pltpu.get_barrier_semaphore()
    for nb in (left, right):
        pl.semaphore_signal(barrier, inc=1, device_id=(nb, t), device_id_type=MESH)
    pl.semaphore_wait(barrier, 2)


def gather_kernel(n, subs, own_ref, out_ref, hold, local_sem, ssem, rsem):
    t = lax.axis_index("tensor")
    d, p, right, left = ring_neighbours(n)
    rows = own_ref.shape[0]
    half = rows // 2
    sub = half // subs
    fetch = pltpu.make_async_copy(own_ref, hold, local_sem.at[0])
    fetch.start()
    ring_barrier(left, right, t)

    def copy(way, step, c, from_own):
        target = right if way == 0 else left
        owner = ring_dev(lax.rem(p + (n - step if way == 0 else step), n), n)
        at = pl.multiple_of(owner * rows + way * half + c * sub, 8)
        src = own_ref.at[pl.ds(way * half + c * sub, sub)] if from_own else out_ref.at[pl.ds(at, sub)]
        return pltpu.make_async_remote_copy(
            src_ref=src,
            dst_ref=out_ref.at[pl.ds(at, sub)],
            send_sem=ssem.at[way, step, c],
            recv_sem=rsem.at[way, step, c],
            device_id=(target, t),
            device_id_type=MESH,
        )

    for c in range(subs):
        for way in (0, 1):
            copy(way, 0, c, True).start()
    fetch.wait()
    store = pltpu.make_async_copy(
        hold, out_ref.at[pl.ds(pl.multiple_of(d * rows, 8), rows)], local_sem.at[1]
    )
    store.start()
    for step in range(1, n - 1):
        for c in range(subs):
            for way in (0, 1):
                copy(way, step - 1, c, step == 1).wait_recv()
                copy(way, step, c, False).start()
    for c in range(subs):
        for way in (0, 1):
            copy(way, n - 2, c, n == 2).wait_recv()
    store.wait()
    for step in range(n - 1):
        for c in range(subs):
            for way in (0, 1):
                copy(way, step, c, step == 0).wait_send()


def ring_gather(own, n):
    rows, cols = own.shape
    subs = 2
    return pl.pallas_call(
        functools.partial(gather_kernel, n, subs),
        out_shape=jax.ShapeDtypeStruct((n * rows, cols), own.dtype),
        in_specs=[pl.BlockSpec(memory_space=pl.ANY)],
        out_specs=pl.BlockSpec(memory_space=pl.ANY),
        scratch_shapes=[
            pltpu.VMEM((rows, cols), own.dtype),
            pltpu.SemaphoreType.DMA((2,)),
            pltpu.SemaphoreType.DMA((2, n - 1, subs)),
            pltpu.SemaphoreType.DMA((2, n - 1, subs)),
        ],
        cost_estimate=pl.CostEstimate(flops=10**9, bytes_accessed=1500 * 10**6, transcendentals=0),
        compiler_params=pltpu.CompilerParams(
            collective_id=0, has_side_effects=True, vmem_limit_bytes=32 << 20
        ),
        name="ring_gather",
    )(own)


def piece_of(half):
    for size in (64, 32, 16):
        if half % size == 0:
            return size


def reduce_kernel(n, shard_lines, left_ref, right_refs, qkv_ref, out_ref, slots, lines, ssem, rsem, out_sem):
    t = lax.axis_index("tensor")
    d, p, right, left = ring_neighbours(n)
    rows = BIG_ROWS // n
    half = rows // 2
    SUB = piece_of(half)
    subs = half // SUB
    ring_barrier(left, right, t)
    qkv_at = BIG_OFF["w_qkv"]
    qkv_rows = dict(BIG)["w_qkv"]

    def own_into(at, put):
        in_qkv = jnp.logical_and(at >= qkv_at, at < qkv_at + qkv_rows)
        which = jnp.int32(0)
        for name, _ in BIG[1:]:
            if name != "w_qkv":
                which = which + jnp.where(at >= BIG_OFF[name], 1, 0)

        @pl.when(in_qkv)
        def _():
            put(qkv_ref[pl.ds(pl.multiple_of(at - qkv_at, SUB), SUB), :].astype(F32))

        @pl.when(jnp.logical_not(in_qkv))
        def _():
            row = jnp.where(at >= qkv_at + qkv_rows, at - qkv_rows, at)
            lt = left_ref[pl.ds(pl.multiple_of(row, SUB), SUB), :]
            put(jnp.dot(lt, right_refs[which], preferred_element_type=F32))

    def owner_of(way, step):
        return ring_dev(lax.rem(p + (n - 1 - step if way == 0 else 1 + step), n), n)

    def copy(way, step, c):
        target = right if way == 0 else left
        return pltpu.make_async_remote_copy(
            src_ref=slots.at[way, step, pl.ds(pl.multiple_of(c * SUB, SUB), SUB)],
            dst_ref=slots.at[way, step + 1, pl.ds(pl.multiple_of(c * SUB, SUB), SUB)],
            send_sem=ssem.at[way, step, c],
            recv_sem=rsem.at[way, step, c],
            device_id=(target, t),
            device_id_type=MESH,
        )

    def run(step):
        @pl.loop(0, subs)
        def _(c):
            here = pl.ds(pl.multiple_of(c * SUB, SUB), SUB)
            for way in (0, 1):
                at = owner_of(way, step) * rows + way * half + c * SUB
                if step > 0:
                    copy(way, step - 1, c).wait_recv()

                def put(value):
                    if step > 0:
                        value = value + slots[way, step, here, :].astype(F32)
                    if step < n - 1:
                        slots[way, step, here, :] = value.astype(BF)
                    else:
                        for j in range(LINES):
                            lines[way, pl.ds(j, SUB, stride=LINES), :] = value[:, j * LANES : (j + 1) * LANES]

                if step == n - 1:

                    @pl.when(c > 0)
                    def _():
                        leave(way, c - 1).wait()

                own_into(at, put)
                if step < n - 1:
                    copy(way, step, c).start()
                else:
                    leave(way, c).start()

    def leave(way, c):
        row = d * rows + way * half + c * SUB
        to = row * LINES + LEAD + jnp.where(row >= FIRST // LINES, SMALL_ROWS, 0) - d * shard_lines + SLACK
        return pltpu.make_async_copy(
            lines.at[way], out_ref.at[pl.ds(to, SUB * LINES), 0], out_sem.at[way]
        )

    for step in range(n):
        run(step)
    for way in (0, 1):
        leave(way, subs - 1).wait()

    @pl.loop(0, subs)
    def _(c):
        for way in (0, 1):
            for step in range(n - 1):
                copy(way, step, c).wait_send()


def ring_reduce(left_t, rights, qkv_grad, n, shard_lines):
    rows = BIG_ROWS // n
    sub = piece_of(rows // 2)
    subs = rows // 2 // sub
    vm = pl.BlockSpec(memory_space=pltpu.VMEM)
    return pl.pallas_call(
        functools.partial(reduce_kernel, n, shard_lines),
        out_shape=jax.ShapeDtypeStruct((shard_lines + 2 * SLACK, 1, LANES), F32),
        in_specs=[vm, vm, vm],
        out_specs=pl.BlockSpec(memory_space=pl.ANY),
        scratch_shapes=[
            pltpu.VMEM((2, n, rows // 2, D), BF),
            pltpu.VMEM((2, sub * LINES, LANES), F32),
            pltpu.SemaphoreType.DMA((2, n - 1, subs)),
            pltpu.SemaphoreType.DMA((2, n - 1, subs)),
            pltpu.SemaphoreType.DMA((2,)),
        ],
        cost_estimate=pl.CostEstimate(flops=10**9, bytes_accessed=1500 * 10**6, transcendentals=0),
        compiler_params=pltpu.CompilerParams(
            collective_id=1, has_side_effects=True, vmem_limit_bytes=67043328
        ),
        name="ring_reduce",
    )(left_t, rights, qkv_grad)


def pair_kernel(parts, x_ref, out_ref, from_mate, chip, from_far, s1, r1, s2, r2, s3, r3):
    d = lax.axis_index("dp")
    t = lax.axis_index("tensor")
    core = lax.rem(t, 2)
    mate = t + 1 - 2 * core
    far = lax.rem(t + 2, 4)
    half = x_ref.shape[0] // 2
    q = half // parts
    barrier = pltpu.get_barrier_semaphore()
    for peer in (mate, far):
        pl.semaphore_signal(barrier, inc=1, device_id=(d, peer), device_id_type=MESH)
    pl.semaphore_wait(barrier, 2)

    def mine(k):
        return pl.ds(pl.multiple_of(core * half + k * q, 16), q)

    def theirs(k):
        return pl.ds(pl.multiple_of((1 - core) * half + k * q, 16), q)

    def send(src, dst, ssem, rsem, k, peer):
        return pltpu.make_async_remote_copy(
            src_ref=src,
            dst_ref=dst,
            send_sem=ssem.at[k],
            recv_sem=rsem.at[k],
            device_id=(d, peer),
            device_id_type=MESH,
        )

    def one(k):
        here = pl.ds(k * q, q)
        return send(x_ref.at[theirs(k)], from_mate.at[here], s1, r1, k, mate)

    def two(k):
        here = pl.ds(k * q, q)
        return send(chip.at[here], from_far.at[here], s2, r2, k, far)

    def three(k):
        return send(out_ref.at[mine(k)], out_ref.at[mine(k)], s3, r3, k, mate)

    for k in range(parts):
        one(k).start()
    for k in range(parts):
        here = slice(k * q, (k + 1) * q)
        one(k).wait_recv()
        chip[here, :] = (x_ref[mine(k), :].astype(F32) + from_mate[here, :].astype(F32)).astype(BF)
        two(k).start()
    for k in range(parts):
        here = slice(k * q, (k + 1) * q)
        two(k).wait_recv()
        out_ref[mine(k), :] = (chip[here, :].astype(F32) + from_far[here, :].astype(F32)).astype(BF)
        three(k).start()
    for k in range(parts):
        three(k).wait_recv()
    for k in range(parts):
        one(k).wait_send()
        two(k).wait_send()
        three(k).wait_send()


def sum_tensor(value):
    rows, cols = value.shape
    parts = 8 if cols >= 1024 else 1
    vm = pl.BlockSpec(memory_space=pltpu.VMEM)
    dma = pltpu.SemaphoreType.DMA
    part = pltpu.VMEM((rows // 2, cols), BF)
    return pl.pallas_call(
        functools.partial(pair_kernel, parts),
        out_shape=jax.ShapeDtypeStruct((rows, cols), BF),
        in_specs=[vm],
        out_specs=vm,
        scratch_shapes=[part, part, part] + [dma((parts,))] * 6,
        compiler_params=pltpu.CompilerParams(
            collective_id=3 if cols >= 1024 else 4, has_side_effects=True
        ),
        name="sum_tensor",
    )(value)


def sum_proj(value):
    cols = value.shape[1]
    padded = jnp.pad(value, ((0, 0), (0, -cols % LANES)))
    return sum_tensor(padded)[:, :cols]


def rows_kernel(src, dst, src_ref, out_ref, inn, out):
    wide = src_ref.shape[1] // LANES
    thin = out_ref.shape[1] // LANES
    groups = src_ref.shape[0] // src
    for b in range(wide):
        inn[b] = src_ref[:, b * LANES : (b + 1) * LANES].astype(F32)
    for q in range(src * wide):
        a, b = divmod(q, wide)
        j, c = divmod(q, thin)
        out[c, pl.ds(j, groups, stride=dst), :] = inn[b, pl.ds(a, groups, stride=src), :]
    for c in range(thin):
        out_ref[:, c * LANES : (c + 1) * LANES] = out[c].astype(BF)


def change_rows(value, start, count, width):
    cols = value.shape[1]
    unit = math.gcd(cols, width)
    src, dst = width // unit, cols // unit
    block = 32 * src
    first = start // block
    return pl.pallas_call(
        functools.partial(rows_kernel, src, dst),
        grid=(count // block,),
        out_shape=jax.ShapeDtypeStruct((count * cols // width, width), BF),
        in_specs=[pl.BlockSpec((block, cols), lambda i: (i + first, 0))],
        out_specs=pl.BlockSpec((32 * dst, width), lambda i: (i, 0)),
        scratch_shapes=[
            pltpu.VMEM((cols // LANES, block, LANES), F32),
            pltpu.VMEM((width // LANES, 32 * dst, LANES), F32),
        ],
        compiler_params=pltpu.CompilerParams(vmem_limit_bytes=24 << 20),
        name="change_rows",
    )(value)


def spread(ref, value):
    rows = value.shape[0]
    for j in range(EI // LANES):
        ref[pl.ds(j, rows, stride=EI // LANES), :] = value[:, j * LANES : (j + 1) * LANES]


def collect(ref, rows):
    return jnp.concatenate(
        [ref[pl.ds(j, rows, stride=EI // LANES), :] for j in range(EI // LANES)], axis=1
    )


SUBL = EI // LANES


def scan_kernel(slots, proj_ref, bc_ref, unit_ref, gate_ref, w_dt_ref, bias_ref, skip_ref, alog_ref,
                gated_ref, step_s, su_s, y_s, rate_s):
    pre = jnp.dot(proj_ref[:, :DTR], w_dt_ref[...], preferred_element_type=F32) + bias_ref[...]
    step = softplus(pre)
    unit = unit_ref[...].astype(F32)
    spread(step_s, step)
    spread(su_s, step * unit)
    rate_s[...] = -jnp.exp(alog_ref[...]) * LOG2E

    def body(t, states):
        new = []
        for m in range(slots):
            r = m * SLOT + t
            row = pl.ds(pl.multiple_of(r * SUBL, SUBL), SUBL)
            st = step_s[row, :]
            su = su_s[row, :]
            y = jnp.zeros((SUBL, LANES), F32)
            for k in range(NSTATE):
                dec = jnp.exp2(rate_s[k * SUBL : (k + 1) * SUBL, :] * st)
                s = dec * states[m * NSTATE + k] + bc_ref[r, k] * su
                y = y + bc_ref[r, NSTATE + k] * s
                new.append(s)
            y_s[row, :] = y
        return tuple(new)

    init = tuple(jnp.zeros((SUBL, LANES), F32) for _ in range(slots * NSTATE))
    lax.fori_loop(0, SLOT, body, init)
    y = collect(y_s, slots * SLOT) + skip_ref[...] * unit
    z = gate_ref[...]
    gated_ref[...] = (y * silu(z)).astype(BF)


def scan_forward(proj, bc, unit, gate, w_dt, dt_bias, d_skip, a_log):
    rows = unit.shape[0]
    vm = pl.BlockSpec(memory_space=pltpu.VMEM)
    sm = pl.BlockSpec(memory_space=pltpu.SMEM)
    return pl.pallas_call(
        functools.partial(scan_kernel, rows // SLOT),
        out_shape=jax.ShapeDtypeStruct((rows, EI), BF),
        in_specs=[vm, sm, vm, vm, vm, vm, vm, vm],
        out_specs=vm,
        scratch_shapes=[
            pltpu.VMEM((rows * SUBL, LANES), F32),
            pltpu.VMEM((rows * SUBL, LANES), F32),
            pltpu.VMEM((rows * SUBL, LANES), F32),
            pltpu.VMEM((NSTATE * SUBL, LANES), F32),
        ],
        compiler_params=pltpu.CompilerParams(vmem_limit_bytes=60 << 20),
        name="scan_forward",
    )(proj, bc, unit, gate, w_dt, dt_bias, d_skip, a_log)


def adjoint_kernel(slots, proj_ref, bc_ref, unit_ref, gate_ref, w_dt_ref, bias_ref, skip_ref, alog_ref,
                   grad_ref, gz_ref, gunit_ref, gproj_ref, gdt_ref, gbias_ref, gskip_ref, galog_ref,
                   step_s, su_s, unit_s, y_s, gy_s, gs_s, lb_s, rate_s, hist, lams):
    rows = slots * SLOT
    pre = jnp.dot(proj_ref[:, :DTR], w_dt_ref[...], preferred_element_type=F32) + bias_ref[...]
    step = softplus(pre)
    unit = unit_ref[...].astype(F32)
    spread(step_s, step)
    spread(unit_s, unit)
    spread(su_s, step * unit)
    z = gate_ref[...]
    sig = jax.nn.sigmoid(z)
    gg = grad_ref[...]
    gy = gg * z * sig
    spread(gy_s, gy)
    rate_s[...] = -jnp.exp(alog_ref[...])
    galog_ref[...] = jnp.zeros_like(galog_ref)
    zero = jnp.zeros((SUBL, LANES), F32)
    span = SLOT + 1

    def hist_at(k, t):
        return pl.ds(pl.multiple_of((k * span + t) * SUBL, SUBL), SUBL)

    def lam_at(k, t):
        return pl.ds(pl.multiple_of((k * SLOT + t) * SUBL, SUBL), SUBL)

    for m in range(slots):
        for k in range(NSTATE):
            hist[hist_at(k, 0), :] = zero

        def forward(t, states):
            r = m * SLOT + t
            row = pl.ds(pl.multiple_of(r * SUBL, SUBL), SUBL)
            st = step_s[row, :] * LOG2E
            su = su_s[row, :]
            y = zero
            new = []
            for k in range(NSTATE):
                dec = jnp.exp2(rate_s[k * SUBL : (k + 1) * SUBL, :] * st)
                s = dec * states[k] + bc_ref[r, k] * su
                y = y + bc_ref[r, NSTATE + k] * s
                hist[hist_at(k, t + 1), :] = s
                new.append(s)
            y_s[row, :] = y
            return tuple(new)

        lax.fori_loop(0, SLOT, forward, tuple(zero for _ in range(NSTATE)))

        def backward(i, carry):
            t = SLOT - 1 - i
            r = m * SLOT + t
            row = pl.ds(pl.multiple_of(r * SUBL, SUBL), SUBL)
            st = step_s[row, :]
            st2 = st * LOG2E
            gyt = gy_s[row, :]
            lb = zero
            gs = zero
            new = []
            for k in range(NSTATE):
                rate = rate_s[k * SUBL : (k + 1) * SUBL, :]
                dec = jnp.exp2(rate * st2)
                lam = bc_ref[r, NSTATE + k] * gyt + carry[k]
                ld = dec * lam
                new.append(ld)
                lams[lam_at(k, t), :] = lam
                lb = lb + bc_ref[r, k] * lam
                x = ld * hist[hist_at(k, t), :]
                gs = gs + rate * x
                at = slice(k * SUBL, (k + 1) * SUBL)
                galog_ref[at, :] = galog_ref[at, :] + st * x
            lb_s[row, :] = lb
            gs_s[row, :] = gs + unit_s[row, :] * lb
            return tuple(new)

        lax.fori_loop(0, SLOT, backward, tuple(zero for _ in range(NSTATE)))
        out = slice(m * SLOT, (m + 1) * SLOT)
        base = m * SLOT * SUBL

        lane = lax.broadcasted_iota(jnp.int32, (SLOT, LANES), 1)

        def reduce_state(k, acc):
            ab = jnp.zeros((SLOT, LANES), F32)
            ac = jnp.zeros((SLOT, LANES), F32)
            for j in range(SUBL):
                cols = slice(j * LANES, (j + 1) * LANES)
                lam = lams[pl.ds(k * SLOT * SUBL + j, SLOT, stride=SUBL), :]
                h = hist[pl.ds((k * span + 1) * SUBL + j, SLOT, stride=SUBL), :]
                sj = su_s[pl.ds(base + j, SLOT, stride=SUBL), :]
                gj = gy_s[pl.ds(base + j, SLOT, stride=SUBL), :]
                ab = ab + lam * sj
                ac = ac + h * gj
            sb = jnp.sum(ab, axis=1, keepdims=True)
            sc = jnp.sum(ac, axis=1, keepdims=True)
            return acc + jnp.where(lane == k, sb, 0.0) + jnp.where(lane == NSTATE + k, sc, 0.0)

        sums = lax.fori_loop(0, NSTATE, reduce_state, jnp.zeros((SLOT, LANES), F32))
        gproj_ref[out, DTR : DTR + LANES] = sums.astype(BF)
    galog_ref[...] = galog_ref[...] * rate_s[...]
    y = collect(y_s, rows) + skip_ref[...] * unit
    gz_ref[...] = (gg * y * sig * (1.0 + z * (1.0 - sig))).astype(BF)
    gunit_ref[...] = gy * skip_ref[...] + step * collect(lb_s, rows)
    gskip_ref[...] = jnp.sum(gy * unit, axis=0, keepdims=True)
    q = collect(gs_s, rows) * jax.nn.sigmoid(pre)
    gbias_ref[...] = jnp.sum(q, axis=0, keepdims=True)
    ql = q.astype(BF)
    gdt_ref[...] = mat_tn(proj_ref[:, :DTR], ql)
    gproj_ref[:, :DTR] = mat_nt(ql, w_dt_ref[...]).astype(BF)


def scan_backward(proj, bc, unit, gate, w_dt, dt_bias, d_skip, a_log, grad):
    rows = unit.shape[0]
    vm = pl.BlockSpec(memory_space=pltpu.VMEM)
    sm = pl.BlockSpec(memory_space=pltpu.SMEM)
    sds = jax.ShapeDtypeStruct
    flat = pltpu.VMEM((rows * SUBL, LANES), F32)
    return pl.pallas_call(
        functools.partial(adjoint_kernel, rows // SLOT),
        out_shape=(
            sds((rows, EI), BF),
            sds((rows, EI), F32),
            sds((rows, DTR + LANES), BF),
            sds((DTR, EI), F32),
            sds((1, EI), F32),
            sds((1, EI), F32),
            sds((NSTATE * SUBL, LANES), F32),
        ),
        in_specs=[vm, sm, vm, vm, vm, vm, vm, vm, vm],
        out_specs=(vm,) * 7,
        scratch_shapes=[flat] * 7
        + [
            pltpu.VMEM((NSTATE * SUBL, LANES), F32),
            pltpu.VMEM((NSTATE * (SLOT + 1) * SUBL, LANES), F32),
            pltpu.VMEM((NSTATE * SLOT * SUBL, LANES), F32),
        ],
        compiler_params=pltpu.CompilerParams(vmem_limit_bytes=60 << 20),
        name="scan_backward",
    )(proj, bc, unit, gate, w_dt, dt_bias, d_skip, a_log, grad)


def rope_tables(length, head_dim):
    half_dim = head_dim // 2
    freq_index = jnp.arange(half_dim, dtype=F32)
    inv_freq = jnp.exp(-math.log(ROPE_BASE) * 2.0 * freq_index / head_dim)
    angles = jnp.arange(length, dtype=F32)[:, None] * inv_freq[None, :]
    return (jnp.cos(angles)[None, :, None, :], jnp.sin(angles)[None, :, None, :])


def rope_apply(values, cosine, sine):
    half_dim = values.shape[-1] // 2
    a = values[..., :half_dim]
    b = values[..., half_dim:]
    return jnp.concatenate([a * cosine - b * sine, b * cosine + a * sine], axis=-1)


def rms_parts(v, g):
    s = lax.rsqrt(jnp.mean(v * v, axis=-1, keepdims=True) + EPS_NORM)
    return s, v * s


def rms_back(v, g, gh):
    s, nrm = rms_parts(v, g)
    gg = jnp.sum(gh * nrm, axis=0)
    gv = s * (gh * g - nrm * jnp.mean(gh * g * nrm, axis=-1, keepdims=True))
    return gv, gg


def total(partial_out):
    return sum_tensor(partial_out.astype(BF)).astype(F32)


def shift_down(v, by):
    if by == 0:
        return v
    return jnp.pad(v, ((0, 0), (by, 0), (0, 0)))[:, : v.shape[1]]


def shift_up(v, by):
    if by == 0:
        return v
    return jnp.pad(v, ((0, 0), (0, by), (0, 0)))[:, by:]


def attend(query, keys, values):
    scale = HEAD_DIM ** (-0.5)
    distance = jnp.arange(SLOT)[:, None] - jnp.arange(SLOT)[None, :]
    allowed = (distance >= 0) & (distance < WINDOW)
    scores = jnp.einsum("mqhd,mkhd->mhqk", query, keys, preferred_element_type=F32) * scale
    scores = jnp.where(allowed, scores, NEG_FILL)
    expo = jnp.exp(scores - jnp.max(scores, axis=-1, keepdims=True))
    return expo / jnp.sum(expo, axis=-1, keepdims=True)


def ffn_forward(h, w_gu, w_down):
    pre = mat_nn(h, w_gu)
    act = (silu(pre[:, :FI]) * pre[:, FI:]).astype(BF)
    return total(mat_nn(act, w_down)), pre, act


def ffn_backward(pre, w_gu, w_down, grad_low):
    gate = pre[:, :FI]
    up = pre[:, FI:]
    ga = mat_nt(grad_low, w_down)
    sig = jax.nn.sigmoid(gate)
    grad_gate = ga * up * sig * (1.0 + gate * (1.0 - sig))
    grad_up = ga * gate * sig
    gp = jnp.concatenate([grad_gate, grad_up], axis=1).astype(BF)
    return total(mat_nt(gp, w_gu)), gp


def layer(x, grad_out, w, small, gains, n):
    rows = x.shape[0]
    m = rows // SLOT
    hr = HW // HEAD_DIM
    cosine, sine = rope_tables(SLOT, HEAD_DIM)
    s1, n1 = rms_parts(x, gains[0])
    h1 = (n1 * gains[0]).astype(BF)
    mixed = mat_nn(h1, w["w_in"])
    mix_x = mixed[:, :EI].reshape(m, SLOT, EI)
    gate_z = mixed[:, EI:]
    conv_w = small["conv_w"].astype(F32)
    pre_conv = small["conv_b"].astype(F32)[None, None, :]
    for j in range(CONV):
        pre_conv = pre_conv + conv_w[j] * shift_down(mix_x, CONV - 1 - j)
    unit = silu(pre_conv).astype(BF).reshape(rows, EI)
    proj = sum_proj(mat_nn(unit, small["w_x"]).astype(BF))
    bc = proj[:, DTR:].astype(F32)
    scan_args = (
        proj[:, :DTR],
        bc,
        unit,
        gate_z,
        small["w_dt"],
        small["dt_bias"].astype(F32)[None],
        small["d_skip"].astype(F32)[None],
        small["a_log"].astype(F32).reshape(NSTATE * SUBL, LANES),
    )
    gated = scan_forward(*scan_args)
    x1 = x + total(mat_nn(gated, w["w_out"]))
    h2 = (rms_parts(x1, 0)[1] * gains[1]).astype(BF)
    branch, pre1, act1 = ffn_forward(h2, w["w_gu1"], w["w_down1"])
    x2 = x1 + branch
    h3 = (rms_parts(x2, 0)[1] * gains[2]).astype(BF)
    packed = mat_nn(h3, w["w_qkv"]).reshape(m, SLOT, 3, hr, HEAD_DIM)
    query = rope_apply(packed[:, :, 0], cosine, sine).astype(BF)
    keys = rope_apply(packed[:, :, 1], cosine, sine).astype(BF)
    values = packed[:, :, 2].astype(BF)
    probs = attend(query, keys, values)
    probs_low = probs.astype(BF)
    attended = jnp.einsum("mhqk,mkhd->mqhd", probs_low, values, preferred_element_type=F32)
    attended = attended.reshape(rows, HW).astype(BF)
    x3 = x2 + total(mat_nn(attended, w["w_o"]))
    h4 = (rms_parts(x3, 0)[1] * gains[3]).astype(BF)
    pre2 = mat_nn(h4, w["w_gu2"])
    act2 = (silu(pre2[:, :FI]) * pre2[:, FI:]).astype(BF)
    last = mat_nn(act2, w["w_down2"]).astype(BF)

    gb4 = grad_out.astype(BF)
    gh, gp2 = ffn_backward(pre2, w["w_gu2"], w["w_down2"], gb4)
    gv, gg4 = rms_back(x3, gains[3], gh)
    g3 = grad_out + gv
    gb3 = g3.astype(BF)
    gatt = mat_nt(gb3, w["w_o"]).astype(BF).reshape(m, SLOT, hr, HEAD_DIM)
    grad_p = jnp.einsum("mqhd,mkhd->mhqk", gatt, values, preferred_element_type=F32)
    inner = jnp.sum(probs * grad_p, axis=-1, keepdims=True)
    gs = (probs * (grad_p - inner)).astype(BF)
    scale = HEAD_DIM ** (-0.5)
    gq = jnp.einsum("mhqk,mkhd->mqhd", gs, keys, preferred_element_type=F32) * scale
    gk = jnp.einsum("mhqk,mqhd->mkhd", gs, query, preferred_element_type=F32) * scale
    gvv = jnp.einsum("mhqk,mqhd->mkhd", probs_low, gatt, preferred_element_type=F32)
    gpk = (
        jnp.stack([rope_apply(gq, cosine, -sine), rope_apply(gk, cosine, -sine), gvv], axis=2)
        .reshape(rows, 3 * HW)
        .astype(BF)
    )
    gv, gg3 = rms_back(x2, gains[2], total(mat_nt(gpk, w["w_qkv"])))
    g2 = g3 + gv
    gb2 = g2.astype(BF)
    gh, gp1 = ffn_backward(pre1, w["w_gu1"], w["w_down1"], gb2)
    gv, gg2 = rms_back(x1, gains[1], gh)
    g1 = g2 + gv
    gb1 = g1.astype(BF)
    ggated = mat_nt(gb1, w["w_out"])
    gz, gunit, gproj, g_dt, g_bias, g_skip, g_alog = scan_backward(*scan_args, ggated)
    gproj = sum_tensor(gproj)[:, : DTR + 2 * NSTATE]
    g_wx = mat_tn(unit, gproj)
    gu = gunit + mat_nt(gproj, small["w_x"])
    sig = jax.nn.sigmoid(pre_conv)
    gpre = gu.reshape(m, SLOT, EI) * sig * (1.0 + pre_conv * (1.0 - sig))
    g_conv_b = jnp.sum(gpre, axis=(0, 1))
    g_conv_w = jnp.stack(
        [jnp.sum(gpre * shift_down(mix_x, CONV - 1 - j), axis=(0, 1)) for j in range(CONV)]
    )
    gmx = sum(conv_w[j] * shift_up(gpre, CONV - 1 - j) for j in range(CONV))
    gmixed = jnp.concatenate([gmx.reshape(rows, EI).astype(BF), gz], axis=1)
    gv, gg1 = rms_back(x, gains[0], total(mat_nt(gmixed, w["w_in"])))
    g0 = g1 + gv

    left_t = jnp.concatenate([h1, gated, h2, act1, attended, h4, act2], axis=1).T
    rights = jnp.stack([gmixed, gb1, gp1, gb2, gb3, gp2, gb4])
    g_qkv = mat_tn(h3, gpk).astype(BF)
    g_qkv = change_rows(g_qkv, 0, D, D)
    start = lax.axis_index("tensor") * DG
    g_gain = lax.dynamic_slice_in_dim(jnp.stack([gg1, gg2, gg3, gg4]), start, DG, 1)
    pieces = [g_gain, g_conv_w, g_conv_b, g_bias, g_skip, g_alog, g_wx, g_dt]
    small_grads = jnp.concatenate([p.reshape(-1, LANES).astype(BF) for p in pieces])
    g0, small_grads, last, left_t = lax.optimization_barrier((g0, small_grads, last, left_t))
    return x3, last, g0, (left_t, rights, g_qkv), small_grads


def extents(n, shard_rows):
    slab = BIG_ROWS * LINES // n
    before = 0
    after = 0
    back_before = 0
    back_after = 0
    for d in range(n):
        lo, hi = slab * d, slab * (d + 1) - 1
        qs = [p + LEAD + (SMALL_ROWS if p >= FIRST else 0) - shard_rows * d for p in (lo, hi)]
        before = max(before, -qs[0])
        after = max(after, qs[1] + 1 - shard_rows)
    return before, after


def shift_perm(n, by):
    return [(i, i + by) for i in range(n) if 0 <= i + by < n]


def stack_kernel(n, shard_lines, before, per, top_ref, own_ref, bottom_ref, out_ref, hold, sem):
    d = lax.axis_index("dp")
    i = pl.program_id(0)
    steps = BIG_ROWS // n // per
    size = per * LINES

    def fetch(k, slot):
        row = d * (BIG_ROWS // n) + k * per
        a = row * LINES + LEAD + jnp.where(row >= FIRST // LINES, SMALL_ROWS, 0) - d * shard_lines
        high = a < 0
        low = a + size > shard_lines

        @pl.when(high)
        def _():
            pltpu.make_async_copy(top_ref.at[pl.ds(a + before, size), 0], hold.at[slot], sem.at[slot]).start()

        @pl.when(low)
        def _():
            pltpu.make_async_copy(
                bottom_ref.at[pl.ds(a + size - shard_lines, size), 0], hold.at[slot], sem.at[slot]
            ).start()

        @pl.when(jnp.logical_not(jnp.logical_or(high, low)))
        def _():
            pltpu.make_async_copy(own_ref.at[pl.ds(a, size), 0], hold.at[slot], sem.at[slot]).start()

    @pl.when(i == 0)
    def _():
        for k in range(min(3, steps)):
            fetch(k, k)

    @pl.when(i + 3 < steps)
    def _():
        fetch(i + 3, lax.rem(i + 3, 4))

    slot = lax.rem(i, 4)
    pltpu.make_async_copy(own_ref.at[pl.ds(0, size), 0], hold.at[slot], sem.at[slot]).wait()
    for j in range(LINES):
        out_ref[:, j * LANES : (j + 1) * LANES] = hold[slot, pl.ds(j, per, stride=LINES), :].astype(BF)


def stack_own(lines3, n):
    shard_lines = lines3.shape[0]
    before, after = extents(n, shard_lines)
    rows = BIG_ROWS // n
    per = 64 if rows % 64 == 0 else 32
    size = per * LINES
    nxt = lax.ppermute(lines3[:after], "dp", shift_perm(n, -1))
    prv = lax.ppermute(lines3[shard_lines - before :], "dp", shift_perm(n, 1))
    top = jnp.concatenate([prv, lines3[:size]])
    bottom = jnp.concatenate([lines3[shard_lines - size :], nxt])
    hbm = pl.BlockSpec(memory_space=pl.ANY)
    return pl.pallas_call(
        functools.partial(stack_kernel, n, shard_lines, before, per),
        grid=(rows // per,),
        out_shape=jax.ShapeDtypeStruct((rows, D), BF),
        in_specs=[hbm] * 3,
        out_specs=pl.BlockSpec((per, D), lambda i: (i, 0)),
        scratch_shapes=[pltpu.VMEM((4, size, LANES), F32), pltpu.SemaphoreType.DMA((4,))],
        compiler_params=pltpu.CompilerParams(vmem_limit_bytes=24 << 20),
        name="stack_own",
    )(top, lines3, bottom)


def low_kernel(x_ref, out_ref):
    out_ref[...] = x_ref[:, 0, :].astype(BF)


def to_low(value):
    vm = pl.BlockSpec(memory_space=pltpu.VMEM)
    return pl.pallas_call(
        low_kernel,
        out_shape=jax.ShapeDtypeStruct((value.shape[0], LANES), BF),
        in_specs=[vm],
        out_specs=vm,
        name="to_low",
    )(value)


def window(values, shift, size):
    length = values.shape[0]
    s = jnp.clip(shift, 0, length - size)
    got = lax.dynamic_slice_in_dim(values, s, size, 0)
    room = jnp.zeros((3 * size,) + values.shape[1:], values.dtype)
    room = lax.dynamic_update_slice_in_dim(room, got, size + jnp.clip(s - shift, -size, size), 0)
    return room[size : 2 * size]


STRIP = 8192


def lone_group(groups, bounds_ref, start, stop):
    def look(g, found):
        holds = jnp.logical_and(bounds_ref[2 * g] <= start, bounds_ref[2 * g + 1] >= stop)
        return jnp.where(holds, g, found)

    return lax.fori_loop(0, groups, look, jnp.int32(-1))


def moments_kernel(groups, shard, bounds_ref, grad_ref, w_ref, one_ref, two_ref,
                   first_ref, second_ref, grad_out, sums_ref, hold):
    i = pl.program_id(0)
    size = CHUNK * LANES
    lanes = STRIP // 8

    @pl.when(i == 0)
    def _():
        @pl.loop(0, 2 * groups)
        def _(g):
            sums_ref[g] = 0.0

    def strip(k, carry):
        here = pl.ds(pl.multiple_of(k * STRIP, STRIP), STRIP)
        grad = grad_ref[:, here]
        w = w_ref[:, here]
        first = BETA_ONE * one_ref[:, here] + (1.0 - BETA_ONE) * grad
        second = BETA_TWO * two_ref[:, here] + (1.0 - BETA_TWO) * grad * grad
        ratio = first / (jnp.sqrt(second) + ADAM_EPS) + DECAY_W * w
        first_ref[:, here] = first
        second_ref[:, here] = second
        grad_out[:, here] = grad
        hold[:, here] = ratio
        wsq, rsq = carry
        for j in range(8):
            part = slice(j * lanes, (j + 1) * lanes)
            wsq = wsq + w[:, part] * w[:, part]
            rsq = rsq + ratio[:, part] * ratio[:, part]
        return wsq, rsq

    zero = jnp.zeros((1, lanes), F32)
    wsq, rsq = lax.fori_loop(0, size // STRIP, strip, (zero, zero))
    d = lax.axis_index("dp")
    start = d * shard + i * size
    limit = (d + 1) * shard
    alone = lone_group(groups, bounds_ref, start, start + size)
    alone = jnp.where(start + size <= limit, alone, -1)

    @pl.when(alone >= 0)
    def _():
        sums_ref[2 * alone] = sums_ref[2 * alone] + jnp.sum(wsq)
        sums_ref[2 * alone + 1] = sums_ref[2 * alone + 1] + jnp.sum(rsq)

    @pl.when(alone < 0)
    def _():
        @pl.loop(0, groups)
        def _(g):
            low = jnp.maximum(bounds_ref[2 * g], start)
            high = jnp.minimum(bounds_ref[2 * g + 1], jnp.minimum(start + size, limit))

            @pl.when(low < high)
            def _():
                def masked(k, carry):
                    at = pl.multiple_of(k * lanes, lanes)
                    here = pl.ds(at, lanes)
                    index = start + at + lax.broadcasted_iota(jnp.int32, (1, lanes), 1)
                    inside = (index >= low) & (index < high)
                    wv = w_ref[:, here]
                    rv = hold[:, here]
                    return (
                        carry[0] + jnp.where(inside, wv * wv, 0.0),
                        carry[1] + jnp.where(inside, rv * rv, 0.0),
                    )

                k0 = (low - start) // lanes
                k1 = (high - start + lanes - 1) // lanes
                wv, rv = lax.fori_loop(k0, k1, masked, (zero, zero))
                sums_ref[2 * g] = sums_ref[2 * g] + jnp.sum(wv)
                sums_ref[2 * g + 1] = sums_ref[2 * g + 1] + jnp.sum(rv)


def moments(bounds, lines, master, one, two):
    shard = master.shape[1]
    size = CHUNK * LANES
    groups = bounds.shape[0] // 2
    block = pl.BlockSpec((1, size), lambda i: (0, i))
    ahead = SLACK // CHUNK
    flat = jax.ShapeDtypeStruct((1, shard), F32)
    smem = pl.BlockSpec(memory_space=pltpu.SMEM)
    return pl.pallas_call(
        functools.partial(moments_kernel, groups, shard),
        grid=(pl.cdiv(shard, size),),
        out_shape=(flat, flat, flat, jax.ShapeDtypeStruct((2 * groups,), F32)),
        in_specs=[smem, pl.BlockSpec((1, size), lambda i: (0, i + ahead)), block, block, block],
        out_specs=(block, block, block, smem),
        scratch_shapes=[pltpu.VMEM((1, size), F32)],
        compiler_params=pltpu.CompilerParams(vmem_limit_bytes=40 << 20),
        name="moments",
    )(bounds, lines.reshape(1, -1), master, one, two)


def update_kernel(groups, shard, bounds_ref, trust_ref, w_ref, first_ref, second_ref, new_ref, low_ref, hold):
    i = pl.program_id(0)
    size = CHUNK * LANES
    lanes = STRIP // 8
    start = lax.axis_index("dp") * shard + i * size
    alone = lone_group(groups, bounds_ref, start, start + size)

    def step(trust_of):
        @pl.loop(0, size // STRIP)
        def _(k):
            here = pl.ds(pl.multiple_of(k * STRIP, STRIP), STRIP)
            w = w_ref[:, here]
            ratio = first_ref[:, here] / (jnp.sqrt(second_ref[:, here]) + ADAM_EPS) + DECAY_W * w
            new = w - LEARN_RATE * trust_of(here) * ratio
            new_ref[:, here] = new
            low_ref[:, here] = new.astype(BF)

    @pl.when(alone >= 0)
    def _():
        trust = trust_ref[jnp.maximum(alone, 0)]
        step(lambda here: trust)

    @pl.when(alone < 0)
    def _():
        hold[...] = jnp.zeros_like(hold)

        @pl.loop(0, groups)
        def _(g):
            low = jnp.maximum(bounds_ref[2 * g], start)
            high = jnp.minimum(bounds_ref[2 * g + 1], start + size)

            @pl.when(low < high)
            def _():
                @pl.loop((low - start) // lanes, (high - start + lanes - 1) // lanes)
                def _(k):
                    at = pl.multiple_of(k * lanes, lanes)
                    here = pl.ds(at, lanes)
                    index = start + at + lax.broadcasted_iota(jnp.int32, (1, lanes), 1)
                    hold[:, here] = jnp.where((index >= low) & (index < high), trust_ref[g], hold[:, here])

        step(lambda here: hold[:, here])


def update(bounds, trust, master, first, second):
    shard = master.shape[1]
    size = CHUNK * LANES
    groups = bounds.shape[0] // 2
    block = pl.BlockSpec((1, size), lambda i: (0, i))
    smem = pl.BlockSpec(memory_space=pltpu.SMEM)
    return pl.pallas_call(
        functools.partial(update_kernel, groups, shard),
        grid=(pl.cdiv(shard, size),),
        out_shape=(jax.ShapeDtypeStruct((1, shard), F32), jax.ShapeDtypeStruct((1, shard), BF)),
        in_specs=[smem, smem, block, block, block],
        out_specs=(block, block),
        scratch_shapes=[pltpu.VMEM((1, size), F32)],
        compiler_params=pltpu.CompilerParams(vmem_limit_bytes=40 << 20),
        name="update",
    )(bounds, trust, master, first, second)


def norms_kernel(n, m, own_ref, out_ref, across, along, part, ssem, rsem, ssem2, rsem2):
    d = lax.axis_index("dp")
    t = lax.axis_index("tensor")
    barrier = pltpu.get_barrier_semaphore()
    for k in range(1, m):
        pl.semaphore_signal(barrier, inc=1, device_id=(d, lax.rem(t + k, m)), device_id_type=MESH)

    @pl.loop(1, n)
    def _(k):
        pl.semaphore_signal(barrier, inc=1, device_id=(lax.rem(d + k, n), t), device_id_type=MESH)

    pl.semaphore_wait(barrier, n + m - 2)

    def over_tensor(k):
        return pltpu.make_async_remote_copy(
            src_ref=own_ref,
            dst_ref=across.at[k - 1],
            send_sem=ssem.at[k - 1],
            recv_sem=rsem.at[k - 1],
            device_id=(d, lax.rem(t + k, m)),
            device_id_type=MESH,
        )

    def over_dp(k):
        return pltpu.make_async_remote_copy(
            src_ref=part,
            dst_ref=along.at[k - 1],
            send_sem=ssem2.at[k - 1],
            recv_sem=rsem2.at[k - 1],
            device_id=(lax.rem(d + k, n), t),
            device_id_type=MESH,
        )

    for k in range(1, m):
        over_tensor(k).start()
    total_ = own_ref[...]
    for k in range(1, m):
        over_tensor(k).wait_recv()
    for k in range(1, m):
        total_ = total_ + across[k - 1]
    part[...] = total_

    @pl.loop(1, n)
    def _(k):
        over_dp(k).start()

    @pl.loop(1, n)
    def _(k):
        over_dp(k).wait_recv()

    def add(k, acc):
        return acc + along[k - 1]

    out_ref[...] = lax.fori_loop(1, n, add, part[...])
    for k in range(1, m):
        over_tensor(k).wait_send()

    @pl.loop(1, n)
    def _(k):
        over_dp(k).wait_send()


def sum_everywhere(values, n, m):
    vm = pl.BlockSpec(memory_space=pltpu.VMEM)
    dma = pltpu.SemaphoreType.DMA
    tile = pltpu.VMEM((8, LANES), F32)
    return pl.pallas_call(
        functools.partial(norms_kernel, n, m),
        out_shape=jax.ShapeDtypeStruct((8, LANES), F32),
        in_specs=[vm],
        out_specs=vm,
        scratch_shapes=[
            pltpu.VMEM((m - 1, 8, LANES), F32),
            pltpu.VMEM((n - 1, 8, LANES), F32),
            tile,
            dma((m - 1,)),
            dma((m - 1,)),
            dma((n - 1,)),
            dma((n - 1,)),
        ],
        compiler_params=pltpu.CompilerParams(collective_id=2, has_side_effects=True),
        name="sum_everywhere",
    )(values)


def per_device(n, m, tokens, cotangent, lengths, master, moment_one, moment_two):
    d = lax.axis_index("dp")
    shard = master.shape[1]
    lines = shard // LANES
    lines3 = master.reshape(lines, 1, LANES)
    base = d * lines
    mid = LEAD + FIRST
    small_own = jnp.concatenate(
        [window(lines3, -base, GAIN_ROWS), window(lines3, mid - base, SMALL_ROWS)]
    )
    small_flat = lax.psum(to_low(small_own), "dp")
    weights = ring_gather(stack_own(lines3, n), n)
    weights, small_flat = lax.optimization_barrier((weights, small_flat))
    gains = lax.all_gather(small_flat[:GAIN_ROWS].reshape(4, DG), "tensor", axis=1, tiled=True)
    gains = gains.astype(F32)
    small = {}
    at = GAIN_ROWS
    for name, shape in SMALL:
        count = math.prod(shape) // LANES
        small[name] = small_flat[at : at + count].reshape(shape)
        at += count
    w = {}
    for name, rows in BIG:
        w[name] = weights[BIG_OFF[name] : BIG_OFF[name] + rows]
    w["w_qkv"] = change_rows(weights, BIG_OFF["w_qkv"], dict(BIG)["w_qkv"], 3 * HW)
    x = tokens.astype(F32)
    pos = lax.broadcasted_iota(jnp.int32, (tokens.shape[0] // SLOT, SLOT), 1)
    valid = (pos < lengths[:, None]).astype(F32).reshape(-1, 1)
    grad = cotangent.astype(F32) * valid
    x3, last, grad_in, operands, small_grads = layer(x, grad, w, small, gains, n)
    small_sum = lax.psum(small_grads, "dp")
    laid = ring_reduce(*operands, n, lines)
    branch = lax.psum(last, "tensor")
    laid, small_sum, branch = lax.optimization_barrier((laid, small_sum, branch))
    out = (x3 + branch.astype(F32)).astype(BF)
    small_sum = small_sum.astype(F32).reshape(-1, 1, LANES)

    before, after = extents(n, lines)
    slab_lines = BIG_ROWS * LINES // n

    def local(row):
        return row * LINES + LEAD + jnp.where(row >= FIRST // LINES, SMALL_ROWS, 0) - base

    begin = local(d * (BIG_ROWS // n))
    close = local((d + 1) * (BIG_ROWS // n) - 1) + LINES
    tail, head, laid = lax.optimization_barrier(
        (laid[SLACK + lines : SLACK + lines + after], laid[SLACK - before : SLACK], laid)
    )
    from_prev = lax.ppermute(tail, "dp", shift_perm(n, 1))
    from_next = lax.ppermute(head, "dp", shift_perm(n, -1))
    line = lax.broadcasted_iota(jnp.int32, (after, 1, 1), 0)
    top = jnp.where(line < begin, from_prev, laid[SLACK : SLACK + after])
    line = lax.broadcasted_iota(jnp.int32, (before, 1, 1), 0) + (lines - before)
    bottom = jnp.where(line >= close, from_next, laid[SLACK + lines - before : SLACK + lines])
    laid = laid.at[SLACK : SLACK + after].set(top)
    laid = laid.at[SLACK + lines - before : SLACK + lines].set(bottom)

    def place(laid, values, at):
        count = values.shape[0]
        return lax.dynamic_update_slice_in_dim(laid, values, SLACK + jnp.clip(at - base, -count, lines), 0)

    laid = place(laid, small_sum[GAIN_ROWS:], mid)
    laid = place(laid, small_sum[:GAIN_ROWS], 0)
    used = LEAD + SMALL_ROWS + BIG_ROWS * LINES
    rest = lines * n - used
    if rest:
        laid = place(laid, jnp.zeros((rest, 1, LANES), F32), used)

    bounds = jnp.asarray([v for pair in group_bounds() for v in pair], jnp.int32)
    first, second, grad_shard, sums = moments(bounds, laid, master, moment_one, moment_two)
    count = sums.shape[0]
    tile = jnp.pad(sums, (0, 8 * LANES - count)).reshape(8, LANES)
    squares = sum_everywhere(tile, n, m).reshape(-1)[:count].reshape(-1, 2)
    trust = jnp.sqrt(squares[:, 0] + TRUST_EPSILON) * lax.rsqrt(squares[:, 1] + TRUST_EPSILON)
    master_new, low = update(bounds, trust, master, first, second)
    return (out, grad_in, master_new, first, second, low, grad_shard, jnp.sqrt(squares))


def solution(mesh):
    row = P("dp", None)
    flat = P("tensor", "dp")
    return jax.shard_map(
        functools.partial(per_device, mesh.shape["dp"], mesh.shape["tensor"]),
        mesh=mesh,
        in_specs=(row, row, P("dp"), flat, flat, flat),
        out_specs=(row, row, flat, flat, flat, flat, flat, P()),
        check_vma=False,
    )
```

```python
import functools
import math

import jax
import jax.numpy as jnp
from jax import lax
from jax.experimental import pallas as pl
from jax.experimental.pallas import tpu as pltpu
from jax.sharding import PartitionSpec as P

D = 2048
INNER = 4096
NSTATE = 16
DTR = 128
HEADS = 32
HEAD_DIM = 64
FF = 4096
CONV = 4
WINDOW = 2048
SLOT = 128
LANES = 128

EPS_NORM = 1e-05
TRUST_EPSILON = 1e-06
ROPE_BASE = 10000.0
BETA_ONE = 0.5
BETA_TWO = 0.55
ADAM_EPS = 1e-06
DECAY_W = 0.01
LEARN_RATE = 0.2
NEG_FILL = -1e30
LOG2E = 1.4426950408889634
MESH = pl.DeviceIdType.MESH
BF = jnp.bfloat16
F32 = jnp.float32

EI = INNER // 4
FI = FF // 4
HW = HEADS * HEAD_DIM // 4
DG = D // 4

SMALL = [
    ("conv_w", (CONV, EI)),
    ("conv_b", (EI,)),
    ("dt_bias", (EI,)),
    ("d_skip", (EI,)),
    ("a_log", (NSTATE, EI)),
    ("w_x", (EI, DTR + 2 * NSTATE)),
    ("w_dt", (DTR, EI)),
]
SMALL_ROWS = sum(math.prod(s) for _, s in SMALL) // LANES
GAIN_ROWS = 4 * DG // LANES
BIG = [
    ("w_in", D),
    ("w_out", EI),
    ("w_gu1", D),
    ("w_down1", FI),
    ("w_qkv", D * 3 * HW // D),
    ("w_o", HW),
    ("w_gu2", D),
    ("w_down2", FI),
]
BIG_OFF = {}
_at = 0
for _name, _rows in BIG:
    BIG_OFF[_name] = _at
    _at += _rows
BIG_ROWS = _at
LINES = D // LANES
FIRST = BIG_OFF["w_out"] * LINES
LEAD = GAIN_ROWS
CHUNK = 2048
SLACK = -(-(SMALL_ROWS + GAIN_ROWS) // CHUNK) * CHUNK


def group_bounds():
    bounds = []
    for k in range(4):
        bounds.append((k * DG, (k + 1) * DG))
    at = 4 * DG
    entries = [("w_in", D * 2 * EI)]
    entries += [(name, math.prod(shape)) for name, shape in SMALL]
    entries += [
        ("w_out", EI * D),
        ("w_gu1", D * 2 * FI),
        ("w_down1", FI * D),
        ("w_qkv", D * 3 * HW),
        ("w_o", HW * D),
        ("w_gu2", D * 2 * FI),
        ("w_down2", FI * D),
    ]
    for _, count in entries:
        bounds.append((at, at + count))
        at += count
    return bounds


def silu(v):
    return v * jax.nn.sigmoid(v)


def softplus(v):
    return jnp.maximum(v, 0.0) + jnp.log1p(jnp.exp(-jnp.abs(v)))


def mat_nn(a, b):
    return jnp.dot(a, b, preferred_element_type=F32)


def mat_tn(a, b):
    return lax.dot_general(a, b, (((0,), (0,)), ((), ())), preferred_element_type=F32)


def mat_nt(a, b):
    return lax.dot_general(a, b, (((1,), (1,)), ((), ())), preferred_element_type=F32)


def ring_pos(d, n):
    return jnp.where(lax.rem(d, 2) == 0, lax.div(d, 2), n - 1 - lax.div(d, 2))


def ring_dev(p, n):
    return jnp.where(p < n // 2, 2 * p, 2 * (n - 1 - p) + 1)


def ring_neighbours(n):
    d = lax.axis_index("dp")
    p = ring_pos(d, n)
    right = ring_dev(lax.rem(p + 1, n), n)
    left = ring_dev(lax.rem(p + n - 1, n), n)
    return d, p, right, left


def ring_barrier(left, right, t):
    barrier = pltpu.get_barrier_semaphore()
    for nb in (left, right):
        pl.semaphore_signal(barrier, inc=1, device_id=(nb, t), device_id_type=MESH)
    pl.semaphore_wait(barrier, 2)


def gather_kernel(n, subs, own_ref, out_ref, hold, local_sem, ssem, rsem):
    t = lax.axis_index("tensor")
    d, p, right, left = ring_neighbours(n)
    rows = own_ref.shape[0]
    half = rows // 2
    sub = half // subs
    fetch = pltpu.make_async_copy(own_ref, hold, local_sem.at[0])
    fetch.start()
    ring_barrier(left, right, t)

    def copy(way, step, c, from_own):
        target = right if way == 0 else left
        owner = ring_dev(lax.rem(p + (n - step if way == 0 else step), n), n)
        at = pl.multiple_of(owner * rows + way * half + c * sub, 8)
        src = own_ref.at[pl.ds(way * half + c * sub, sub)] if from_own else out_ref.at[pl.ds(at, sub)]
        return pltpu.make_async_remote_copy(
            src_ref=src,
            dst_ref=out_ref.at[pl.ds(at, sub)],
            send_sem=ssem.at[way, step, c],
            recv_sem=rsem.at[way, step, c],
            device_id=(target, t),
            device_id_type=MESH,
        )

    for c in range(subs):
        for way in (0, 1):
            copy(way, 0, c, True).start()
    fetch.wait()
    store = pltpu.make_async_copy(
        hold, out_ref.at[pl.ds(pl.multiple_of(d * rows, 8), rows)], local_sem.at[1]
    )
    store.start()
    for step in range(1, n - 1):
        for c in range(subs):
            for way in (0, 1):
                copy(way, step - 1, c, step == 1).wait_recv()
                copy(way, step, c, False).start()
    for c in range(subs):
        for way in (0, 1):
            copy(way, n - 2, c, n == 2).wait_recv()
    store.wait()
    for step in range(n - 1):
        for c in range(subs):
            for way in (0, 1):
                copy(way, step, c, step == 0).wait_send()


def ring_gather(own, n):
    rows, cols = own.shape
    subs = 2
    return pl.pallas_call(
        functools.partial(gather_kernel, n, subs),
        out_shape=jax.ShapeDtypeStruct((n * rows, cols), own.dtype),
        in_specs=[pl.BlockSpec(memory_space=pl.ANY)],
        out_specs=pl.BlockSpec(memory_space=pl.ANY),
        scratch_shapes=[
            pltpu.VMEM((rows, cols), own.dtype),
            pltpu.SemaphoreType.DMA((2,)),
            pltpu.SemaphoreType.DMA((2, n - 1, subs)),
            pltpu.SemaphoreType.DMA((2, n - 1, subs)),
        ],
        cost_estimate=pl.CostEstimate(flops=10**9, bytes_accessed=1500 * 10**6, transcendentals=0),
        compiler_params=pltpu.CompilerParams(
            collective_id=0, has_side_effects=True, vmem_limit_bytes=32 << 20
        ),
        name="ring_gather",
    )(own)


def piece_of(half):
    for size in (64, 32, 16):
        if half % size == 0:
            return size


def reduce_kernel(n, shard_lines, left_ref, right_refs, qkv_ref, out_ref, slots, lines, ssem, rsem, out_sem):
    t = lax.axis_index("tensor")
    d, p, right, left = ring_neighbours(n)
    rows = BIG_ROWS // n
    half = rows // 2
    SUB = piece_of(half)
    subs = half // SUB
    ring_barrier(left, right, t)
    qkv_at = BIG_OFF["w_qkv"]
    qkv_rows = dict(BIG)["w_qkv"]

    def own_into(at, put):
        in_qkv = jnp.logical_and(at >= qkv_at, at < qkv_at + qkv_rows)
        which = jnp.int32(0)
        for name, _ in BIG[1:]:
            if name != "w_qkv":
                which = which + jnp.where(at >= BIG_OFF[name], 1, 0)

        @pl.when(in_qkv)
        def _():
            put(qkv_ref[pl.ds(pl.multiple_of(at - qkv_at, SUB), SUB), :].astype(F32))

        @pl.when(jnp.logical_not(in_qkv))
        def _():
            row = jnp.where(at >= qkv_at + qkv_rows, at - qkv_rows, at)
            lt = left_ref[pl.ds(pl.multiple_of(row, SUB), SUB), :]
            put(jnp.dot(lt, right_refs[which], preferred_element_type=F32))

    def owner_of(way, step):
        return ring_dev(lax.rem(p + (n - 1 - step if way == 0 else 1 + step), n), n)

    def copy(way, step, c):
        target = right if way == 0 else left
        return pltpu.make_async_remote_copy(
            src_ref=slots.at[way, step, pl.ds(pl.multiple_of(c * SUB, SUB), SUB)],
            dst_ref=slots.at[way, step + 1, pl.ds(pl.multiple_of(c * SUB, SUB), SUB)],
            send_sem=ssem.at[way, step, c],
            recv_sem=rsem.at[way, step, c],
            device_id=(target, t),
            device_id_type=MESH,
        )

    def run(step):
        @pl.loop(0, subs)
        def _(c):
            here = pl.ds(pl.multiple_of(c * SUB, SUB), SUB)
            for way in (0, 1):
                at = owner_of(way, step) * rows + way * half + c * SUB
                if step > 0:
                    copy(way, step - 1, c).wait_recv()

                def put(value):
                    if step > 0:
                        value = value + slots[way, step, here, :].astype(F32)
                    if step < n - 1:
                        slots[way, step, here, :] = value.astype(BF)
                    else:
                        for j in range(LINES):
                            lines[way, pl.ds(j, SUB, stride=LINES), :] = value[:, j * LANES : (j + 1) * LANES]

                if step == n - 1:

                    @pl.when(c > 0)
                    def _():
                        leave(way, c - 1).wait()

                own_into(at, put)
                if step < n - 1:
                    copy(way, step, c).start()
                else:
                    leave(way, c).start()

    def leave(way, c):
        row = d * rows + way * half + c * SUB
        to = row * LINES + LEAD + jnp.where(row >= FIRST // LINES, SMALL_ROWS, 0) - d * shard_lines + SLACK
        return pltpu.make_async_copy(
            lines.at[way], out_ref.at[pl.ds(to, SUB * LINES), 0], out_sem.at[way]
        )

    for step in range(n):
        run(step)
    for way in (0, 1):
        leave(way, subs - 1).wait()

    @pl.loop(0, subs)
    def _(c):
        for way in (0, 1):
            for step in range(n - 1):
                copy(way, step, c).wait_send()


def ring_reduce(left_t, rights, qkv_grad, n, shard_lines):
    rows = BIG_ROWS // n
    sub = piece_of(rows // 2)
    subs = rows // 2 // sub
    vm = pl.BlockSpec(memory_space=pltpu.VMEM)
    return pl.pallas_call(
        functools.partial(reduce_kernel, n, shard_lines),
        out_shape=jax.ShapeDtypeStruct((shard_lines + 2 * SLACK, 1, LANES), F32),
        in_specs=[vm, vm, vm],
        out_specs=pl.BlockSpec(memory_space=pl.ANY),
        scratch_shapes=[
            pltpu.VMEM((2, n, rows // 2, D), BF),
            pltpu.VMEM((2, sub * LINES, LANES), F32),
            pltpu.SemaphoreType.DMA((2, n - 1, subs)),
            pltpu.SemaphoreType.DMA((2, n - 1, subs)),
            pltpu.SemaphoreType.DMA((2,)),
        ],
        cost_estimate=pl.CostEstimate(flops=10**9, bytes_accessed=1500 * 10**6, transcendentals=0),
        compiler_params=pltpu.CompilerParams(
            collective_id=1, has_side_effects=True, vmem_limit_bytes=67043328
        ),
        name="ring_reduce",
    )(left_t, rights, qkv_grad)


def pair_kernel(parts, x_ref, out_ref, from_mate, chip, from_far, s1, r1, s2, r2, s3, r3):
    d = lax.axis_index("dp")
    t = lax.axis_index("tensor")
    core = lax.rem(t, 2)
    mate = t + 1 - 2 * core
    far = lax.rem(t + 2, 4)
    half = x_ref.shape[0] // 2
    q = half // parts
    barrier = pltpu.get_barrier_semaphore()
    for peer in (mate, far):
        pl.semaphore_signal(barrier, inc=1, device_id=(d, peer), device_id_type=MESH)
    pl.semaphore_wait(barrier, 2)

    def mine(k):
        return pl.ds(pl.multiple_of(core * half + k * q, 16), q)

    def theirs(k):
        return pl.ds(pl.multiple_of((1 - core) * half + k * q, 16), q)

    def send(src, dst, ssem, rsem, k, peer):
        return pltpu.make_async_remote_copy(
            src_ref=src,
            dst_ref=dst,
            send_sem=ssem.at[k],
            recv_sem=rsem.at[k],
            device_id=(d, peer),
            device_id_type=MESH,
        )

    def one(k):
        here = pl.ds(k * q, q)
        return send(x_ref.at[theirs(k)], from_mate.at[here], s1, r1, k, mate)

    def two(k):
        here = pl.ds(k * q, q)
        return send(chip.at[here], from_far.at[here], s2, r2, k, far)

    def three(k):
        return send(out_ref.at[mine(k)], out_ref.at[mine(k)], s3, r3, k, mate)

    for k in range(parts):
        one(k).start()
    for k in range(parts):
        here = slice(k * q, (k + 1) * q)
        one(k).wait_recv()
        chip[here, :] = (x_ref[mine(k), :].astype(F32) + from_mate[here, :].astype(F32)).astype(BF)
        two(k).start()
    for k in range(parts):
        here = slice(k * q, (k + 1) * q)
        two(k).wait_recv()
        out_ref[mine(k), :] = (chip[here, :].astype(F32) + from_far[here, :].astype(F32)).astype(BF)
        three(k).start()
    for k in range(parts):
        three(k).wait_recv()
    for k in range(parts):
        one(k).wait_send()
        two(k).wait_send()
        three(k).wait_send()


def sum_tensor(value):
    rows, cols = value.shape
    parts = 8 if cols >= 1024 else 1
    vm = pl.BlockSpec(memory_space=pltpu.VMEM)
    dma = pltpu.SemaphoreType.DMA
    part = pltpu.VMEM((rows // 2, cols), BF)
    return pl.pallas_call(
        functools.partial(pair_kernel, parts),
        out_shape=jax.ShapeDtypeStruct((rows, cols), BF),
        in_specs=[vm],
        out_specs=vm,
        scratch_shapes=[part, part, part] + [dma((parts,))] * 6,
        compiler_params=pltpu.CompilerParams(
            collective_id=3 if cols >= 1024 else 4, has_side_effects=True
        ),
        name="sum_tensor",
    )(value)


def sum_proj(value):
    cols = value.shape[1]
    padded = jnp.pad(value, ((0, 0), (0, -cols % LANES)))
    return sum_tensor(padded)[:, :cols]


def rows_kernel(src, dst, src_ref, out_ref, inn, out):
    wide = src_ref.shape[1] // LANES
    thin = out_ref.shape[1] // LANES
    groups = src_ref.shape[0] // src
    for b in range(wide):
        inn[b] = src_ref[:, b * LANES : (b + 1) * LANES].astype(F32)
    for q in range(src * wide):
        a, b = divmod(q, wide)
        j, c = divmod(q, thin)
        out[c, pl.ds(j, groups, stride=dst), :] = inn[b, pl.ds(a, groups, stride=src), :]
    for c in range(thin):
        out_ref[:, c * LANES : (c + 1) * LANES] = out[c].astype(BF)


def change_rows(value, start, count, width):
    cols = value.shape[1]
    unit = math.gcd(cols, width)
    src, dst = width // unit, cols // unit
    block = 32 * src
    first = start // block
    return pl.pallas_call(
        functools.partial(rows_kernel, src, dst),
        grid=(count // block,),
        out_shape=jax.ShapeDtypeStruct((count * cols // width, width), BF),
        in_specs=[pl.BlockSpec((block, cols), lambda i: (i + first, 0))],
        out_specs=pl.BlockSpec((32 * dst, width), lambda i: (i, 0)),
        scratch_shapes=[
            pltpu.VMEM((cols // LANES, block, LANES), F32),
            pltpu.VMEM((width // LANES, 32 * dst, LANES), F32),
        ],
        compiler_params=pltpu.CompilerParams(vmem_limit_bytes=24 << 20),
        name="change_rows",
    )(value)


def spread(ref, value):
    rows = value.shape[0]
    for j in range(EI // LANES):
        ref[pl.ds(j, rows, stride=EI // LANES), :] = value[:, j * LANES : (j + 1) * LANES]


def collect(ref, rows):
    return jnp.concatenate(
        [ref[pl.ds(j, rows, stride=EI // LANES), :] for j in range(EI // LANES)], axis=1
    )


SUBL = EI // LANES


def scan_kernel(slots, proj_ref, bc_ref, unit_ref, gate_ref, w_dt_ref, bias_ref, skip_ref, alog_ref,
                gated_ref, step_s, su_s, y_s, rate_s):
    pre = jnp.dot(proj_ref[:, :DTR], w_dt_ref[...], preferred_element_type=F32) + bias_ref[...]
    step = softplus(pre)
    unit = unit_ref[...].astype(F32)
    spread(step_s, step)
    spread(su_s, step * unit)
    rate_s[...] = -jnp.exp(alog_ref[...]) * LOG2E

    def body(t, states):
        new = []
        for m in range(slots):
            r = m * SLOT + t
            row = pl.ds(pl.multiple_of(r * SUBL, SUBL), SUBL)
            st = step_s[row, :]
            su = su_s[row, :]
            y = jnp.zeros((SUBL, LANES), F32)
            for k in range(NSTATE):
                dec = jnp.exp2(rate_s[k * SUBL : (k + 1) * SUBL, :] * st)
                s = dec * states[m * NSTATE + k] + bc_ref[r, k] * su
                y = y + bc_ref[r, NSTATE + k] * s
                new.append(s)
            y_s[row, :] = y
        return tuple(new)

    init = tuple(jnp.zeros((SUBL, LANES), F32) for _ in range(slots * NSTATE))
    lax.fori_loop(0, SLOT, body, init)
    y = collect(y_s, slots * SLOT) + skip_ref[...] * unit
    z = gate_ref[...]
    gated_ref[...] = (y * silu(z)).astype(BF)


def scan_forward(proj, bc, unit, gate, w_dt, dt_bias, d_skip, a_log):
    rows = unit.shape[0]
    vm = pl.BlockSpec(memory_space=pltpu.VMEM)
    sm = pl.BlockSpec(memory_space=pltpu.SMEM)
    return pl.pallas_call(
        functools.partial(scan_kernel, rows // SLOT),
        out_shape=jax.ShapeDtypeStruct((rows, EI), BF),
        in_specs=[vm, sm, vm, vm, vm, vm, vm, vm],
        out_specs=vm,
        scratch_shapes=[
            pltpu.VMEM((rows * SUBL, LANES), F32),
            pltpu.VMEM((rows * SUBL, LANES), F32),
            pltpu.VMEM((rows * SUBL, LANES), F32),
            pltpu.VMEM((NSTATE * SUBL, LANES), F32),
        ],
        compiler_params=pltpu.CompilerParams(vmem_limit_bytes=60 << 20),
        name="scan_forward",
    )(proj, bc, unit, gate, w_dt, dt_bias, d_skip, a_log)


def adjoint_kernel(slots, proj_ref, bc_ref, unit_ref, gate_ref, w_dt_ref, bias_ref, skip_ref, alog_ref,
                   grad_ref, gz_ref, gunit_ref, gproj_ref, gdt_ref, gbias_ref, gskip_ref, galog_ref,
                   step_s, su_s, unit_s, y_s, gy_s, gs_s, lb_s, rate_s, hist, lams):
    rows = slots * SLOT
    pre = jnp.dot(proj_ref[:, :DTR], w_dt_ref[...], preferred_element_type=F32) + bias_ref[...]
    step = softplus(pre)
    unit = unit_ref[...].astype(F32)
    spread(step_s, step)
    spread(unit_s, unit)
    spread(su_s, step * unit)
    z = gate_ref[...]
    sig = jax.nn.sigmoid(z)
    gg = grad_ref[...]
    gy = gg * z * sig
    spread(gy_s, gy)
    rate_s[...] = -jnp.exp(alog_ref[...])
    galog_ref[...] = jnp.zeros_like(galog_ref)
    zero = jnp.zeros((SUBL, LANES), F32)
    span = SLOT + 1

    def hist_at(k, t):
        return pl.ds(pl.multiple_of((k * span + t) * SUBL, SUBL), SUBL)

    def lam_at(k, t):
        return pl.ds(pl.multiple_of((k * SLOT + t) * SUBL, SUBL), SUBL)

    for m in range(slots):
        for k in range(NSTATE):
            hist[hist_at(k, 0), :] = zero

        def forward(t, states):
            r = m * SLOT + t
            row = pl.ds(pl.multiple_of(r * SUBL, SUBL), SUBL)
            st = step_s[row, :] * LOG2E
            su = su_s[row, :]
            y = zero
            new = []
            for k in range(NSTATE):
                dec = jnp.exp2(rate_s[k * SUBL : (k + 1) * SUBL, :] * st)
                s = dec * states[k] + bc_ref[r, k] * su
                y = y + bc_ref[r, NSTATE + k] * s
                hist[hist_at(k, t + 1), :] = s
                new.append(s)
            y_s[row, :] = y
            return tuple(new)

        lax.fori_loop(0, SLOT, forward, tuple(zero for _ in range(NSTATE)))

        def backward(i, carry):
            t = SLOT - 1 - i
            r = m * SLOT + t
            row = pl.ds(pl.multiple_of(r * SUBL, SUBL), SUBL)
            st = step_s[row, :]
            st2 = st * LOG2E
            gyt = gy_s[row, :]
            lb = zero
            gs = zero
            new = []
            for k in range(NSTATE):
                rate = rate_s[k * SUBL : (k + 1) * SUBL, :]
                dec = jnp.exp2(rate * st2)
                lam = bc_ref[r, NSTATE + k] * gyt + carry[k]
                ld = dec * lam
                new.append(ld)
                lams[lam_at(k, t), :] = lam
                lb = lb + bc_ref[r, k] * lam
                x = ld * hist[hist_at(k, t), :]
                gs = gs + rate * x
                at = slice(k * SUBL, (k + 1) * SUBL)
                galog_ref[at, :] = galog_ref[at, :] + st * x
            lb_s[row, :] = lb
            gs_s[row, :] = gs + unit_s[row, :] * lb
            return tuple(new)

        lax.fori_loop(0, SLOT, backward, tuple(zero for _ in range(NSTATE)))
        out = slice(m * SLOT, (m + 1) * SLOT)
        base = m * SLOT * SUBL

        lane = lax.broadcasted_iota(jnp.int32, (SLOT, LANES), 1)

        def reduce_state(k, acc):
            ab = jnp.zeros((SLOT, LANES), F32)
            ac = jnp.zeros((SLOT, LANES), F32)
            for j in range(SUBL):
                cols = slice(j * LANES, (j + 1) * LANES)
                lam = lams[pl.ds(k * SLOT * SUBL + j, SLOT, stride=SUBL), :]
                h = hist[pl.ds((k * span + 1) * SUBL + j, SLOT, stride=SUBL), :]
                sj = su_s[pl.ds(base + j, SLOT, stride=SUBL), :]
                gj = gy_s[pl.ds(base + j, SLOT, stride=SUBL), :]
                ab = ab + lam * sj
                ac = ac + h * gj
            sb = jnp.sum(ab, axis=1, keepdims=True)
            sc = jnp.sum(ac, axis=1, keepdims=True)
            return acc + jnp.where(lane == k, sb, 0.0) + jnp.where(lane == NSTATE + k, sc, 0.0)

        sums = lax.fori_loop(0, NSTATE, reduce_state, jnp.zeros((SLOT, LANES), F32))
        gproj_ref[out, DTR : DTR + LANES] = sums.astype(BF)
    galog_ref[...] = galog_ref[...] * rate_s[...]
    y = collect(y_s, rows) + skip_ref[...] * unit
    gz_ref[...] = (gg * y * sig * (1.0 + z * (1.0 - sig))).astype(BF)
    gunit_ref[...] = gy * skip_ref[...] + step * collect(lb_s, rows)
    gskip_ref[...] = jnp.sum(gy * unit, axis=0, keepdims=True)
    q = collect(gs_s, rows) * jax.nn.sigmoid(pre)
    gbias_ref[...] = jnp.sum(q, axis=0, keepdims=True)
    ql = q.astype(BF)
    gdt_ref[...] = mat_tn(proj_ref[:, :DTR], ql)
    gproj_ref[:, :DTR] = mat_nt(ql, w_dt_ref[...]).astype(BF)


def scan_backward(proj, bc, unit, gate, w_dt, dt_bias, d_skip, a_log, grad):
    rows = unit.shape[0]
    vm = pl.BlockSpec(memory_space=pltpu.VMEM)
    sm = pl.BlockSpec(memory_space=pltpu.SMEM)
    sds = jax.ShapeDtypeStruct
    flat = pltpu.VMEM((rows * SUBL, LANES), F32)
    return pl.pallas_call(
        functools.partial(adjoint_kernel, rows // SLOT),
        out_shape=(
            sds((rows, EI), BF),
            sds((rows, EI), F32),
            sds((rows, DTR + LANES), BF),
            sds((DTR, EI), F32),
            sds((1, EI), F32),
            sds((1, EI), F32),
            sds((NSTATE * SUBL, LANES), F32),
        ),
        in_specs=[vm, sm, vm, vm, vm, vm, vm, vm, vm],
        out_specs=(vm,) * 7,
        scratch_shapes=[flat] * 7
        + [
            pltpu.VMEM((NSTATE * SUBL, LANES), F32),
            pltpu.VMEM((NSTATE * (SLOT + 1) * SUBL, LANES), F32),
            pltpu.VMEM((NSTATE * SLOT * SUBL, LANES), F32),
        ],
        compiler_params=pltpu.CompilerParams(vmem_limit_bytes=60 << 20),
        name="scan_backward",
    )(proj, bc, unit, gate, w_dt, dt_bias, d_skip, a_log, grad)


def rope_tables(length, head_dim):
    half_dim = head_dim // 2
    freq_index = jnp.arange(half_dim, dtype=F32)
    inv_freq = jnp.exp(-math.log(ROPE_BASE) * 2.0 * freq_index / head_dim)
    angles = jnp.arange(length, dtype=F32)[:, None] * inv_freq[None, :]
    return (jnp.cos(angles)[None, :, None, :], jnp.sin(angles)[None, :, None, :])


def rope_apply(values, cosine, sine):
    half_dim = values.shape[-1] // 2
    a = values[..., :half_dim]
    b = values[..., half_dim:]
    return jnp.concatenate([a * cosine - b * sine, b * cosine + a * sine], axis=-1)


def rms_parts(v, g):
    s = lax.rsqrt(jnp.mean(v * v, axis=-1, keepdims=True) + EPS_NORM)
    return s, v * s


def rms_back(v, g, gh):
    s, nrm = rms_parts(v, g)
    gg = jnp.sum(gh * nrm, axis=0)
    gv = s * (gh * g - nrm * jnp.mean(gh * g * nrm, axis=-1, keepdims=True))
    return gv, gg


def total(partial_out):
    return sum_tensor(partial_out.astype(BF)).astype(F32)


def shift_down(v, by):
    if by == 0:
        return v
    return jnp.pad(v, ((0, 0), (by, 0), (0, 0)))[:, : v.shape[1]]


def shift_up(v, by):
    if by == 0:
        return v
    return jnp.pad(v, ((0, 0), (0, by), (0, 0)))[:, by:]


def attend(query, keys, values):
    scale = HEAD_DIM ** (-0.5)
    distance = jnp.arange(SLOT)[:, None] - jnp.arange(SLOT)[None, :]
    allowed = (distance >= 0) & (distance < WINDOW)
    scores = jnp.einsum("mqhd,mkhd->mhqk", query, keys, preferred_element_type=F32) * scale
    scores = jnp.where(allowed, scores, NEG_FILL)
    expo = jnp.exp(scores - jnp.max(scores, axis=-1, keepdims=True))
    return expo / jnp.sum(expo, axis=-1, keepdims=True)


def ffn_forward(h, w_gu, w_down):
    pre = mat_nn(h, w_gu)
    act = (silu(pre[:, :FI]) * pre[:, FI:]).astype(BF)
    return total(mat_nn(act, w_down)), pre, act


def ffn_backward(pre, w_gu, w_down, grad_low):
    gate = pre[:, :FI]
    up = pre[:, FI:]
    ga = mat_nt(grad_low, w_down)
    sig = jax.nn.sigmoid(gate)
    grad_gate = ga * up * sig * (1.0 + gate * (1.0 - sig))
    grad_up = ga * gate * sig
    gp = jnp.concatenate([grad_gate, grad_up], axis=1).astype(BF)
    return total(mat_nt(gp, w_gu)), gp


def layer(x, grad_out, w, small, gains, n):
    rows = x.shape[0]
    m = rows // SLOT
    hr = HW // HEAD_DIM
    cosine, sine = rope_tables(SLOT, HEAD_DIM)
    s1, n1 = rms_parts(x, gains[0])
    h1 = (n1 * gains[0]).astype(BF)
    mixed = mat_nn(h1, w["w_in"])
    mix_x = mixed[:, :EI].reshape(m, SLOT, EI)
    gate_z = mixed[:, EI:]
    conv_w = small["conv_w"].astype(F32)
    pre_conv = small["conv_b"].astype(F32)[None, None, :]
    for j in range(CONV):
        pre_conv = pre_conv + conv_w[j] * shift_down(mix_x, CONV - 1 - j)
    unit = silu(pre_conv).astype(BF).reshape(rows, EI)
    proj = sum_proj(mat_nn(unit, small["w_x"]).astype(BF))
    bc = proj[:, DTR:].astype(F32)
    scan_args = (
        proj[:, :DTR],
        bc,
        unit,
        gate_z,
        small["w_dt"],
        small["dt_bias"].astype(F32)[None],
        small["d_skip"].astype(F32)[None],
        small["a_log"].astype(F32).reshape(NSTATE * SUBL, LANES),
    )
    gated = scan_forward(*scan_args)
    x1 = x + total(mat_nn(gated, w["w_out"]))
    h2 = (rms_parts(x1, 0)[1] * gains[1]).astype(BF)
    branch, pre1, act1 = ffn_forward(h2, w["w_gu1"], w["w_down1"])
    x2 = x1 + branch
    h3 = (rms_parts(x2, 0)[1] * gains[2]).astype(BF)
    packed = mat_nn(h3, w["w_qkv"]).reshape(m, SLOT, 3, hr, HEAD_DIM)
    query = rope_apply(packed[:, :, 0], cosine, sine).astype(BF)
    keys = rope_apply(packed[:, :, 1], cosine, sine).astype(BF)
    values = packed[:, :, 2].astype(BF)
    probs = attend(query, keys, values)
    probs_low = probs.astype(BF)
    attended = jnp.einsum("mhqk,mkhd->mqhd", probs_low, values, preferred_element_type=F32)
    attended = attended.reshape(rows, HW).astype(BF)
    x3 = x2 + total(mat_nn(attended, w["w_o"]))
    h4 = (rms_parts(x3, 0)[1] * gains[3]).astype(BF)
    pre2 = mat_nn(h4, w["w_gu2"])
    act2 = (silu(pre2[:, :FI]) * pre2[:, FI:]).astype(BF)
    last = mat_nn(act2, w["w_down2"]).astype(BF)

    gb4 = grad_out.astype(BF)
    gh, gp2 = ffn_backward(pre2, w["w_gu2"], w["w_down2"], gb4)
    gv, gg4 = rms_back(x3, gains[3], gh)
    g3 = grad_out + gv
    gb3 = g3.astype(BF)
    gatt = mat_nt(gb3, w["w_o"]).astype(BF).reshape(m, SLOT, hr, HEAD_DIM)
    grad_p = jnp.einsum("mqhd,mkhd->mhqk", gatt, values, preferred_element_type=F32)
    inner = jnp.sum(probs * grad_p, axis=-1, keepdims=True)
    gs = (probs * (grad_p - inner)).astype(BF)
    scale = HEAD_DIM ** (-0.5)
    gq = jnp.einsum("mhqk,mkhd->mqhd", gs, keys, preferred_element_type=F32) * scale
    gk = jnp.einsum("mhqk,mqhd->mkhd", gs, query, preferred_element_type=F32) * scale
    gvv = jnp.einsum("mhqk,mqhd->mkhd", probs_low, gatt, preferred_element_type=F32)
    gpk = (
        jnp.stack([rope_apply(gq, cosine, -sine), rope_apply(gk, cosine, -sine), gvv], axis=2)
        .reshape(rows, 3 * HW)
        .astype(BF)
    )
    gv, gg3 = rms_back(x2, gains[2], total(mat_nt(gpk, w["w_qkv"])))
    g2 = g3 + gv
    gb2 = g2.astype(BF)
    gh, gp1 = ffn_backward(pre1, w["w_gu1"], w["w_down1"], gb2)
    gv, gg2 = rms_back(x1, gains[1], gh)
    g1 = g2 + gv
    gb1 = g1.astype(BF)
    ggated = mat_nt(gb1, w["w_out"])
    gz, gunit, gproj, g_dt, g_bias, g_skip, g_alog = scan_backward(*scan_args, ggated)
    gproj = sum_tensor(gproj)[:, : DTR + 2 * NSTATE]
    g_wx = mat_tn(unit, gproj)
    gu = gunit + mat_nt(gproj, small["w_x"])
    sig = jax.nn.sigmoid(pre_conv)
    gpre = gu.reshape(m, SLOT, EI) * sig * (1.0 + pre_conv * (1.0 - sig))
    g_conv_b = jnp.sum(gpre, axis=(0, 1))
    g_conv_w = jnp.stack(
        [jnp.sum(gpre * shift_down(mix_x, CONV - 1 - j), axis=(0, 1)) for j in range(CONV)]
    )
    gmx = sum(conv_w[j] * shift_up(gpre, CONV - 1 - j) for j in range(CONV))
    gmixed = jnp.concatenate([gmx.reshape(rows, EI).astype(BF), gz], axis=1)
    gv, gg1 = rms_back(x, gains[0], total(mat_nt(gmixed, w["w_in"])))
    g0 = g1 + gv

    left_t = jnp.concatenate([h1, gated, h2, act1, attended, h4, act2], axis=1).T
    rights = jnp.stack([gmixed, gb1, gp1, gb2, gb3, gp2, gb4])
    g_qkv = mat_tn(h3, gpk).astype(BF)
    g_qkv = change_rows(g_qkv, 0, D, D)
    start = lax.axis_index("tensor") * DG
    g_gain = lax.dynamic_slice_in_dim(jnp.stack([gg1, gg2, gg3, gg4]), start, DG, 1)
    pieces = [g_gain, g_conv_w, g_conv_b, g_bias, g_skip, g_alog, g_wx, g_dt]
    small_grads = jnp.concatenate([p.reshape(-1, LANES).astype(BF) for p in pieces])
    g0, small_grads, last, left_t = lax.optimization_barrier((g0, small_grads, last, left_t))
    return x3, last, g0, (left_t, rights, g_qkv), small_grads


def extents(n, shard_rows):
    slab = BIG_ROWS * LINES // n
    before = 0
    after = 0
    back_before = 0
    back_after = 0
    for d in range(n):
        lo, hi = slab * d, slab * (d + 1) - 1
        qs = [p + LEAD + (SMALL_ROWS if p >= FIRST else 0) - shard_rows * d for p in (lo, hi)]
        before = max(before, -qs[0])
        after = max(after, qs[1] + 1 - shard_rows)
    return before, after


def shift_perm(n, by):
    return [(i, i + by) for i in range(n) if 0 <= i + by < n]


def stack_kernel(n, shard_lines, before, per, top_ref, own_ref, bottom_ref, out_ref, hold, sem):
    d = lax.axis_index("dp")
    i = pl.program_id(0)
    steps = BIG_ROWS // n // per
    size = per * LINES

    def fetch(k, slot):
        row = d * (BIG_ROWS // n) + k * per
        a = row * LINES + LEAD + jnp.where(row >= FIRST // LINES, SMALL_ROWS, 0) - d * shard_lines
        high = a < 0
        low = a + size > shard_lines

        @pl.when(high)
        def _():
            pltpu.make_async_copy(top_ref.at[pl.ds(a + before, size), 0], hold.at[slot], sem.at[slot]).start()

        @pl.when(low)
        def _():
            pltpu.make_async_copy(
                bottom_ref.at[pl.ds(a + size - shard_lines, size), 0], hold.at[slot], sem.at[slot]
            ).start()

        @pl.when(jnp.logical_not(jnp.logical_or(high, low)))
        def _():
            pltpu.make_async_copy(own_ref.at[pl.ds(a, size), 0], hold.at[slot], sem.at[slot]).start()

    @pl.when(i == 0)
    def _():
        for k in range(min(3, steps)):
            fetch(k, k)

    @pl.when(i + 3 < steps)
    def _():
        fetch(i + 3, lax.rem(i + 3, 4))

    slot = lax.rem(i, 4)
    pltpu.make_async_copy(own_ref.at[pl.ds(0, size), 0], hold.at[slot], sem.at[slot]).wait()
    for j in range(LINES):
        out_ref[:, j * LANES : (j + 1) * LANES] = hold[slot, pl.ds(j, per, stride=LINES), :].astype(BF)


def stack_own(lines3, n):
    shard_lines = lines3.shape[0]
    before, after = extents(n, shard_lines)
    rows = BIG_ROWS // n
    per = 64 if rows % 64 == 0 else 32
    size = per * LINES
    nxt = lax.ppermute(lines3[:after], "dp", shift_perm(n, -1))
    prv = lax.ppermute(lines3[shard_lines - before :], "dp", shift_perm(n, 1))
    top = jnp.concatenate([prv, lines3[:size]])
    bottom = jnp.concatenate([lines3[shard_lines - size :], nxt])
    hbm = pl.BlockSpec(memory_space=pl.ANY)
    return pl.pallas_call(
        functools.partial(stack_kernel, n, shard_lines, before, per),
        grid=(rows // per,),
        out_shape=jax.ShapeDtypeStruct((rows, D), BF),
        in_specs=[hbm] * 3,
        out_specs=pl.BlockSpec((per, D), lambda i: (i, 0)),
        scratch_shapes=[pltpu.VMEM((4, size, LANES), F32), pltpu.SemaphoreType.DMA((4,))],
        compiler_params=pltpu.CompilerParams(vmem_limit_bytes=24 << 20),
        name="stack_own",
    )(top, lines3, bottom)


def low_kernel(x_ref, out_ref):
    out_ref[...] = x_ref[:, 0, :].astype(BF)


def to_low(value):
    vm = pl.BlockSpec(memory_space=pltpu.VMEM)
    return pl.pallas_call(
        low_kernel,
        out_shape=jax.ShapeDtypeStruct((value.shape[0], LANES), BF),
        in_specs=[vm],
        out_specs=vm,
        name="to_low",
    )(value)


def window(values, shift, size):
    length = values.shape[0]
    s = jnp.clip(shift, 0, length - size)
    got = lax.dynamic_slice_in_dim(values, s, size, 0)
    room = jnp.zeros((3 * size,) + values.shape[1:], values.dtype)
    room = lax.dynamic_update_slice_in_dim(room, got, size + jnp.clip(s - shift, -size, size), 0)
    return room[size : 2 * size]


STRIP = 8192


def lone_group(groups, bounds_ref, start, stop):
    def look(g, found):
        holds = jnp.logical_and(bounds_ref[2 * g] <= start, bounds_ref[2 * g + 1] >= stop)
        return jnp.where(holds, g, found)

    return lax.fori_loop(0, groups, look, jnp.int32(-1))


def moments_kernel(groups, shard, bounds_ref, grad_ref, w_ref, one_ref, two_ref,
                   first_ref, second_ref, grad_out, sums_ref, hold):
    i = pl.program_id(0)
    size = CHUNK * LANES
    lanes = STRIP // 8

    @pl.when(i == 0)
    def _():
        @pl.loop(0, 2 * groups)
        def _(g):
            sums_ref[g] = 0.0

    def strip(k, carry):
        here = pl.ds(pl.multiple_of(k * STRIP, STRIP), STRIP)
        grad = grad_ref[:, here]
        w = w_ref[:, here]
        first = BETA_ONE * one_ref[:, here] + (1.0 - BETA_ONE) * grad
        second = BETA_TWO * two_ref[:, here] + (1.0 - BETA_TWO) * grad * grad
        ratio = first / (jnp.sqrt(second) + ADAM_EPS) + DECAY_W * w
        first_ref[:, here] = first
        second_ref[:, here] = second
        grad_out[:, here] = grad
        hold[:, here] = ratio
        wsq, rsq = carry
        for j in range(8):
            part = slice(j * lanes, (j + 1) * lanes)
            wsq = wsq + w[:, part] * w[:, part]
            rsq = rsq + ratio[:, part] * ratio[:, part]
        return wsq, rsq

    zero = jnp.zeros((1, lanes), F32)
    wsq, rsq = lax.fori_loop(0, size // STRIP, strip, (zero, zero))
    d = lax.axis_index("dp")
    start = d * shard + i * size
    limit = (d + 1) * shard
    alone = lone_group(groups, bounds_ref, start, start + size)
    alone = jnp.where(start + size <= limit, alone, -1)

    @pl.when(alone >= 0)
    def _():
        sums_ref[2 * alone] = sums_ref[2 * alone] + jnp.sum(wsq)
        sums_ref[2 * alone + 1] = sums_ref[2 * alone + 1] + jnp.sum(rsq)

    @pl.when(alone < 0)
    def _():
        @pl.loop(0, groups)
        def _(g):
            low = jnp.maximum(bounds_ref[2 * g], start)
            high = jnp.minimum(bounds_ref[2 * g + 1], jnp.minimum(start + size, limit))

            @pl.when(low < high)
            def _():
                def masked(k, carry):
                    at = pl.multiple_of(k * lanes, lanes)
                    here = pl.ds(at, lanes)
                    index = start + at + lax.broadcasted_iota(jnp.int32, (1, lanes), 1)
                    inside = (index >= low) & (index < high)
                    wv = w_ref[:, here]
                    rv = hold[:, here]
                    return (
                        carry[0] + jnp.where(inside, wv * wv, 0.0),
                        carry[1] + jnp.where(inside, rv * rv, 0.0),
                    )

                k0 = (low - start) // lanes
                k1 = (high - start + lanes - 1) // lanes
                wv, rv = lax.fori_loop(k0, k1, masked, (zero, zero))
                sums_ref[2 * g] = sums_ref[2 * g] + jnp.sum(wv)
                sums_ref[2 * g + 1] = sums_ref[2 * g + 1] + jnp.sum(rv)


def moments(bounds, lines, master, one, two):
    shard = master.shape[1]
    size = CHUNK * LANES
    groups = bounds.shape[0] // 2
    block = pl.BlockSpec((1, size), lambda i: (0, i))
    ahead = SLACK // CHUNK
    flat = jax.ShapeDtypeStruct((1, shard), F32)
    smem = pl.BlockSpec(memory_space=pltpu.SMEM)
    return pl.pallas_call(
        functools.partial(moments_kernel, groups, shard),
        grid=(pl.cdiv(shard, size),),
        out_shape=(flat, flat, flat, jax.ShapeDtypeStruct((2 * groups,), F32)),
        in_specs=[smem, pl.BlockSpec((1, size), lambda i: (0, i + ahead)), block, block, block],
        out_specs=(block, block, block, smem),
        scratch_shapes=[pltpu.VMEM((1, size), F32)],
        compiler_params=pltpu.CompilerParams(vmem_limit_bytes=40 << 20),
        name="moments",
    )(bounds, lines.reshape(1, -1), master, one, two)


def update_kernel(groups, shard, bounds_ref, trust_ref, w_ref, first_ref, second_ref, new_ref, low_ref, hold):
    i = pl.program_id(0)
    size = CHUNK * LANES
    lanes = STRIP // 8
    start = lax.axis_index("dp") * shard + i * size
    alone = lone_group(groups, bounds_ref, start, start + size)

    def step(trust_of):
        @pl.loop(0, size // STRIP)
        def _(k):
            here = pl.ds(pl.multiple_of(k * STRIP, STRIP), STRIP)
            w = w_ref[:, here]
            ratio = first_ref[:, here] / (jnp.sqrt(second_ref[:, here]) + ADAM_EPS) + DECAY_W * w
            new = w - LEARN_RATE * trust_of(here) * ratio
            new_ref[:, here] = new
            low_ref[:, here] = new.astype(BF)

    @pl.when(alone >= 0)
    def _():
        trust = trust_ref[jnp.maximum(alone, 0)]
        step(lambda here: trust)

    @pl.when(alone < 0)
    def _():
        hold[...] = jnp.zeros_like(hold)

        @pl.loop(0, groups)
        def _(g):
            low = jnp.maximum(bounds_ref[2 * g], start)
            high = jnp.minimum(bounds_ref[2 * g + 1], start + size)

            @pl.when(low < high)
            def _():
                @pl.loop((low - start) // lanes, (high - start + lanes - 1) // lanes)
                def _(k):
                    at = pl.multiple_of(k * lanes, lanes)
                    here = pl.ds(at, lanes)
                    index = start + at + lax.broadcasted_iota(jnp.int32, (1, lanes), 1)
                    hold[:, here] = jnp.where((index >= low) & (index < high), trust_ref[g], hold[:, here])

        step(lambda here: hold[:, here])


def update(bounds, trust, master, first, second):
    shard = master.shape[1]
    size = CHUNK * LANES
    groups = bounds.shape[0] // 2
    block = pl.BlockSpec((1, size), lambda i: (0, i))
    smem = pl.BlockSpec(memory_space=pltpu.SMEM)
    return pl.pallas_call(
        functools.partial(update_kernel, groups, shard),
        grid=(pl.cdiv(shard, size),),
        out_shape=(jax.ShapeDtypeStruct((1, shard), F32), jax.ShapeDtypeStruct((1, shard), BF)),
        in_specs=[smem, smem, block, block, block],
        out_specs=(block, block),
        scratch_shapes=[pltpu.VMEM((1, size), F32)],
        compiler_params=pltpu.CompilerParams(vmem_limit_bytes=40 << 20),
        name="update",
    )(bounds, trust, master, first, second)


def norms_kernel(n, m, own_ref, out_ref, across, along, part, ssem, rsem, ssem2, rsem2):
    d = lax.axis_index("dp")
    t = lax.axis_index("tensor")
    barrier = pltpu.get_barrier_semaphore()
    for k in range(1, m):
        pl.semaphore_signal(barrier, inc=1, device_id=(d, lax.rem(t + k, m)), device_id_type=MESH)

    @pl.loop(1, n)
    def _(k):
        pl.semaphore_signal(barrier, inc=1, device_id=(lax.rem(d + k, n), t), device_id_type=MESH)

    pl.semaphore_wait(barrier, n + m - 2)

    def over_tensor(k):
        return pltpu.make_async_remote_copy(
            src_ref=own_ref,
            dst_ref=across.at[k - 1],
            send_sem=ssem.at[k - 1],
            recv_sem=rsem.at[k - 1],
            device_id=(d, lax.rem(t + k, m)),
            device_id_type=MESH,
        )

    def over_dp(k):
        return pltpu.make_async_remote_copy(
            src_ref=part,
            dst_ref=along.at[k - 1],
            send_sem=ssem2.at[k - 1],
            recv_sem=rsem2.at[k - 1],
            device_id=(lax.rem(d + k, n), t),
            device_id_type=MESH,
        )

    for k in range(1, m):
        over_tensor(k).start()
    total_ = own_ref[...]
    for k in range(1, m):
        over_tensor(k).wait_recv()
    for k in range(1, m):
        total_ = total_ + across[k - 1]
    part[...] = total_

    @pl.loop(1, n)
    def _(k):
        over_dp(k).start()

    @pl.loop(1, n)
    def _(k):
        over_dp(k).wait_recv()

    def add(k, acc):
        return acc + along[k - 1]

    out_ref[...] = lax.fori_loop(1, n, add, part[...])
    for k in range(1, m):
        over_tensor(k).wait_send()

    @pl.loop(1, n)
    def _(k):
        over_dp(k).wait_send()


def sum_everywhere(values, n, m):
    vm = pl.BlockSpec(memory_space=pltpu.VMEM)
    dma = pltpu.SemaphoreType.DMA
    tile = pltpu.VMEM((8, LANES), F32)
    return pl.pallas_call(
        functools.partial(norms_kernel, n, m),
        out_shape=jax.ShapeDtypeStruct((8, LANES), F32),
        in_specs=[vm],
        out_specs=vm,
        scratch_shapes=[
            pltpu.VMEM((m - 1, 8, LANES), F32),
            pltpu.VMEM((n - 1, 8, LANES), F32),
            tile,
            dma((m - 1,)),
            dma((m - 1,)),
            dma((n - 1,)),
            dma((n - 1,)),
        ],
        compiler_params=pltpu.CompilerParams(collective_id=2, has_side_effects=True),
        name="sum_everywhere",
    )(values)


def per_device(n, m, tokens, cotangent, lengths, master, moment_one, moment_two):
    d = lax.axis_index("dp")
    shard = master.shape[1]
    lines = shard // LANES
    lines3 = master.reshape(lines, 1, LANES)
    base = d * lines
    mid = LEAD + FIRST
    small_own = jnp.concatenate(
        [window(lines3, -base, GAIN_ROWS), window(lines3, mid - base, SMALL_ROWS)]
    )
    small_flat = lax.psum(to_low(small_own), "dp")
    weights = ring_gather(stack_own(lines3, n), n)
    weights, small_flat = lax.optimization_barrier((weights, small_flat))
    gains = lax.all_gather(small_flat[:GAIN_ROWS].reshape(4, DG), "tensor", axis=1, tiled=True)
    gains = gains.astype(F32)
    small = {}
    at = GAIN_ROWS
    for name, shape in SMALL:
        count = math.prod(shape) // LANES
        small[name] = small_flat[at : at + count].reshape(shape)
        at += count
    w = {}
    for name, rows in BIG:
        w[name] = weights[BIG_OFF[name] : BIG_OFF[name] + rows]
    w["w_qkv"] = change_rows(weights, BIG_OFF["w_qkv"], dict(BIG)["w_qkv"], 3 * HW)
    x = tokens.astype(F32)
    pos = lax.broadcasted_iota(jnp.int32, (tokens.shape[0] // SLOT, SLOT), 1)
    valid = (pos < lengths[:, None]).astype(F32).reshape(-1, 1)
    grad = cotangent.astype(F32) * valid
    x3, last, grad_in, operands, small_grads = layer(x, grad, w, small, gains, n)
    small_sum = lax.psum(small_grads, "dp")
    laid = ring_reduce(*operands, n, lines)
    branch = lax.psum(last, "tensor")
    laid, small_sum, branch = lax.optimization_barrier((laid, small_sum, branch))
    out = (x3 + branch.astype(F32)).astype(BF)
    small_sum = small_sum.astype(F32).reshape(-1, 1, LANES)

    before, after = extents(n, lines)
    slab_lines = BIG_ROWS * LINES // n

    def local(row):
        return row * LINES + LEAD + jnp.where(row >= FIRST // LINES, SMALL_ROWS, 0) - base

    begin = local(d * (BIG_ROWS // n))
    close = local((d + 1) * (BIG_ROWS // n) - 1) + LINES
    tail, head, laid = lax.optimization_barrier(
        (laid[SLACK + lines : SLACK + lines + after], laid[SLACK - before : SLACK], laid)
    )
    from_prev = lax.ppermute(tail, "dp", shift_perm(n, 1))
    from_next = lax.ppermute(head, "dp", shift_perm(n, -1))
    line = lax.broadcasted_iota(jnp.int32, (after, 1, 1), 0)
    top = jnp.where(line < begin, from_prev, laid[SLACK : SLACK + after])
    line = lax.broadcasted_iota(jnp.int32, (before, 1, 1), 0) + (lines - before)
    bottom = jnp.where(line >= close, from_next, laid[SLACK + lines - before : SLACK + lines])
    laid = laid.at[SLACK : SLACK + after].set(top)
    laid = laid.at[SLACK + lines - before : SLACK + lines].set(bottom)

    def place(laid, values, at):
        count = values.shape[0]
        return lax.dynamic_update_slice_in_dim(laid, values, SLACK + jnp.clip(at - base, -count, lines), 0)

    laid = place(laid, small_sum[GAIN_ROWS:], mid)
    laid = place(laid, small_sum[:GAIN_ROWS], 0)
    used = LEAD + SMALL_ROWS + BIG_ROWS * LINES
    rest = lines * n - used
    if rest:
        laid = place(laid, jnp.zeros((rest, 1, LANES), F32), used)

    bounds = jnp.asarray([v for pair in group_bounds() for v in pair], jnp.int32)
    first, second, grad_shard, sums = moments(bounds, laid, master, moment_one, moment_two)
    count = sums.shape[0]
    tile = jnp.pad(sums, (0, 8 * LANES - count)).reshape(8, LANES)
    squares = sum_everywhere(tile, n, m).reshape(-1)[:count].reshape(-1, 2)
    trust = jnp.sqrt(squares[:, 0] + TRUST_EPSILON) * lax.rsqrt(squares[:, 1] + TRUST_EPSILON)
    master_new, low = update(bounds, trust, master, first, second)
    return (out, grad_in, master_new, first, second, low, grad_shard, jnp.sqrt(squares))


def solution(mesh):
    row = P("dp", None)
    flat = P("tensor", "dp")
    return jax.shard_map(
        functools.partial(per_device, mesh.shape["dp"], mesh.shape["tensor"]),
        mesh=mesh,
        in_specs=(row, row, P("dp"), flat, flat, flat),
        out_specs=(row, row, flat, flat, flat, flat, flat, P()),
        check_vma=False,
    )
```
